256 devices in a mesh: row: 8 (over y, core), col: 32 (over x, z).
Axes of the slice: x: 4, y: 4, z: 8, core: 2. Of those that a mesh axis runs over, the one named last changes fastest.
Arguments:
- features: bfloat16 [64, 1024, 512], P('row', 'col'), may hold values from -6 to 6
- kernel: float32 [7, 7, 512], replicated, may hold values from -0.875 to 0.875
- gain: float32 [512], replicated, may hold values from 0.1 to 1.9
- w_expand: bfloat16 [512, 2048], replicated, may hold values from -0.25 to 0.25
- w_reduce: bfloat16 [2048, 512], replicated, may hold values from -0.125 to 0.125
- layer_scale: float32 [512], replicated, may hold values from 0.25 to 2
- cotangent: bfloat16 [64, 1024, 512], P('row', 'col'), may hold values from -6 to 6
Outputs:
- grad_features: bfloat16 [64, 1024, 512], P('row', 'col')
- grad_kernel: float32 [7, 7, 512], replicated
- scaled_gain_gradient: float32 [512], replicated
- grad_scale: float32 [512], replicated
- grad_expand: float32 [512, 2048], P(('row', 'col'))
- grad_reduce: float32 [2048, 512], P(('row', 'col'))
The draws below stay inside these ranges and needn't reach their ends.
All inputs are finite; a program needn't handle non-finite values.
Results may differ from the reference program's by a relative error of at most 0.013.
Values may be sent and summed in bfloat16 or wider, within the bound.
No kernel may reach another device: no remote copies, remote signals or barrier semaphores. Data moves between devices by JAX's collectives and lax.ppermute only.
A program may use at most 64 MiB of HBM per device.

```python
import math
import jax
import jax.numpy as jnp
from jax import lax

C = 512
HID = 2048
KS = 7
HGT = 64
WID = 1024


def spiked(values, key, source, target, parts, factor):
    owner, partner = [(jnp.arange(values.shape[axis_at]) // (values.shape[axis_at] // parts)).reshape([-1 if axis == axis_at else 1 for axis in range(values.ndim)]) for axis_at in (source, target)]
    chosen = jax.random.permutation(key, parts)[partner]
    strong = (owner == chosen) | (owner == (partner + parts // 2) % parts)
    return jnp.where(strong, factor * values, values)


def shard_levels(key, shape, cuts, low, top_value):
    loudness, own = 1.0, jax.random.fold_in(key, 6)
    for axis_at, parts in cuts:
        heights = jnp.exp(jax.random.uniform(jax.random.fold_in(own, axis_at), (parts,), jnp.float32, low / len(cuts), top_value / len(cuts)))
        loudness = loudness * jnp.repeat(heights, shape[axis_at] // parts).reshape([-1 if axis == axis_at else 1 for axis in range(len(shape))])
    return loudness


def centred(rng, dims, width, bound, cuts=(), kind=jnp.bfloat16):
    factor_of = shard_levels(rng, dims, cuts, -0.22, 0.18) if cuts else 1.0
    result = jax.random.normal(rng, dims, jnp.float32) * width * factor_of
    return jnp.minimum(jnp.maximum(result, -bound), bound).astype(kind)


def gaussian_with(own_key, extent, scale, limit, cuts, heavy, dtype=jnp.bfloat16):
    result = scale * jax.random.normal(own_key, extent, jnp.float32)
    if cuts:
        result = result * shard_levels(own_key, extent, cuts, -0.22, 0.18)
    return jnp.clip(spiked(result, jax.random.fold_in(own_key, 3), *heavy), -limit, limit).astype(dtype)


def setup_inputs(seed: int = 0) -> dict:
    seeds = jax.random.split(jax.random.key(seed), 8)
    return {
        "features": gaussian_with(seeds[0], (HGT, WID, C), 1.0, 6.0, ((0, 8), (1, 32)), (1, 2, 32, 2.75)),
        "kernel": centred(seeds[1], (KS, KS, C), (KS * KS) ** -0.5, 0.875, (), jnp.float32),
        "gain": jnp.clip(1.0 + 0.18 * jax.random.normal(seeds[2], (C,), jnp.float32), 0.1, 1.9),
        "w_expand": centred(seeds[3], (C, HID), C ** -0.5, 0.25),
        "w_reduce": centred(seeds[4], (HID, C), HID ** -0.5, 0.125),
        "layer_scale": jnp.clip(jnp.exp(jax.random.uniform(seeds[5], (C,), jnp.float32, math.log(0.25), math.log(2.0))), 0.25, 2.0),
        "cotangent": gaussian_with(seeds[6], (HGT, WID, C), 1.0, 6.0, ((0, 8), (1, 32)), (0, 2, 8, 2.0)),
    }


ROOT_TWO = math.sqrt(2.0)
INV_ROOT_TWO_PI = 1.0 / math.sqrt(2.0 * math.pi)

def gelu(value):
    return 0.5 * value * (1.0 + lax.erf(value / ROOT_TWO))

def gelu_slope(value):
    return 0.5 * (1.0 + lax.erf(value / ROOT_TWO)) + value * jnp.exp(-0.5 * value * value) * INV_ROOT_TWO_PI

def depthwise(padded, kernel, map_height, map_width, flip):
    total = jnp.zeros((map_height, map_width, padded.shape[2]), jnp.float32)
    side = kernel.shape[0]
    for first in range(side):
        for second in range(side):
            row_off = side - 1 - first if flip else first
            col_off = side - 1 - second if flip else second
            total = total + kernel[first, second] * padded[row_off:row_off + map_height, col_off:col_off + map_width]
    return total

def reference(features, kernel, gain, w_expand, w_reduce, layer_scale, cotangent):
    map_height, map_width = (features.shape[0], features.shape[1])
    reach = KS // 2
    multiplier = 1.0 / math.sqrt(map_height * map_width)
    xpad = jnp.pad(features.astype(jnp.float32), ((reach, reach), (reach, reach), (0, 0)))
    conv = depthwise(xpad, kernel, map_height, map_width, False)
    centered_input = conv - lax.optimization_barrier(jnp.mean(conv, axis=-1, keepdims=True))
    inverse_deviation = lax.rsqrt(lax.optimization_barrier(jnp.mean(centered_input * centered_input, axis=-1, keepdims=True)) + 1e-06)
    standardized_input = centered_input * inverse_deviation
    normalized_input = (standardized_input * gain).astype(jnp.bfloat16)

    def row_step(carry, item):
        nrow, grow = item
        pre = jnp.dot(nrow, w_expand, preferred_element_type=jnp.float32)
        act = gelu(pre).astype(jnp.bfloat16)
        branch = jnp.dot(act, w_reduce, preferred_element_type=jnp.float32)
        gflt = grow.astype(jnp.float32)
        dbranch = (gflt * layer_scale).astype(jnp.bfloat16)
        dscale = carry[2] + lax.optimization_barrier(jnp.sum(gflt * branch, axis=0))
        dreduce = carry[1] + jnp.dot(act.T, dbranch, preferred_element_type=jnp.float32)
        dact = jnp.dot(dbranch, w_reduce.T, preferred_element_type=jnp.float32)
        dpre = (dact * gelu_slope(pre)).astype(jnp.bfloat16)
        dexpand = carry[0] + jnp.dot(nrow.T, dpre, preferred_element_type=jnp.float32)
        normalized_gradient = jnp.dot(dpre, w_expand.T, preferred_element_type=jnp.float32)
        return ((dexpand, dreduce, dscale), normalized_gradient)
    start = (jnp.zeros(w_expand.shape, jnp.float32), jnp.zeros(w_reduce.shape, jnp.float32), jnp.zeros(layer_scale.shape, jnp.float32))
    (dexpand, dreduce, dscale), normalized_gradient = lax.scan(row_step, start, (normalized_input, cotangent))
    scaled_gain_gradient = lax.optimization_barrier(jnp.sum(normalized_gradient * standardized_input, axis=(0, 1))) * multiplier
    rescaled_output = normalized_gradient * gain
    conv_gradient = inverse_deviation * (rescaled_output - lax.optimization_barrier(jnp.mean(rescaled_output, axis=-1, keepdims=True)) - standardized_input * lax.optimization_barrier(jnp.mean(rescaled_output * standardized_input, axis=-1, keepdims=True)))
    pieces = []
    for first in range(KS):
        for second in range(KS):
            pieces.append(lax.optimization_barrier(jnp.sum(conv_gradient * xpad[first:first + map_height, second:second + map_width], axis=(0, 1))))
    grad_kernel = jnp.stack(pieces).reshape(KS, KS, -1) * multiplier
    dpad = jnp.pad(conv_gradient, ((reach, reach), (reach, reach), (0, 0)))
    back = depthwise(dpad, kernel, map_height, map_width, True)
    grad_features = (cotangent.astype(jnp.float32) + back).astype(jnp.bfloat16)
    return (grad_features, grad_kernel, scaled_gain_gradient, dscale * multiplier, dexpand * multiplier, dreduce * multiplier)
```

```python
import functools
import math

import jax
import jax.numpy as jnp
from jax import lax
from jax.experimental import pallas as pl
from jax.experimental.pallas import tpu as pltpu
from jax.sharding import Mesh
from jax.sharding import PartitionSpec as P

Y, CORE, X, Z = 4, 2, 4, 8
ROW, COL = ("y", "core"), ("x", "z")
INV_ROOT_TWO = 1.0 / math.sqrt(2.0)
INV_ROOT_TWO_PI = 1.0 / math.sqrt(2.0 * math.pi)
LANES = 128
LEFT = 8
SMALL = 64

NN = (((1,), (0,)), ((), ()))
NT = (((1,), (1,)), ((), ()))


def product(left, right, dims):
    return lax.dot_general(left, right, dims, preferred_element_type=jnp.float32)


def fill(padded, field, up, down, left, right, reach):
    height, width, channels = field.shape
    for block in range(channels // LANES):
        lanes = pl.ds(block * LANES, LANES)
        own = pl.ds(LEFT, width)
        padded[block, pl.ds(0, reach), own, :] = up[:, :, lanes].astype(jnp.float32)
        padded[block, pl.ds(reach, height), own, :] = field[:, :, lanes].astype(jnp.float32)
        padded[block, pl.ds(reach + height, reach), own, :] = down[:, :, lanes].astype(jnp.float32)
        padded[block, :, pl.ds(LEFT - reach, reach), :] = left[:, :, lanes].astype(jnp.float32)
        padded[block, :, pl.ds(LEFT + width, reach), :] = right[:, :, lanes].astype(jnp.float32)


def depthwise(padded, taps, block, first_col, height, side):
    reach = side // 2
    totals = [None] * height
    for second in range(side):
        columns = pl.ds(LEFT - reach + first_col + second, 8)
        rows = [padded[block, row, columns, :] for row in range(height + side - 1)]
        for first in range(side):
            weight = taps[block, pl.ds(first * side + second, 1), :]
            for row in range(height):
                term = weight * rows[row + first]
                totals[row] = term if totals[row] is None else totals[row] + term
    return totals


def forward_kernel(
    core_ref, field, up, down, left, right, taps, gain, expand_t, reduce, scale, cotangent,
    sent, kept, dpre_out, xhat_out, rstd_out, padded, dscale_out,
    conv, normed, dbranch, turned, chosen, expand_v, reduce_v, sems,
):
    core = core_ref[0]
    copies = [
        pltpu.make_async_copy(expand_t, expand_v, sems.at[0]),
        pltpu.make_async_copy(reduce, reduce_v, sems.at[1]),
    ]
    for copy in copies:
        copy.start()
    height, width, channels = field.shape
    blocks = channels // LANES
    side = 7
    fill(padded, field, up, down, left, right, side // 2)

    def conv_block(block, _):
        for first_col in range(0, width, 8):
            for row, total in enumerate(depthwise(padded, taps, block, first_col, height, side)):
                conv[block, pl.ds(row * width + first_col, 8), :] = total
        return 0

    lax.fori_loop(0, blocks, conv_block, 0)
    for row in range(height):
        pixels = pl.ds(row * width, width)
        values = [conv[block, pixels, :] for block in range(blocks)]
        mean = jnp.sum(sum(values), axis=-1, keepdims=True) / channels
        values = [value - mean for value in values]
        spread = jnp.sum(sum(value * value for value in values), axis=-1, keepdims=True) / channels
        rstd = lax.rsqrt(spread + 1e-06)
        rstd_out[pixels, :] = jnp.broadcast_to(rstd, (width, LANES))
        for block, value in enumerate(values):
            lanes = pl.ds(block * LANES, LANES)
            xhat = value * rstd
            xhat_out[block, pixels, :] = xhat
            normed[pixels, lanes] = (xhat * gain[:, lanes]).astype(jnp.bfloat16)
        dbranch[pixels, :] = (cotangent[row].astype(jnp.float32) * scale[...]).astype(jnp.bfloat16)
    turned[...] = normed[...].T
    part = channels // (Y * CORE)
    for y in range(Y):
        for own in range(CORE):
            owner = core if own else 1 - core
            chosen[pl.ds((own * Y + y) * part, part), :] = turned[
                pl.ds(pl.multiple_of((y * CORE + owner) * part, part), part), :
            ]
    dscale_out[...] = jnp.zeros_like(dscale_out)
    for copy in copies:
        copy.wait()
    step = reduce_v.shape[0] // (Y * CORE)
    per_x = step // X
    part_x = part // X
    wide = channels // step

    def hidden_block(y, _):
        for own, target in ((0, sent), (1, kept)):
            owner = core if own else 1 - core
            chunk = y * CORE + owner
            hidden = pl.ds(pl.multiple_of(chunk * step, step), step)
            pre = product(expand_v[hidden, :], normed[...], NT)
            dact = product(reduce_v[hidden, :], dbranch[...], NT)
            half = 0.5 * (1.0 + lax.erf(pre * INV_ROOT_TWO))
            slope = half + pre * jnp.exp(-0.5 * pre * pre) * INV_ROOT_TWO_PI
            act = (pre * half).astype(jnp.bfloat16)
            dpre = (dact * slope).astype(jnp.bfloat16)
            dpre_out[hidden, :] = dpre
            share = product(act, dbranch[...], NN)
            weighed = share * reduce_v[hidden, :].astype(jnp.float32)
            dscale_out[...] += jnp.sum(weighed.reshape(step // 8, 8, channels), axis=0)
            for x in range(X):
                target[y * X + x, pl.ds(0, per_x), :] = share[x * per_x : (x + 1) * per_x].astype(
                    jnp.bfloat16
                )
            share = product(chosen[...], dpre, NT).astype(jnp.bfloat16)
            rows = pl.ds(pl.multiple_of(per_x + (chunk // wide) * part_x, part_x), part_x)
            lanes = pl.ds(pl.multiple_of((chunk % wide) * step, step), step)
            for place in range(Y * X):
                for back, goal in ((0, sent), (1, kept)):
                    first = back * Y * part + place * part_x
                    goal[place, rows, lanes] = share[first : first + part_x]
        return 0

    lax.fori_loop(0, Y, hidden_block, 0)


def backward_kernel(
    multiplier, dpre, expand, xhat, rstd, padded, gain, dscale, scale, dconv_out, small, dconv
):
    height, width, channels = dconv_out.shape
    blocks = channels // LANES
    side = 7
    for block in range(blocks):
        lanes = pl.ds(block * LANES, LANES)
        dconv[block] = product(expand[lanes, :], dpre[...], NN).T
        small[block] = jnp.zeros_like(small[block])
    sums = [jnp.zeros((width, LANES), jnp.float32)] * blocks
    for row in range(height):
        pixels = pl.ds(row * width, width)
        grads = [dconv[block, pixels, :] for block in range(blocks)]
        hats = [xhat[block, pixels, :] for block in range(blocks)]
        sums = [total + grad * hat for total, grad, hat in zip(sums, grads, hats)]
        grads = [grad * gain[:, pl.ds(block * LANES, LANES)] for block, grad in enumerate(grads)]
        mean = jnp.sum(sum(grads), axis=-1, keepdims=True) / channels
        slant = sum(grad * hat for grad, hat in zip(grads, hats))
        slant = jnp.sum(slant, axis=-1, keepdims=True) / channels
        for block in range(blocks):
            value = rstd[pixels, :] * (grads[block] - mean - hats[block] * slant)
            dconv[block, pixels, :] = value
            dconv_out[row, :, pl.ds(block * LANES, LANES)] = value.astype(jnp.bfloat16)
    taps = side * side
    for block in range(blocks):
        lanes = pl.ds(block * LANES, LANES)
        total = jnp.sum(sums[block], axis=0, keepdims=True)
        small[block, pl.ds(taps, 1), :] = total * multiplier
        total = jnp.sum(dscale[:, lanes], axis=0, keepdims=True)
        small[block, pl.ds(taps + 1, 1), :] = total / scale[:, lanes] * multiplier

    def tap_block(block, _):
        for second in range(side):
            totals = [jnp.zeros((8, LANES), jnp.float32)] * side
            for first_col in range(0, width, 8):
                grads = [
                    dconv[block, pl.ds(row * width + first_col, 8), :] for row in range(height)
                ]
                columns = pl.ds(LEFT - side // 2 + first_col + second, 8)
                for row in range(height + side - 1):
                    value = padded[block, row, columns, :]
                    for first in range(max(0, row - height + 1), min(side, row + 1)):
                        totals[first] = totals[first] + grads[row - first] * value
            for first, total in enumerate(totals):
                total = jnp.sum(total, axis=0, keepdims=True) * multiplier
                small[block, pl.ds(first * side + second, 1), :] = total
        return 0

    lax.fori_loop(0, blocks, tap_block, 0)


def feature_kernel(field, up, down, left, right, taps, cotangent, out, padded):
    height, width, channels = field.shape
    side = 7
    fill(padded, field, up, down, left, right, side // 2)
    for block in range(channels // LANES):
        lanes = pl.ds(block * LANES, LANES)
        for first_col in range(0, width, 8):
            columns = pl.ds(first_col, 8)
            for row, total in enumerate(depthwise(padded, taps, block, first_col, height, side)):
                total = total + cotangent[row, columns, lanes].astype(jnp.float32)
                out[row, columns, lanes] = total.astype(jnp.bfloat16)


VMEM = pl.BlockSpec(memory_space=pltpu.VMEM)
ANY = pl.BlockSpec(memory_space=pl.ANY)
SMEM = pl.BlockSpec(memory_space=pltpu.SMEM)
PARAMS = pltpu.CompilerParams(vmem_limit_bytes=40 << 20)


def shifted(value, axes, by):
    count = lax.axis_size(axes)
    pairs = [(i, i + by) for i in range(count) if 0 <= i + by < count]
    return lax.ppermute(value, axes, pairs)


def borders(field, reach):
    up = shifted(field[-reach:], ROW, 1)
    down = shifted(field[:reach], ROW, -1)
    left, right = (
        jnp.concatenate([part[:, columns] for part in (up, field, down)])
        for columns in (slice(-reach, None), slice(0, reach))
    )
    return up, down, shifted(left, COL, 1), shifted(right, COL, -1)


def exchanged(chunks, axes):
    return lax.all_to_all(chunks, axes, 0, 0, tiled=True)


def summed(chunks):
    return jnp.sum(chunks.astype(jnp.float32), axis=0)


def everywhere(small):
    chunks = exchanged(small.reshape(Y * CORE * X, 8, LANES), ("y", "core", "x"))
    part = summed(chunks)
    part = summed(exchanged(jnp.broadcast_to(part, (Z, *part.shape)), "z"))
    full = exchanged(jnp.broadcast_to(part, (Y * CORE * X, *part.shape)), ("y", "core", "x"))
    return full.reshape(small.shape)


def shards(features, kernel, gain, w_expand, w_reduce, layer_scale, cotangent):
    height, width, channels = features.shape
    hidden = w_reduce.shape[0]
    side = kernel.shape[0]
    taps_total = side * side
    reach = side // 2
    blocks = channels // LANES
    pixels = height * width
    multiplier = 1.0 / math.sqrt(pixels * lax.axis_size(ROW) * lax.axis_size(COL))
    taps = kernel.reshape(taps_total, blocks, LANES).transpose(1, 0, 2)
    flipped = taps[:, ::-1]
    gain_row = gain.reshape(1, channels)
    scale_row = layer_scale.reshape(1, channels)
    core = lax.axis_index("core").reshape(1)
    places = Y * X
    rows = hidden // (Y * CORE * X)
    f32, bf16 = jnp.float32, jnp.bfloat16
    shape = jax.ShapeDtypeStruct
    padded_shape = (blocks, height + side - 1, LEFT + width + 8, LANES)

    sent, kept, dpre, xhat, rstd, padded, dscale = pl.pallas_call(
        forward_kernel,
        name="forward",
        in_specs=[SMEM] + [VMEM] * 7 + [ANY] * 2 + [VMEM] * 2,
        out_specs=[VMEM] * 7,
        out_shape=[
            shape((places, 2 * rows, channels), bf16),
            shape((places, 2 * rows, channels), bf16),
            shape((hidden, pixels), bf16),
            shape((blocks, pixels, LANES), f32),
            shape((pixels, LANES), f32),
            shape(padded_shape, f32),
            shape((8, channels), f32),
        ],
        scratch_shapes=[
            pltpu.VMEM((blocks, pixels, LANES), f32),
            pltpu.VMEM((pixels, channels), bf16),
            pltpu.VMEM((pixels, channels), bf16),
            pltpu.VMEM((channels, pixels), bf16),
            pltpu.VMEM((channels, pixels), bf16),
            pltpu.VMEM((hidden, channels), bf16),
            pltpu.VMEM((hidden, channels), bf16),
            pltpu.SemaphoreType.DMA((2,)),
        ],
        compiler_params=PARAMS,
    )(
        core, features, *borders(features, reach), taps, gain_row, w_expand.T, w_reduce,
        scale_row, cotangent,
    )

    came = lax.ppermute(sent, "core", [(0, 1), (1, 0)])
    chip = (kept.astype(f32) + came.astype(f32)).astype(bf16)
    plane = summed(exchanged(chip, ("y", "x")))
    first = plane[:rows].reshape(Z, -1, channels)
    second = plane[rows:].reshape(hidden // channels, Z, -1, channels).transpose(1, 2, 0, 3)
    second = second.reshape(Z, -1, channels)
    line = jnp.concatenate([first, second], axis=1).astype(bf16)
    own = summed(exchanged(line, "z")) * multiplier
    dreduce = own[: rows // Z]
    dexpand = own[rows // Z :].reshape(-1, hidden)

    dconv, small = pl.pallas_call(
        functools.partial(backward_kernel, multiplier),
        name="backward",
        in_specs=[VMEM] * 8,
        out_specs=[VMEM] * 2,
        out_shape=[
            shape((height, width, channels), bf16),
            shape((blocks, SMALL, LANES), f32),
        ],
        scratch_shapes=[pltpu.VMEM((blocks, pixels, LANES), f32)],
        compiler_params=PARAMS,
    )(dpre, w_expand, xhat, rstd, padded, gain_row, dscale, scale_row)

    small = everywhere(small).transpose(1, 0, 2).reshape(SMALL, channels)
    grad_features = pl.pallas_call(
        feature_kernel,
        name="features",
        in_specs=[VMEM] * 7,
        out_specs=VMEM,
        out_shape=shape((height, width, channels), bf16),
        scratch_shapes=[pltpu.VMEM(padded_shape, f32)],
        compiler_params=PARAMS,
    )(dconv, *borders(dconv, reach), flipped, cotangent)
    return (
        grad_features,
        small[:taps_total].reshape(side, side, channels),
        small[taps_total],
        small[taps_total + 1],
        dexpand,
        dreduce,
    )


def solution(mesh):
    pixels = P(ROW, COL, None)
    return jax.shard_map(
        shards,
        mesh=Mesh(mesh.devices.reshape(Y, CORE, X, Z), (*ROW, *COL)),
        in_specs=(pixels, P(), P(), P(), P(), P(), pixels),
        out_specs=(pixels, P(), P(), P(), P((*ROW, *COL), None), P((*ROW, *COL), None)),
        check_vma=False,
    )
```

```python
import functools
import math

import jax
import jax.numpy as jnp
from jax import lax
from jax.experimental import pallas as pl
from jax.experimental.pallas import tpu as pltpu
from jax.sharding import Mesh
from jax.sharding import PartitionSpec as P

Y, CORE, X, Z = 4, 2, 4, 8
ROW, COL = ("y", "core"), ("x", "z")
INV_ROOT_TWO = 1.0 / math.sqrt(2.0)
INV_ROOT_TWO_PI = 1.0 / math.sqrt(2.0 * math.pi)
LANES = 128
LEFT = 8
SMALL = 64

NN = (((1,), (0,)), ((), ()))
NT = (((1,), (1,)), ((), ()))
TN = (((0,), (0,)), ((), ()))


def product(left, right, dims):
    return lax.dot_general(left, right, dims, preferred_element_type=jnp.float32)


def fill(padded, field, up, down, left, right, reach):
    height, width, channels = field.shape
    for block in range(channels // LANES):
        lanes = pl.ds(block * LANES, LANES)
        own = pl.ds(LEFT, width)
        padded[block, pl.ds(0, reach), own, :] = up[:, :, lanes].astype(jnp.float32)
        padded[block, pl.ds(reach, height), own, :] = field[:, :, lanes].astype(jnp.float32)
        padded[block, pl.ds(reach + height, reach), own, :] = down[:, :, lanes].astype(jnp.float32)
        padded[block, :, pl.ds(LEFT - reach, reach), :] = left[:, :, lanes].astype(jnp.float32)
        padded[block, :, pl.ds(LEFT + width, reach), :] = right[:, :, lanes].astype(jnp.float32)


def depthwise(padded, taps, block, first_col, height, side):
    reach = side // 2
    totals = [None] * height
    for second in range(side):
        columns = pl.ds(LEFT - reach + first_col + second, 8)
        rows = [padded[block, row, columns, :] for row in range(height + side - 1)]
        for first in range(side):
            weight = taps[block, pl.ds(first * side + second, 1), :]
            for row in range(height):
                term = weight * rows[row + first]
                totals[row] = term if totals[row] is None else totals[row] + term
    return totals


def forward_kernel(
    core_ref, field, up, down, left, right, taps, gain, expand, reduce, scale, cotangent,
    sent, kept, dpre_out, xhat_out, rstd_out, padded, dscale_out,
    conv, normed, dbranch, turned, chosen, expand_v, reduce_v, sems,
):
    core = core_ref[0]
    copies = [
        pltpu.make_async_copy(expand, expand_v, sems.at[0]),
        pltpu.make_async_copy(reduce, reduce_v, sems.at[1]),
    ]
    for copy in copies:
        copy.start()
    height, width, channels = field.shape
    blocks = channels // LANES
    side = 7
    fill(padded, field, up, down, left, right, side // 2)

    def conv_block(block, _):
        for first_col in range(0, width, 8):
            for row, total in enumerate(depthwise(padded, taps, block, first_col, height, side)):
                conv[block, pl.ds(row * width + first_col, 8), :] = total
        return 0

    lax.fori_loop(0, blocks, conv_block, 0)
    for row in range(height):
        pixels = pl.ds(row * width, width)
        values = [conv[block, pixels, :] for block in range(blocks)]
        mean = jnp.sum(sum(values), axis=-1, keepdims=True) / channels
        values = [value - mean for value in values]
        spread = jnp.sum(sum(value * value for value in values), axis=-1, keepdims=True) / channels
        rstd = lax.rsqrt(spread + 1e-06)
        rstd_out[pixels, :] = jnp.broadcast_to(rstd, (width, LANES))
        for block, value in enumerate(values):
            lanes = pl.ds(block * LANES, LANES)
            xhat = value * rstd
            xhat_out[block, pixels, :] = xhat
            normed[pixels, lanes] = (xhat * gain[:, lanes]).astype(jnp.bfloat16)
        dbranch[pixels, :] = (cotangent[row].astype(jnp.float32) * scale[...]).astype(jnp.bfloat16)
    turned[...] = normed[...].T
    part = channels // (Y * CORE)
    for y in range(Y):
        for own in range(CORE):
            owner = core if own else 1 - core
            chosen[pl.ds((own * Y + y) * part, part), :] = turned[
                pl.ds(pl.multiple_of((y * CORE + owner) * part, part), part), :
            ]
    dscale_out[...] = jnp.zeros_like(dscale_out)
    for copy in copies:
        copy.wait()
    step = reduce_v.shape[0] // (Y * CORE)
    per_x = step // X
    part_x = part // X
    wide = channels // step

    def hidden_block(y, _):
        for own, target in ((0, sent), (1, kept)):
            owner = core if own else 1 - core
            chunk = y * CORE + owner
            hidden = pl.ds(pl.multiple_of(chunk * step, step), step)
            pre = product(normed[...], expand_v[:, hidden], NN)
            dact = product(dbranch[...], reduce_v[hidden, :], NT)
            half = 0.5 * (1.0 + lax.erf(pre * INV_ROOT_TWO))
            slope = half + pre * jnp.exp(-0.5 * pre * pre) * INV_ROOT_TWO_PI
            act = (pre * half).astype(jnp.bfloat16)
            dpre = (dact * slope).astype(jnp.bfloat16)
            dpre_out[:, hidden] = dpre
            share = product(act, dbranch[...], TN)
            weighed = share * reduce_v[hidden, :].astype(jnp.float32)
            dscale_out[...] += jnp.sum(weighed.reshape(step // 8, 8, channels), axis=0)
            for x in range(X):
                target[y * X + x, pl.ds(0, per_x), :] = share[x * per_x : (x + 1) * per_x].astype(
                    jnp.bfloat16
                )
            share = product(chosen[...], dpre, NN).astype(jnp.bfloat16)
            rows = pl.ds(pl.multiple_of(per_x + (chunk // wide) * part_x, part_x), part_x)
            lanes = pl.ds(pl.multiple_of((chunk % wide) * step, step), step)
            for place in range(Y * X):
                for back, goal in ((0, sent), (1, kept)):
                    first = back * Y * part + place * part_x
                    goal[place, rows, lanes] = share[first : first + part_x]
        return 0

    lax.fori_loop(0, Y, hidden_block, 0)


def backward_kernel(
    multiplier, dpre, expand, xhat, rstd, padded, gain, dscale, scale, dconv_out, small, dconv
):
    height, width, channels = dconv_out.shape
    blocks = channels // LANES
    side = 7
    dnormed = product(dpre[...], expand[...], NT)
    for block in range(blocks):
        dconv[block] = dnormed[:, block * LANES : (block + 1) * LANES]
    sums = [jnp.zeros((width, LANES), jnp.float32)] * blocks
    for row in range(height):
        pixels = pl.ds(row * width, width)
        grads = [dconv[block, pixels, :] for block in range(blocks)]
        hats = [xhat[block, pixels, :] for block in range(blocks)]
        sums = [total + grad * hat for total, grad, hat in zip(sums, grads, hats)]
        grads = [grad * gain[:, pl.ds(block * LANES, LANES)] for block, grad in enumerate(grads)]
        mean = jnp.sum(sum(grads), axis=-1, keepdims=True) / channels
        slant = sum(grad * hat for grad, hat in zip(grads, hats))
        slant = jnp.sum(slant, axis=-1, keepdims=True) / channels
        for block in range(blocks):
            value = rstd[pixels, :] * (grads[block] - mean - hats[block] * slant)
            dconv[block, pixels, :] = value
            dconv_out[row, :, pl.ds(block * LANES, LANES)] = value.astype(jnp.bfloat16)
    taps = side * side
    small[pl.ds(taps + 2, SMALL - taps - 2), :] = jnp.zeros(
        (SMALL - taps - 2, channels), jnp.float32
    )
    for block in range(blocks):
        lanes = pl.ds(block * LANES, LANES)
        total = jnp.sum(sums[block], axis=0, keepdims=True)
        small[pl.ds(taps, 1), lanes] = total * multiplier
        total = jnp.sum(dscale[:, lanes], axis=0, keepdims=True)
        small[pl.ds(taps + 1, 1), lanes] = total / scale[:, lanes] * multiplier

    def tap_block(block, _):
        lanes = pl.ds(pl.multiple_of(block * LANES, LANES), LANES)
        for second in range(side):
            totals = [jnp.zeros((8, LANES), jnp.float32)] * side
            for first_col in range(0, width, 8):
                grads = [
                    dconv[block, pl.ds(row * width + first_col, 8), :] for row in range(height)
                ]
                columns = pl.ds(LEFT - side // 2 + first_col + second, 8)
                for row in range(height + side - 1):
                    value = padded[block, row, columns, :]
                    for first in range(max(0, row - height + 1), min(side, row + 1)):
                        totals[first] = totals[first] + grads[row - first] * value
            for first, total in enumerate(totals):
                total = jnp.sum(total, axis=0, keepdims=True) * multiplier
                small[pl.ds(first * side + second, 1), lanes] = total
        return 0

    lax.fori_loop(0, blocks, tap_block, 0)


def feature_kernel(field, up, down, left, right, taps, cotangent, out, padded):
    height, width, channels = field.shape
    side = 7
    fill(padded, field, up, down, left, right, side // 2)
    for block in range(channels // LANES):
        lanes = pl.ds(block * LANES, LANES)
        for first_col in range(0, width, 8):
            columns = pl.ds(first_col, 8)
            for row, total in enumerate(depthwise(padded, taps, block, first_col, height, side)):
                total = total + cotangent[row, columns, lanes].astype(jnp.float32)
                out[row, columns, lanes] = total.astype(jnp.bfloat16)


def merge_kernel(kept, came, small, small_came, out):
    rows = kept.shape[1]
    out[:, pl.ds(0, rows), :] = (
        kept[...].astype(jnp.float32) + came[...].astype(jnp.float32)
    ).astype(jnp.bfloat16)
    total = small[...] + small_came[...]
    high = total.astype(jnp.bfloat16)
    low = (total - high.astype(jnp.float32)).astype(jnp.bfloat16)
    out[:, pl.ds(rows, 2 * total.shape[1]), :] = jnp.concatenate([high, low], axis=1)


def plane_kernel(chunks, out, total):
    total[...] = jnp.sum(chunks[...].astype(jnp.float32), axis=0)
    rows = total.shape[0] - 8
    each = rows // 2 // Z
    wide = rows // 2 // (2 * Z)
    small = total[pl.ds(rows, 4), :] + total[pl.ds(rows + 4, 4), :]
    high = small.astype(jnp.bfloat16).astype(jnp.float32)
    for z in range(Z):
        parts = [total[pl.ds(z * each, each), :]]
        parts += [
            total[pl.ds(rows // 2 + q * 2 * Z + 2 * z, 2), :] for q in range(wide)
        ]
        out[z] = jnp.concatenate([*parts, high, small - high]).astype(jnp.bfloat16)


def line_kernel(multiplier, chunks, dreduce, dexpand, small):
    total = jnp.sum(chunks[...].astype(jnp.float32), axis=0)
    each, channels = dreduce.shape
    dreduce[...] = total[:each] * multiplier
    for q in range(dexpand.shape[1] // channels):
        first = each + 2 * q
        dexpand[:, pl.ds(q * channels, channels)] = total[first : first + 2] * multiplier
    part = total[2 * each : 2 * each + 4] + total[2 * each + 4 :]
    small[...] = jnp.broadcast_to(part[None], small.shape)


def small_kernel(full, dkernel, dgain, dscale):
    side = dkernel.shape[0]
    for place in range(side * side):
        dkernel[place // side, pl.ds(place % side, 1), :] = full[place // 4, pl.ds(place % 4, 1), :]
    for place, out in ((side * side, dgain), (side * side + 1, dscale)):
        out[...] = full[place // 4, pl.ds(place % 4, 1), :]


VMEM = pl.BlockSpec(memory_space=pltpu.VMEM)
HBM = pl.BlockSpec(memory_space=pltpu.HBM)
SMEM = pl.BlockSpec(memory_space=pltpu.SMEM)
PARAMS = pltpu.CompilerParams(vmem_limit_bytes=24 << 20)


def shifted(value, axes, by):
    count = lax.axis_size(axes)
    pairs = [(i, i + by) for i in range(count) if 0 <= i + by < count]
    return lax.ppermute(value, axes, pairs)


def borders(field, reach):
    up = shifted(field[-reach:], ROW, 1)
    down = shifted(field[:reach], ROW, -1)
    left, right = (
        jnp.concatenate([part[:, columns] for part in (up, field, down)])
        for columns in (slice(-reach, None), slice(0, reach))
    )
    return up, down, shifted(left, COL, 1), shifted(right, COL, -1)


def exchanged(chunks, axes):
    return lax.all_to_all(chunks, axes, 0, 0, tiled=True)


def shards(features, kernel, gain, w_expand, w_reduce, layer_scale, cotangent):
    height, width, channels = features.shape
    hidden = w_reduce.shape[0]
    side = kernel.shape[0]
    taps_total = side * side
    reach = side // 2
    blocks = channels // LANES
    pixels = height * width
    multiplier = 1.0 / math.sqrt(pixels * lax.axis_size(ROW) * lax.axis_size(COL))
    taps = kernel.reshape(taps_total, blocks, LANES).transpose(1, 0, 2)
    flipped = taps[:, ::-1]
    gain_row = gain.reshape(1, channels)
    scale_row = layer_scale.reshape(1, channels)
    core = lax.axis_index("core").reshape(1)
    places = Y * X
    rows = hidden // (Y * CORE * X)
    f32, bf16 = jnp.float32, jnp.bfloat16
    shape = jax.ShapeDtypeStruct
    padded_shape = (blocks, height + side - 1, LEFT + width + 8, LANES)

    sent, kept, dpre, xhat, rstd, padded, dscale = pl.pallas_call(
        forward_kernel,
        name="forward",
        in_specs=[SMEM] + [VMEM] * 7 + [HBM] * 2 + [VMEM] * 2,
        out_specs=[VMEM] * 7,
        out_shape=[
            shape((places, 2 * rows, channels), bf16),
            shape((places, 2 * rows, channels), bf16),
            shape((pixels, hidden), bf16),
            shape((blocks, pixels, LANES), f32),
            shape((pixels, LANES), f32),
            shape(padded_shape, f32),
            shape((8, channels), f32),
        ],
        scratch_shapes=[
            pltpu.VMEM((blocks, pixels, LANES), f32),
            pltpu.VMEM((pixels, channels), bf16),
            pltpu.VMEM((pixels, channels), bf16),
            pltpu.VMEM((channels, pixels), bf16),
            pltpu.VMEM((channels, pixels), bf16),
            pltpu.VMEM((channels, hidden), bf16),
            pltpu.VMEM((hidden, channels), bf16),
            pltpu.SemaphoreType.DMA((2,)),
        ],
        compiler_params=PARAMS,
    )(
        core, features, *borders(features, reach), taps, gain_row,
        pltpu.with_memory_space_constraint(w_expand, pltpu.HBM),
        pltpu.with_memory_space_constraint(w_reduce, pltpu.HBM),

        scale_row, cotangent,
    )

    swap = [(0, 1), (1, 0)]
    came = lax.ppermute(sent, "core", swap)
    dconv, small = pl.pallas_call(
        functools.partial(backward_kernel, multiplier),
        name="backward",
        in_specs=[VMEM] * 8,
        out_specs=[VMEM] * 2,
        out_shape=[
            shape((height, width, channels), bf16),
            shape((SMALL, channels), f32),
        ],
        scratch_shapes=[pltpu.VMEM((blocks, pixels, LANES), f32)],
        compiler_params=PARAMS,
    )(dpre, w_expand, xhat, rstd, padded, gain_row, dscale, scale_row)

    small_came = lax.ppermute(small, "core", swap)
    each = SMALL // places
    whole = 2 * rows + 2 * each
    chip = pl.pallas_call(
        merge_kernel,
        name="merge",
        grid=(Y,),
        in_specs=[pl.BlockSpec((X, 2 * rows, channels), lambda i: (i, 0, 0))] * 2
        + [pl.BlockSpec((X, each, channels), lambda i: (i, 0, 0))] * 2,
        out_specs=pl.BlockSpec((X, whole, channels), lambda i: (i, 0, 0)),
        out_shape=shape((places, whole, channels), bf16),
        compiler_params=PARAMS,
    )(
        kept, came, small.reshape(places, each, channels),
        small_came.reshape(places, each, channels),
    )
    chip, dconv = lax.optimization_barrier((chip, dconv))
    chunks, edges = lax.optimization_barrier((exchanged(chip, ("y", "x")), borders(dconv, reach)))
    line = pl.pallas_call(
        plane_kernel,
        name="plane",
        in_specs=[VMEM],
        out_specs=VMEM,
        out_shape=shape((Z, 2 * rows // Z + 2 * each, channels), bf16),
        scratch_shapes=[pltpu.VMEM((whole, channels), f32)],
        compiler_params=PARAMS,
    )(chunks)
    dreduce, dexpand, part = pl.pallas_call(
        functools.partial(line_kernel, multiplier),
        name="line",
        in_specs=[VMEM],
        out_specs=[VMEM] * 3,
        out_shape=[
            shape((rows // Z, channels), f32),
            shape((channels * rows // Z // hidden, hidden), f32),
            shape((places, each, channels), f32),
        ],
        compiler_params=PARAMS,
    )(exchanged(line, "z"))
    dkernel, dgain, dscale = pl.pallas_call(
        small_kernel,
        name="small",
        in_specs=[VMEM],
        out_specs=[VMEM] * 3,
        out_shape=[shape((side, side, channels), f32)] + [shape((1, channels), f32)] * 2,
        compiler_params=PARAMS,
    )(exchanged(part, ("y", "x")))
    grad_features = pl.pallas_call(
        feature_kernel,
        name="features",
        in_specs=[VMEM] * 7,
        out_specs=VMEM,
        out_shape=shape((height, width, channels), bf16),
        scratch_shapes=[pltpu.VMEM(padded_shape, f32)],
        compiler_params=PARAMS,
    )(dconv, *edges, flipped, cotangent)
    return (
        grad_features,
        dkernel,
        dgain.reshape(channels),
        dscale.reshape(channels),
        dexpand,
        dreduce,
    )


def solution(mesh):
    pixels = P(ROW, COL, None)
    return jax.shard_map(
        shards,
        mesh=Mesh(mesh.devices.reshape(Y, CORE, X, Z), (*ROW, *COL)),
        in_specs=(pixels, P(), P(), P(), P(), P(), pixels),
        out_specs=(pixels, P(), P(), P(), P((*ROW, *COL), None), P((*ROW, *COL), None)),
        check_vma=False,
    )
```

```python
import functools
import math

import jax
import jax.numpy as jnp
from jax import lax
from jax.experimental import pallas as pl
from jax.experimental.pallas import tpu as pltpu
from jax.sharding import Mesh
from jax.sharding import PartitionSpec as P

Y, CORE, X, Z = 4, 2, 4, 8
ROW, COL = ("y", "core"), ("x", "z")
INV_ROOT_TWO = 1.0 / math.sqrt(2.0)
INV_ROOT_TWO_PI = 1.0 / math.sqrt(2.0 * math.pi)
LANES = 128
LEFT = 8
SMALL = 64

NN = (((1,), (0,)), ((), ()))
NT = (((1,), (1,)), ((), ()))
TN = (((0,), (0,)), ((), ()))


def product(left, right, dims):
    return lax.dot_general(left, right, dims, preferred_element_type=jnp.float32)


def fill(padded, field, up, down, left, right, reach):
    height, width, channels = field.shape
    for block in range(channels // LANES):
        lanes = pl.ds(block * LANES, LANES)
        own = pl.ds(LEFT, width)
        padded[block, pl.ds(0, reach), own, :] = up[:, :, lanes].astype(jnp.float32)
        padded[block, pl.ds(reach, height), own, :] = field[:, :, lanes].astype(jnp.float32)
        padded[block, pl.ds(reach + height, reach), own, :] = down[:, :, lanes].astype(jnp.float32)
        padded[block, :, pl.ds(LEFT - reach, reach), :] = left[:, :, lanes].astype(jnp.float32)
        padded[block, :, pl.ds(LEFT + width, reach), :] = right[:, :, lanes].astype(jnp.float32)


def depthwise(padded, taps, block, first_col, height, side, flip):
    reach = side // 2
    totals = [None] * height
    lanes = pl.ds(pl.multiple_of(block * LANES, LANES), LANES)
    for second in range(side):
        columns = pl.ds(LEFT - reach + first_col + second, 8)
        rows = [padded[block, row, columns, :] for row in range(height + side - 1)]
        for first in range(side):
            if flip:
                weight = taps[side - 1 - first, pl.ds(side - 1 - second, 1), lanes]
            else:
                weight = taps[first, pl.ds(second, 1), lanes]
            for row in range(height):
                term = weight * rows[row + first]
                totals[row] = term if totals[row] is None else totals[row] + term
    return totals


def forward_kernel(
    core_ref, field_h, up, down, left, right, taps_h, gain_h, expand_h, reduce_h, scale_h,
    cotangent_h,
    sent_e, kept_e, sent_r, kept_r, dpre_out, xhat_out, rstd_out, padded, rows_out,
    conv, normed, dbranch, turned, chosen, field, taps, gain, expand, reduce, scale, cotangent,
    sems,
):
    core = core_ref[0]
    copies = [
        pltpu.make_async_copy(source, target, sems.at[i])
        for i, (source, target) in enumerate(
            (
                (field_h, field),
                (taps_h, taps),
                (gain_h, gain),
                (scale_h, scale),
                (cotangent_h, cotangent),
                (expand_h, expand),
                (reduce_h, reduce),
            )
        )
    ]
    for copy in copies:
        copy.start()
    for copy in copies[:2]:
        copy.wait()
    height, width, channels = field.shape
    blocks = channels // LANES
    side = 7
    fill(padded, field, up, down, left, right, side // 2)

    def conv_block(block, _):
        for first_col in range(0, width, 8):
            for row, total in enumerate(
                depthwise(padded, taps, block, first_col, height, side, False)
            ):
                conv[block, pl.ds(row * width + first_col, 8), :] = total
        return 0

    lax.fori_loop(0, blocks, conv_block, 0)
    for copy in copies[2:5]:
        copy.wait()
    for row in range(height):
        pixels = pl.ds(row * width, width)
        values = [conv[block, pixels, :] for block in range(blocks)]
        mean = jnp.sum(sum(values), axis=-1, keepdims=True) / channels
        values = [value - mean for value in values]
        spread = jnp.sum(sum(value * value for value in values), axis=-1, keepdims=True) / channels
        rstd = lax.rsqrt(spread + 1e-06)
        rstd_out[pixels, :] = jnp.broadcast_to(rstd, (width, LANES))
        for block, value in enumerate(values):
            lanes = pl.ds(block * LANES, LANES)
            xhat = value * rstd
            xhat_out[block, pixels, :] = xhat
            normed[pixels, lanes] = (xhat * gain[:, lanes]).astype(jnp.bfloat16)
        dbranch[pixels, :] = (cotangent[row].astype(jnp.float32) * scale[...]).astype(jnp.bfloat16)
    turned[...] = normed[...].T
    part = channels // (Y * CORE)
    for y in range(Y):
        for own in range(CORE):
            owner = core if own else 1 - core
            chosen[pl.ds((own * Y + y) * part, part), :] = turned[
                pl.ds(pl.multiple_of((y * CORE + owner) * part, part), part), :
            ]
    rows_out[pl.ds(0, 8), :] = jnp.zeros((8, channels), jnp.float32)
    rows_out[pl.ds(8, 8), :] = jnp.broadcast_to(gain[...], (8, channels))
    rows_out[pl.ds(16, 8), :] = jnp.broadcast_to(scale[...], (8, channels))
    for copy in copies[5:]:
        copy.wait()
    step = reduce.shape[0] // (Y * CORE)
    per_z = step // (X * Z)
    part_x = part // X
    wide = channels // step

    def hidden_block(y, _):
        for own, target in ((0, sent_r), (1, kept_r)):
            owner = core if own else 1 - core
            chunk = y * CORE + owner
            hidden = pl.ds(pl.multiple_of(chunk * step, step), step)
            pre = product(normed[...], expand[:, hidden], NN)
            dact = product(dbranch[...], reduce[hidden, :], NT)
            half = 0.5 * (1.0 + lax.erf(pre * INV_ROOT_TWO))
            slope = half + pre * jnp.exp(-0.5 * pre * pre) * INV_ROOT_TWO_PI
            act = (pre * half).astype(jnp.bfloat16)
            dpre = (dact * slope).astype(jnp.bfloat16)
            dpre_out[:, hidden] = dpre
            share = product(act, dbranch[...], TN)
            weighed = share * reduce[hidden, :].astype(jnp.float32)
            rows_out[pl.ds(0, 8), :] += jnp.sum(weighed.reshape(step // 8, 8, channels), axis=0)
            share = share.astype(jnp.bfloat16)
            for place in range(X * Z):
                x, z = place // Z, place % Z
                target[z, y * X + x] = share[place * per_z : (place + 1) * per_z]
            share = product(chosen[...], dpre, NN).astype(jnp.bfloat16)
            rows = pl.ds(pl.multiple_of((chunk // wide) * part_x, part_x), part_x)
            lanes = pl.ds(pl.multiple_of((chunk % wide) * step, step), step)
            for place in range(Y * X):
                for back, goal in ((0, sent_e), (1, kept_e)):
                    first = back * Y * part + place * part_x
                    goal[place, rows, lanes] = share[first : first + part_x]
        return 0

    lax.fori_loop(0, Y, hidden_block, 0)


def backward_kernel(
    multiplier, dpre, expand, xhat, rstd, padded, rows, dconv_out, small, dconv
):
    height, width, channels = dconv_out.shape
    blocks = channels // LANES
    side = 7
    dnormed = product(dpre[...], expand[...], NT)
    for block in range(blocks):
        dconv[block] = dnormed[:, block * LANES : (block + 1) * LANES]
    sums = [jnp.zeros((width, LANES), jnp.float32)] * blocks
    for row in range(height):
        pixels = pl.ds(row * width, width)
        grads = [dconv[block, pixels, :] for block in range(blocks)]
        hats = [xhat[block, pixels, :] for block in range(blocks)]
        sums = [total + grad * hat for total, grad, hat in zip(sums, grads, hats)]
        grads = [grad * rows[pl.ds(8, 1), pl.ds(block * LANES, LANES)] for block, grad in enumerate(grads)]
        mean = jnp.sum(sum(grads), axis=-1, keepdims=True) / channels
        slant = sum(grad * hat for grad, hat in zip(grads, hats))
        slant = jnp.sum(slant, axis=-1, keepdims=True) / channels
        for block in range(blocks):
            value = rstd[pixels, :] * (grads[block] - mean - hats[block] * slant)
            dconv[block, pixels, :] = value
            dconv_out[row, :, pl.ds(block * LANES, LANES)] = value.astype(jnp.bfloat16)
    taps = side * side
    small[pl.ds(taps + 2, SMALL - taps - 2), :] = jnp.zeros(
        (SMALL - taps - 2, channels), jnp.float32
    )
    for block in range(blocks):
        lanes = pl.ds(block * LANES, LANES)
        total = jnp.sum(sums[block], axis=0, keepdims=True)
        small[pl.ds(taps, 1), lanes] = total * multiplier
        total = jnp.sum(rows[pl.ds(0, 8), lanes], axis=0, keepdims=True)
        small[pl.ds(taps + 1, 1), lanes] = total / rows[pl.ds(16, 1), lanes] * multiplier

    def tap_block(block, _):
        lanes = pl.ds(pl.multiple_of(block * LANES, LANES), LANES)
        for second in range(side):
            totals = [jnp.zeros((8, LANES), jnp.float32)] * side
            for first_col in range(0, width, 8):
                grads = [
                    dconv[block, pl.ds(row * width + first_col, 8), :] for row in range(height)
                ]
                columns = pl.ds(LEFT - side // 2 + first_col + second, 8)
                for row in range(height + side - 1):
                    value = padded[block, row, columns, :]
                    for first in range(max(0, row - height + 1), min(side, row + 1)):
                        totals[first] = totals[first] + grads[row - first] * value
            for first, total in enumerate(totals):
                total = jnp.sum(total, axis=0, keepdims=True) * multiplier
                small[pl.ds(first * side + second, 1), lanes] = total
        return 0

    lax.fori_loop(0, blocks, tap_block, 0)


def feature_kernel(field, up, down, left, right, taps, cotangent, out, padded):
    height, width, channels = field.shape
    side = 7
    fill(padded, field, up, down, left, right, side // 2)
    for block in range(channels // LANES):
        lanes = pl.ds(block * LANES, LANES)
        for first_col in range(0, width, 8):
            columns = pl.ds(first_col, 8)
            for row, total in enumerate(
                depthwise(padded, taps, block, first_col, height, side, True)
            ):
                total = total + cotangent[row, columns, lanes].astype(jnp.float32)
                out[row, columns, lanes] = total.astype(jnp.bfloat16)


def halves(value):
    high = value.astype(jnp.bfloat16)
    return high, (value - high.astype(jnp.float32)).astype(jnp.bfloat16)


def added(left, right):
    return (left.astype(jnp.float32) + right.astype(jnp.float32)).astype(jnp.bfloat16)


def merge_kernel(kept, came, small, small_came, out):
    rows = kept.shape[1]
    out[:, pl.ds(0, rows), :] = added(kept[...], came[...])
    total = small[...] + small_came[...]
    out[:, pl.ds(rows, 2 * total.shape[1]), :] = jnp.concatenate(halves(total), axis=1)


def join_kernel(kept, came, out):
    out[...] = added(kept[...], came[...])


def plane_kernel(chunks, out, total):
    total[...] = jnp.sum(chunks[...].astype(jnp.float32), axis=0)
    rows = total.shape[0] - 8
    small = jnp.concatenate(halves(total[pl.ds(rows, 4), :] + total[pl.ds(rows + 4, 4), :]))
    for z in range(Z):
        parts = [total[pl.ds(q * 2 * Z + 2 * z, 2), :] for q in range(rows // (2 * Z))]
        own = jnp.concatenate(parts).astype(jnp.bfloat16)
        out[z] = jnp.concatenate([own, small])


def line_kernel(multiplier, chunks, line, dexpand, out):
    total = jnp.sum(chunks[...].astype(jnp.float32), axis=0)
    each = total.shape[0] - 8
    channels = total.shape[1]
    for q in range(each // 2):
        dexpand[:, pl.ds(q * channels, channels)] = total[2 * q : 2 * q + 2] * multiplier
    small = jnp.concatenate(halves(total[each : each + 4] + total[each + 4 :]))
    for place in range(out.shape[0]):
        out[place, pl.ds(0, each), :] = line[place]
        out[place, pl.ds(each, 8), :] = small


def last_kernel(multiplier, chunks, dreduce, dkernel, dgain, dscale, full):
    each = dreduce.shape[0]
    total = jnp.sum(chunks[:, pl.ds(0, each), :].astype(jnp.float32), axis=0)
    dreduce[...] = total * multiplier
    full[...] = chunks[:, pl.ds(each, 4), :].astype(jnp.float32) + chunks[
        :, pl.ds(each + 4, 4), :
    ].astype(jnp.float32)
    side = dkernel.shape[0]
    for place in range(side * side):
        dkernel[place // side, pl.ds(place % side, 1), :] = full[place // 4, pl.ds(place % 4, 1), :]
    for place, out in ((side * side, dgain), (side * side + 1, dscale)):
        out[...] = full[place // 4, pl.ds(place % 4, 1), :]


VMEM = pl.BlockSpec(memory_space=pltpu.VMEM)
HBM = pl.BlockSpec(memory_space=pltpu.HBM)
SMEM = pl.BlockSpec(memory_space=pltpu.SMEM)
PARAMS = pltpu.CompilerParams(vmem_limit_bytes=24 << 20)


def in_hbm(value):
    return pltpu.with_memory_space_constraint(value, pltpu.HBM)


def shifted(value, axes, by):
    count = lax.axis_size(axes)
    pairs = [(i, i + by) for i in range(count) if 0 <= i + by < count]
    return lax.ppermute(value, axes, pairs)


def borders(field, reach):
    up = shifted(field[-reach:], ROW, 1)
    down = shifted(field[:reach], ROW, -1)
    left, right = (
        jnp.concatenate([part[:, columns] for part in (up, field, down)])
        for columns in (slice(-reach, None), slice(0, reach))
    )
    return up, down, shifted(left, COL, 1), shifted(right, COL, -1)


def exchanged(chunks, axes):
    return lax.all_to_all(chunks, axes, 0, 0, tiled=True)


def shards(features, kernel, gain, w_expand, w_reduce, layer_scale, cotangent):
    height, width, channels = features.shape
    hidden = w_reduce.shape[0]
    side = kernel.shape[0]
    reach = side // 2
    blocks = channels // LANES
    pixels = height * width
    multiplier = 1.0 / math.sqrt(pixels * lax.axis_size(ROW) * lax.axis_size(COL))
    gain_row = gain.reshape(1, channels)
    scale_row = layer_scale.reshape(1, channels)
    core = lax.axis_index("core").reshape(1)
    places = Y * X
    rows = hidden // (Y * CORE * X)
    f32, bf16 = jnp.float32, jnp.bfloat16
    shape = jax.ShapeDtypeStruct
    padded_shape = (blocks, height + side - 1, LEFT + width + 8, LANES)

    sent_e, kept_e, sent_r, kept_r, dpre, xhat, rstd, padded, row_sums = pl.pallas_call(
        forward_kernel,
        name="forward",
        in_specs=[SMEM, HBM] + [VMEM] * 4 + [HBM] * 6,
        out_specs=[VMEM] * 9,
        out_shape=[shape((places, rows, channels), bf16)] * 2
        + [shape((Z, places, rows // Z, channels), bf16)] * 2
        + [
            shape((pixels, hidden), bf16),
            shape((blocks, pixels, LANES), f32),
            shape((pixels, LANES), f32),
            shape(padded_shape, f32),
            shape((24, channels), f32),
        ],
        scratch_shapes=[
            pltpu.VMEM((blocks, pixels, LANES), f32),
            pltpu.VMEM((pixels, channels), bf16),
            pltpu.VMEM((pixels, channels), bf16),
            pltpu.VMEM((channels, pixels), bf16),
            pltpu.VMEM((channels, pixels), bf16),
            pltpu.VMEM(features.shape, bf16),
            pltpu.VMEM(kernel.shape, f32),
            pltpu.VMEM((1, channels), f32),
            pltpu.VMEM((channels, hidden), bf16),
            pltpu.VMEM((hidden, channels), bf16),
            pltpu.VMEM((1, channels), f32),
            pltpu.VMEM(cotangent.shape, bf16),
            pltpu.SemaphoreType.DMA((7,)),
        ],
        compiler_params=PARAMS,
    )(
        core, in_hbm(features), *borders(features, reach), in_hbm(kernel), in_hbm(gain_row),
        in_hbm(w_expand), in_hbm(w_reduce), in_hbm(scale_row), in_hbm(cotangent),
    )

    swap = [(0, 1), (1, 0)]
    came_e = lax.ppermute(sent_e, "core", swap)
    came_r = lax.ppermute(sent_r, "core", swap)
    dconv, small = pl.pallas_call(
        functools.partial(backward_kernel, multiplier),
        name="backward",
        in_specs=[VMEM] * 6,
        out_specs=[VMEM] * 2,
        out_shape=[
            shape((height, width, channels), bf16),
            shape((SMALL, channels), f32),
        ],
        scratch_shapes=[pltpu.VMEM((blocks, pixels, LANES), f32)],
        compiler_params=PARAMS,
    )(dpre, w_expand, xhat, rstd, padded, row_sums)

    small_came = lax.ppermute(small, "core", swap)
    each = SMALL // places
    whole = rows + 2 * each
    chip = pl.pallas_call(
        merge_kernel,
        name="merge",
        grid=(Y,),
        in_specs=[pl.BlockSpec((X, rows, channels), lambda i: (i, 0, 0))] * 2
        + [pl.BlockSpec((X, each, channels), lambda i: (i, 0, 0))] * 2,
        out_specs=pl.BlockSpec((X, whole, channels), lambda i: (i, 0, 0)),
        out_shape=shape((places, whole, channels), bf16),
        compiler_params=PARAMS,
    )(
        kept_e, came_e, small.reshape(places, each, channels),
        small_came.reshape(places, each, channels),
    )
    chip, dconv, kept_r = lax.optimization_barrier((chip, dconv, kept_r))
    block = pl.BlockSpec((2, places, rows // Z, channels), lambda i: (i, 0, 0, 0))
    joined = pl.pallas_call(
        join_kernel,
        name="join",
        grid=(Z // 2,),
        in_specs=[block] * 2,
        out_specs=block,
        out_shape=shape(kept_r.shape, bf16),
        compiler_params=PARAMS,
    )(kept_r, came_r)
    line = lax.psum_scatter(
        joined.reshape(Z * rows * places // Z, channels), "z", scatter_dimension=0, tiled=True
    ).reshape(places, rows // Z, channels)
    chunks, edges = lax.optimization_barrier((exchanged(chip, ("y", "x")), borders(dconv, reach)))
    chunks = pl.pallas_call(
        plane_kernel,
        name="plane",
        in_specs=[VMEM],
        out_specs=VMEM,
        out_shape=shape((Z, rows // Z + 2 * each, channels), bf16),
        scratch_shapes=[pltpu.VMEM((whole, channels), f32)],
        compiler_params=PARAMS,
    )(chunks)
    dexpand, chunks = pl.pallas_call(
        functools.partial(line_kernel, multiplier),
        name="line",
        in_specs=[VMEM] * 2,
        out_specs=[VMEM] * 2,
        out_shape=[
            shape((channels * rows // Z // hidden, hidden), f32),
            shape((places, rows // Z + 2 * each, channels), bf16),
        ],
        compiler_params=PARAMS,
    )(exchanged(chunks, "z"), line)
    dreduce, dkernel, dgain, dscale = pl.pallas_call(
        functools.partial(last_kernel, multiplier),
        name="last",
        in_specs=[VMEM],
        out_specs=[VMEM] * 4,
        out_shape=[shape((rows // Z, channels), f32), shape((side, side, channels), f32)]
        + [shape((1, channels), f32)] * 2,
        scratch_shapes=[pltpu.VMEM((places, each, channels), f32)],
        compiler_params=PARAMS,
    )(exchanged(chunks, ("y", "x")))
    grad_features = pl.pallas_call(
        feature_kernel,
        name="features",
        in_specs=[VMEM] * 7,
        out_specs=VMEM,
        out_shape=shape((height, width, channels), bf16),
        scratch_shapes=[pltpu.VMEM(padded_shape, f32)],
        compiler_params=PARAMS,
    )(dconv, *edges, kernel, cotangent)
    return (
        grad_features,
        dkernel,
        dgain.reshape(channels),
        dscale.reshape(channels),
        dexpand,
        dreduce,
    )


def solution(mesh):
    pixels = P(ROW, COL, None)
    return jax.shard_map(
        shards,
        mesh=Mesh(mesh.devices.reshape(Y, CORE, X, Z), (*ROW, *COL)),
        in_specs=(pixels, P(), P(), P(), P(), P(), pixels),
        out_specs=(pixels, P(), P(), P(), P((*ROW, *COL), None), P((*ROW, *COL), None)),
        check_vma=False,
    )
```

```python
import functools
import math

import jax
import jax.numpy as jnp
from jax import lax
from jax.experimental import pallas as pl
from jax.experimental.pallas import tpu as pltpu
from jax.sharding import Mesh
from jax.sharding import PartitionSpec as P

Y, CORE, X, Z = 4, 2, 4, 8
ROW, COL = ("y", "core"), ("x", "z")
INV_ROOT_TWO = 1.0 / math.sqrt(2.0)
INV_ROOT_TWO_PI = 1.0 / math.sqrt(2.0 * math.pi)
LANES = 128
LEFT = 8
SMALL = 4

NN = (((1,), (0,)), ((), ()))
NT = (((1,), (1,)), ((), ()))
TN = (((0,), (0,)), ((), ()))


def product(left, right, dims):
    return lax.dot_general(left, right, dims, preferred_element_type=jnp.float32)


def fill(padded, field, up, down, left, right, reach):
    height, width, channels = field.shape
    for block in range(channels // LANES):
        lanes = pl.ds(block * LANES, LANES)
        own = pl.ds(LEFT, width)
        padded[block, pl.ds(0, reach), own, :] = up[:, :, lanes].astype(jnp.float32)
        padded[block, pl.ds(reach, height), own, :] = field[:, :, lanes].astype(jnp.float32)
        padded[block, pl.ds(reach + height, reach), own, :] = down[:, :, lanes].astype(jnp.float32)
        padded[block, :, pl.ds(LEFT - reach, reach), :] = left[:, :, lanes].astype(jnp.float32)
        padded[block, :, pl.ds(LEFT + width, reach), :] = right[:, :, lanes].astype(jnp.float32)


def depthwise(padded, taps, block, first_col, height, side, flip):
    reach = side // 2
    totals = [None] * height
    lanes = pl.ds(pl.multiple_of(block * LANES, LANES), LANES)
    for second in range(side):
        columns = pl.ds(LEFT - reach + first_col + second, 8)
        rows = [padded[block, row, columns, :] for row in range(height + side - 1)]
        for first in range(side):
            if flip:
                weight = taps[side - 1 - first, pl.ds(side - 1 - second, 1), lanes]
            else:
                weight = taps[first, pl.ds(second, 1), lanes]
            for row in range(height):
                term = weight * rows[row + first]
                totals[row] = term if totals[row] is None else totals[row] + term
    return totals


def forward_kernel(
    core_ref, field_h, up, down, left, right, taps_h, gain_h, expand_h, reduce_h, scale_h,
    cotangent_h,
    sent, kept, sent_z, kept_z, dpre_out, xhat_out, rstd_out, padded, rows_out,
    conv, normed, dbranch, turned, chosen, field, taps, gain, expand, reduce, scale, cotangent,
    sems,
):
    core = core_ref[0]
    copies = [
        pltpu.make_async_copy(source, target, sems.at[i])
        for i, (source, target) in enumerate(
            (
                (field_h, field),
                (taps_h, taps),
                (gain_h, gain),
                (scale_h, scale),
                (cotangent_h, cotangent),
                (expand_h, expand),
                (reduce_h, reduce),
            )
        )
    ]
    for copy in copies:
        copy.start()
    for copy in copies[:2]:
        copy.wait()
    height, width, channels = field.shape
    blocks = channels // LANES
    side = 7
    fill(padded, field, up, down, left, right, side // 2)

    def conv_block(block, _):
        for first_col in range(0, width, 8):
            for row, total in enumerate(
                depthwise(padded, taps, block, first_col, height, side, False)
            ):
                conv[block, pl.ds(row * width + first_col, 8), :] = total
        return 0

    lax.fori_loop(0, blocks, conv_block, 0)
    for copy in copies[2:5]:
        copy.wait()
    for row in range(height):
        pixels = pl.ds(row * width, width)
        values = [conv[block, pixels, :] for block in range(blocks)]
        mean = jnp.sum(sum(values), axis=-1, keepdims=True) / channels
        values = [value - mean for value in values]
        spread = jnp.sum(sum(value * value for value in values), axis=-1, keepdims=True) / channels
        rstd = lax.rsqrt(spread + 1e-06)
        rstd_out[pixels, :] = jnp.broadcast_to(rstd, (width, LANES))
        for block, value in enumerate(values):
            lanes = pl.ds(block * LANES, LANES)
            xhat = value * rstd
            xhat_out[block, pixels, :] = xhat
            normed[pixels, lanes] = (xhat * gain[:, lanes]).astype(jnp.bfloat16)
        dbranch[pixels, :] = (cotangent[row].astype(jnp.float32) * scale[...]).astype(jnp.bfloat16)
    turned[...] = normed[...].T
    part = channels // (Y * CORE)
    for y in range(Y):
        for own in range(CORE):
            owner = core if own else 1 - core
            chosen[pl.ds((own * Y + y) * part, part), :] = turned[
                pl.ds(pl.multiple_of((y * CORE + owner) * part, part), part), :
            ]
    rows_out[pl.ds(0, 8), :] = jnp.zeros((8, channels), jnp.float32)
    rows_out[pl.ds(8, 8), :] = jnp.broadcast_to(gain[...], (8, channels))
    rows_out[pl.ds(16, 8), :] = jnp.broadcast_to(scale[...], (8, channels))
    for copy in copies[5:]:
        copy.wait()
    step = reduce.shape[0] // (Y * CORE)
    per_z = step // (X * Z)
    part_x = part // X
    wide = channels // step
    narrow = channels // 2
    top = per_z * Z // 2

    def hidden_block(y, _):
        for own, target, target_z in ((0, sent, sent_z), (1, kept, kept_z)):
            owner = core if own else 1 - core
            chunk = y * CORE + owner
            hidden = pl.ds(pl.multiple_of(chunk * step, step), step)
            pre = product(normed[...], expand[:, hidden], NN)
            dact = product(dbranch[...], reduce[hidden, :], NT)
            half = 0.5 * (1.0 + lax.erf(pre * INV_ROOT_TWO))
            slope = half + pre * jnp.exp(-0.5 * pre * pre) * INV_ROOT_TWO_PI
            act = (pre * half).astype(jnp.bfloat16)
            dpre = (dact * slope).astype(jnp.bfloat16)
            dpre_out[:, hidden] = dpre
            share = product(act, dbranch[...], TN)
            weighed = share * reduce[hidden, :].astype(jnp.float32)
            rows_out[pl.ds(0, 8), :] += jnp.sum(weighed.reshape(step // 8, 8, channels), axis=0)
            share = share.astype(jnp.bfloat16)
            for place in range(X * Z):
                x, z = place // Z, place % Z
                mine = share[place * per_z : (place + 1) * per_z]
                target[
                    y * X + x, pl.ds(z // 2 * per_z, per_z), pl.ds(z % 2 * narrow, narrow)
                ] = mine[:, :narrow]
                target_z[
                    z, y * (X // 2) + x // 2, :, pl.ds(x % 2 * narrow, narrow)
                ] = mine[:, narrow:]
            share = product(chosen[...], dpre, NN).astype(jnp.bfloat16)
            rows = pl.ds(pl.multiple_of(top + (chunk // wide) * part_x, part_x), part_x)
            lanes = pl.ds(pl.multiple_of((chunk % wide) * step, step), step)
            for place in range(Y * X):
                for back, goal in ((0, sent), (1, kept)):
                    first = back * Y * part + place * part_x
                    goal[place, rows, lanes] = share[first : first + part_x]
        return 0

    lax.fori_loop(0, Y, hidden_block, 0)


def backward_kernel(
    multiplier, dpre, expand, xhat, rstd, padded, rows, dconv_out, out, dconv, small
):
    height, width, channels = dconv_out.shape
    blocks = channels // LANES
    side = 7
    dnormed = product(dpre[...], expand[...], NT)
    for block in range(blocks):
        dconv[block] = dnormed[:, block * LANES : (block + 1) * LANES]
    sums = [jnp.zeros((width, LANES), jnp.float32)] * blocks
    for row in range(height):
        pixels = pl.ds(row * width, width)
        grads = [dconv[block, pixels, :] for block in range(blocks)]
        hats = [xhat[block, pixels, :] for block in range(blocks)]
        sums = [total + grad * hat for total, grad, hat in zip(sums, grads, hats)]
        grads = [grad * rows[pl.ds(8, 1), pl.ds(block * LANES, LANES)] for block, grad in enumerate(grads)]
        mean = jnp.sum(sum(grads), axis=-1, keepdims=True) / channels
        slant = sum(grad * hat for grad, hat in zip(grads, hats))
        slant = jnp.sum(slant, axis=-1, keepdims=True) / channels
        for block in range(blocks):
            value = rstd[pixels, :] * (grads[block] - mean - hats[block] * slant)
            dconv[block, pixels, :] = value
            dconv_out[row, :, pl.ds(block * LANES, LANES)] = value.astype(jnp.bfloat16)
    taps = side * side
    unused = small.shape[0] - taps - 2
    small[pl.ds(taps + 2, unused), :] = jnp.zeros((unused, channels), jnp.float32)
    for block in range(blocks):
        lanes = pl.ds(block * LANES, LANES)
        total = jnp.sum(sums[block], axis=0, keepdims=True)
        small[pl.ds(taps, 1), lanes] = total * multiplier
        total = jnp.sum(rows[pl.ds(0, 8), lanes], axis=0, keepdims=True)
        small[pl.ds(taps + 1, 1), lanes] = total / rows[pl.ds(16, 1), lanes] * multiplier

    def tap_block(block, _):
        lanes = pl.ds(pl.multiple_of(block * LANES, LANES), LANES)
        for second in range(side):
            totals = [jnp.zeros((8, LANES), jnp.float32)] * side
            for first_col in range(0, width, 8):
                grads = [
                    dconv[block, pl.ds(row * width + first_col, 8), :] for row in range(height)
                ]
                columns = pl.ds(LEFT - side // 2 + first_col + second, 8)
                for row in range(height + side - 1):
                    value = padded[block, row, columns, :]
                    for first in range(max(0, row - height + 1), min(side, row + 1)):
                        totals[first] = totals[first] + grads[row - first] * value
            for first, total in enumerate(totals):
                total = jnp.sum(total, axis=0, keepdims=True) * multiplier
                small[pl.ds(first * side + second, 1), lanes] = total
        return 0

    lax.fori_loop(0, blocks, tap_block, 0)
    for place in range(out.shape[0]):
        part = small[pl.ds(place * SMALL, SMALL), :]
        out[place] = jnp.concatenate([part, jnp.zeros_like(part)]).astype(jnp.bfloat16)


def feature_kernel(field, up, down, left, right, taps, cotangent, out, padded):
    height, width, channels = field.shape
    side = 7
    fill(padded, field, up, down, left, right, side // 2)
    for block in range(channels // LANES):
        lanes = pl.ds(block * LANES, LANES)
        for first_col in range(0, width, 8):
            columns = pl.ds(first_col, 8)
            for row, total in enumerate(
                depthwise(padded, taps, block, first_col, height, side, True)
            ):
                total = total + cotangent[row, columns, lanes].astype(jnp.float32)
                out[row, columns, lanes] = total.astype(jnp.bfloat16)


def added(left, right):
    return (left.astype(jnp.float32) + right.astype(jnp.float32)).astype(jnp.bfloat16)


def merge_kernel(kept, came, small, small_came, out):
    rows = kept.shape[1]
    out[:, pl.ds(0, rows), :] = added(kept[...], came[...])
    out[:, pl.ds(rows, small.shape[1]), :] = added(small[...], small_came[...])


def join_kernel(z_ref, kept, came, *outs):
    for step, out in enumerate(outs):
        z = lax.rem(z_ref[0] + step, Z)
        out[...] = added(kept[z], came[z])


def plane_kernel(chunks, out, total):
    total[...] = jnp.sum(chunks[...].astype(jnp.float32), axis=0)
    each = out.shape[1] // 2
    channels = out.shape[2]
    narrow = channels // 2
    top = each * Z // 2
    small = total[pl.ds(total.shape[0] - 2 * SMALL, SMALL), :].astype(jnp.bfloat16)
    small = jnp.concatenate([small[:, :narrow], small[:, narrow:]])
    for z in range(Z):
        parts = [total[pl.ds(top + q * 2 * Z + 2 * z, 2), :] for q in range(each // 2)]
        out[z, pl.ds(0, each), :] = jnp.concatenate(parts).astype(jnp.bfloat16)
        half = total[pl.ds(z // 2 * each, each), pl.ds(z % 2 * narrow, narrow)]
        out[z, pl.ds(each, each), pl.ds(0, narrow)] = half.astype(jnp.bfloat16)
        out[z, pl.ds(each, each), pl.ds(narrow, narrow)] = small


def line_kernel(multiplier, chunks, *refs):
    *came, dexpand, dreduce, out = refs
    total = jnp.sum(chunks[...].astype(jnp.float32), axis=0)
    each = total.shape[0] // 2
    channels = total.shape[1]
    narrow = channels // 2
    for q in range(each // 2):
        dexpand[:, pl.ds(q * channels, channels)] = total[2 * q : 2 * q + 2] * multiplier
    dreduce[...] = total[each:, :narrow] * multiplier
    small = total[each:, narrow:].astype(jnp.bfloat16)
    line = sum(ref[...].astype(jnp.float32) for ref in came).astype(jnp.bfloat16)
    for place in range(out.shape[0]):
        out[place, :, pl.ds(0, narrow)] = line[place // 2][
            :, place % 2 * narrow : (place % 2 + 1) * narrow
        ]
        out[place, :, pl.ds(narrow, narrow)] = small


def last_kernel(multiplier, chunks, half, dreduce, dkernel, dgain, dscale):
    channels = dreduce.shape[1]
    narrow = channels // 2
    dreduce[:, pl.ds(0, narrow)] = half[...]
    total = jnp.sum(chunks[:, :, pl.ds(0, narrow)].astype(jnp.float32), axis=0)
    dreduce[:, pl.ds(narrow, narrow)] = total * multiplier
    side = dkernel.shape[0]
    for place in range(chunks.shape[0]):
        part = chunks[place, :, pl.ds(narrow, narrow)].astype(jnp.float32)
        for row in range(SMALL):
            tap = place * SMALL + row
            for i in range(2):
                lanes = pl.ds(i * narrow, narrow)
                value = part[i * SMALL + row : i * SMALL + row + 1]
                if tap < side * side:
                    dkernel[tap // side, pl.ds(tap % side, 1), lanes] = value
                elif tap == side * side:
                    dgain[:, lanes] = value
                elif tap == side * side + 1:
                    dscale[:, lanes] = value


VMEM = pl.BlockSpec(memory_space=pltpu.VMEM)
HBM = pl.BlockSpec(memory_space=pltpu.HBM)
SMEM = pl.BlockSpec(memory_space=pltpu.SMEM)
PARAMS = pltpu.CompilerParams(vmem_limit_bytes=24 << 20)


def in_hbm(value):
    return pltpu.with_memory_space_constraint(value, pltpu.HBM)


def shifted(value, axes, by):
    count = lax.axis_size(axes)
    pairs = [(i, i + by) for i in range(count) if 0 <= i + by < count]
    return lax.ppermute(value, axes, pairs)


def borders(field, reach):
    up = shifted(field[-reach:], ROW, 1)
    down = shifted(field[:reach], ROW, -1)
    left, right = (
        jnp.concatenate([part[:, columns] for part in (up, field, down)])
        for columns in (slice(-reach, None), slice(0, reach))
    )
    return up, down, shifted(left, COL, 1), shifted(right, COL, -1)


def exchanged(chunks, axes):
    return lax.all_to_all(chunks, axes, 0, 0, tiled=True)


def shards(features, kernel, gain, w_expand, w_reduce, layer_scale, cotangent):
    height, width, channels = features.shape
    hidden = w_reduce.shape[0]
    side = kernel.shape[0]
    reach = side // 2
    blocks = channels // LANES
    pixels = height * width
    multiplier = 1.0 / math.sqrt(pixels * lax.axis_size(ROW) * lax.axis_size(COL))
    gain_row = gain.reshape(1, channels)
    scale_row = layer_scale.reshape(1, channels)
    core = lax.axis_index("core").reshape(1)
    places = Y * X
    rows = hidden // (Y * CORE * X)
    f32, bf16 = jnp.float32, jnp.bfloat16
    shape = jax.ShapeDtypeStruct
    padded_shape = (blocks, height + side - 1, LEFT + width + 8, LANES)

    each = rows // Z
    top = rows // 2
    sent, kept, sent_z, kept_z, dpre, xhat, rstd, padded, row_sums = pl.pallas_call(
        forward_kernel,
        name="forward",
        in_specs=[SMEM, HBM] + [VMEM] * 4 + [HBM] * 6,
        out_specs=[VMEM] * 9,
        out_shape=[shape((places, top + rows, channels), bf16)] * 2
        + [shape((Z, places // 2, each, channels), bf16)] * 2
        + [
            shape((pixels, hidden), bf16),
            shape((blocks, pixels, LANES), f32),
            shape((pixels, LANES), f32),
            shape(padded_shape, f32),
            shape((24, channels), f32),
        ],
        scratch_shapes=[
            pltpu.VMEM((blocks, pixels, LANES), f32),
            pltpu.VMEM((pixels, channels), bf16),
            pltpu.VMEM((pixels, channels), bf16),
            pltpu.VMEM((channels, pixels), bf16),
            pltpu.VMEM((channels, pixels), bf16),
            pltpu.VMEM(features.shape, bf16),
            pltpu.VMEM(kernel.shape, f32),
            pltpu.VMEM((1, channels), f32),
            pltpu.VMEM((channels, hidden), bf16),
            pltpu.VMEM((hidden, channels), bf16),
            pltpu.VMEM((1, channels), f32),
            pltpu.VMEM(cotangent.shape, bf16),
            pltpu.SemaphoreType.DMA((7,)),
        ],
        compiler_params=PARAMS,
    )(
        core, in_hbm(features), *borders(features, reach), in_hbm(kernel), in_hbm(gain_row),
        in_hbm(w_expand), in_hbm(w_reduce), in_hbm(scale_row), in_hbm(cotangent),
    )

    swap = [(0, 1), (1, 0)]
    came = lax.ppermute(sent, "core", swap)
    came_z = lax.ppermute(sent_z, "core", swap)
    dconv, small = pl.pallas_call(
        functools.partial(backward_kernel, multiplier),
        name="backward",
        in_specs=[VMEM] * 6,
        out_specs=[VMEM] * 2,
        out_shape=[
            shape((height, width, channels), bf16),
            shape((places, 2 * SMALL, channels), bf16),
        ],
        scratch_shapes=[
            pltpu.VMEM((blocks, pixels, LANES), f32),
            pltpu.VMEM((places * SMALL, channels), f32),
        ],
        compiler_params=PARAMS,
    )(dpre, w_expand, xhat, rstd, padded, row_sums)

    small_came = lax.ppermute(small, "core", swap)
    whole = top + rows + 2 * SMALL
    chip = pl.pallas_call(
        merge_kernel,
        name="merge",
        grid=(Y,),
        in_specs=[pl.BlockSpec((X, top + rows, channels), lambda i: (i, 0, 0))] * 2
        + [pl.BlockSpec((X, 2 * SMALL, channels), lambda i: (i, 0, 0))] * 2,
        out_specs=pl.BlockSpec((X, whole, channels), lambda i: (i, 0, 0)),
        out_shape=shape((places, whole, channels), bf16),
        compiler_params=PARAMS,
    )(kept, came, small, small_came)
    chip, dconv, came_z = lax.optimization_barrier((chip, dconv, came_z))
    line = pl.pallas_call(
        join_kernel,
        name="join",
        in_specs=[SMEM] + [VMEM] * 2,
        out_specs=[VMEM] * Z,
        out_shape=[shape(kept_z.shape[1:], bf16)] * Z,
        compiler_params=PARAMS,
    )(lax.axis_index("z").reshape(1), kept_z, came_z)
    line = [
        part if step == 0 else lax.ppermute(part, "z", [(i, (i + step) % Z) for i in range(Z)])
        for step, part in enumerate(line)
    ]
    chunks, edges, line = lax.optimization_barrier(
        (exchanged(chip, ("y", "x")), borders(dconv, reach), line)
    )
    chunks = pl.pallas_call(
        plane_kernel,
        name="plane",
        in_specs=[VMEM],
        out_specs=VMEM,
        out_shape=shape((Z, 2 * each, channels), bf16),
        scratch_shapes=[pltpu.VMEM((whole, channels), f32)],
        compiler_params=PARAMS,
    )(chunks)
    dexpand, half, chunks = pl.pallas_call(
        functools.partial(line_kernel, multiplier),
        name="line",
        in_specs=[VMEM] * (1 + Z),
        out_specs=[VMEM] * 3,
        out_shape=[
            shape((channels * each // hidden, hidden), f32),
            shape((each, channels // 2), f32),
            shape((places, each, channels), bf16),
        ],
        compiler_params=PARAMS,
    )(exchanged(chunks, "z"), *line)
    dreduce, dkernel, dgain, dscale = pl.pallas_call(
        functools.partial(last_kernel, multiplier),
        name="last",
        in_specs=[VMEM] * 2,
        out_specs=[VMEM] * 4,
        out_shape=[shape((each, channels), f32), shape((side, side, channels), f32)]
        + [shape((1, channels), f32)] * 2,
        compiler_params=PARAMS,
    )(exchanged(chunks, ("y", "x")), half)
    grad_features = pl.pallas_call(
        feature_kernel,
        name="features",
        in_specs=[VMEM] * 7,
        out_specs=VMEM,
        out_shape=shape((height, width, channels), bf16),
        scratch_shapes=[pltpu.VMEM(padded_shape, f32)],
        compiler_params=PARAMS,
    )(dconv, *edges, kernel, cotangent)
    return (
        grad_features,
        dkernel,
        dgain.reshape(channels),
        dscale.reshape(channels),
        dexpand,
        dreduce,
    )


def solution(mesh):
    pixels = P(ROW, COL, None)
    return jax.shard_map(
        shards,
        mesh=Mesh(mesh.devices.reshape(Y, CORE, X, Z), (*ROW, *COL)),
        in_specs=(pixels, P(), P(), P(), P(), P(), pixels),
        out_specs=(pixels, P(), P(), P(), P((*ROW, *COL), None), P((*ROW, *COL), None)),
        check_vma=False,
    )
```

```python
import functools
import math

import jax
import jax.numpy as jnp
from jax import lax
from jax.experimental import pallas as pl
from jax.experimental.pallas import tpu as pltpu
from jax.sharding import Mesh
from jax.sharding import PartitionSpec as P

Y, CORE, X, Z = 4, 2, 4, 8
ROW, COL = ("y", "core"), ("x", "z")
INV_ROOT_TWO = 1.0 / math.sqrt(2.0)
INV_ROOT_TWO_PI = 1.0 / math.sqrt(2.0 * math.pi)
LANES = 128
LEFT = 8
SMALL = 4

NN = (((1,), (0,)), ((), ()))
NT = (((1,), (1,)), ((), ()))
TN = (((0,), (0,)), ((), ()))


def product(left, right, dims):
    return lax.dot_general(left, right, dims, preferred_element_type=jnp.float32)


def fill(padded, field, up, down, left, right, reach):
    height, width, channels = field.shape
    for block in range(channels // LANES):
        lanes = pl.ds(block * LANES, LANES)
        own = pl.ds(LEFT, width)
        padded[block, pl.ds(0, reach), own, :] = up[:, :, lanes].astype(jnp.float32)
        padded[block, pl.ds(reach, height), own, :] = field[:, :, lanes].astype(jnp.float32)
        padded[block, pl.ds(reach + height, reach), own, :] = down[:, :, lanes].astype(jnp.float32)
        padded[block, :, pl.ds(LEFT - reach, reach), :] = left[:, :, lanes].astype(jnp.float32)
        padded[block, :, pl.ds(LEFT + width, reach), :] = right[:, :, lanes].astype(jnp.float32)


def depthwise(padded, taps, block, first_col, height, side, flip):
    reach = side // 2
    totals = [None] * height
    lanes = pl.ds(pl.multiple_of(block * LANES, LANES), LANES)
    for second in range(side):
        columns = pl.ds(LEFT - reach + first_col + second, 8)
        rows = [padded[block, row, columns, :] for row in range(height + side - 1)]
        for first in range(side):
            if flip:
                weight = taps[side - 1 - first, pl.ds(side - 1 - second, 1), lanes]
            else:
                weight = taps[first, pl.ds(second, 1), lanes]
            for row in range(height):
                term = weight * rows[row + first]
                totals[row] = term if totals[row] is None else totals[row] + term
    return totals


def forward_kernel(
    core_ref, field_h, up, down, left, right, taps_h, gain_h, expand_h, reduce_h, scale_h,
    cotangent_h,
    sent, kept, sent_z, kept_z, dpre_out, xhat_out, rstd_out, padded, rows_out,
    conv, normed, dbranch, turned, chosen, field, taps, gain, expand, reduce, scale, cotangent,
    sems,
):
    core = core_ref[0]
    copies = [
        pltpu.make_async_copy(source, target, sems.at[i])
        for i, (source, target) in enumerate(
            (
                (field_h, field),
                (taps_h, taps),
                (gain_h, gain),
                (scale_h, scale),
                (cotangent_h, cotangent),
                (expand_h, expand),
                (reduce_h, reduce),
            )
        )
    ]
    for copy in copies:
        copy.start()
    for copy in copies[:2]:
        copy.wait()
    height, width, channels = field.shape
    blocks = channels // LANES
    side = 7
    fill(padded, field, up, down, left, right, side // 2)

    def conv_block(block, _):
        for first_col in range(0, width, 8):
            for row, total in enumerate(
                depthwise(padded, taps, block, first_col, height, side, False)
            ):
                conv[block, pl.ds(row * width + first_col, 8), :] = total
        return 0

    lax.fori_loop(0, blocks, conv_block, 0)
    for copy in copies[2:5]:
        copy.wait()
    for row in range(height):
        pixels = pl.ds(row * width, width)
        values = [conv[block, pixels, :] for block in range(blocks)]
        mean = jnp.sum(sum(values), axis=-1, keepdims=True) / channels
        values = [value - mean for value in values]
        spread = jnp.sum(sum(value * value for value in values), axis=-1, keepdims=True) / channels
        rstd = lax.rsqrt(spread + 1e-06)
        rstd_out[pixels, :] = jnp.broadcast_to(rstd, (width, LANES))
        for block, value in enumerate(values):
            lanes = pl.ds(block * LANES, LANES)
            xhat = value * rstd
            xhat_out[block, pixels, :] = xhat
            normed[pixels, lanes] = (xhat * gain[:, lanes]).astype(jnp.bfloat16)
        dbranch[pixels, :] = (cotangent[row].astype(jnp.float32) * scale[...]).astype(jnp.bfloat16)
    turned[...] = normed[...].T
    part = channels // (Y * CORE)
    for y in range(Y):
        for own in range(CORE):
            owner = core if own else 1 - core
            chosen[pl.ds((own * Y + y) * part, part), :] = turned[
                pl.ds(pl.multiple_of((y * CORE + owner) * part, part), part), :
            ]
    rows_out[pl.ds(0, 8), :] = jnp.zeros((8, channels), jnp.float32)
    rows_out[pl.ds(8, 8), :] = jnp.broadcast_to(gain[...], (8, channels))
    rows_out[pl.ds(16, 8), :] = jnp.broadcast_to(scale[...], (8, channels))
    for copy in copies[5:]:
        copy.wait()
    step = reduce.shape[0] // (Y * CORE)
    per_z = step // (X * Z)
    part_x = part // X
    wide = channels // step
    narrow = channels // 2
    top = per_z * Z // 2

    def hidden_block(y, _):
        for own, target, target_z in ((0, sent, sent_z), (1, kept, kept_z)):
            owner = core if own else 1 - core
            chunk = y * CORE + owner
            hidden = pl.ds(pl.multiple_of(chunk * step, step), step)
            pre = product(normed[...], expand[:, hidden], NN)
            dact = product(dbranch[...], reduce[hidden, :], NT)
            half = 0.5 * (1.0 + lax.erf(pre * INV_ROOT_TWO))
            slope = half + pre * jnp.exp(-0.5 * pre * pre) * INV_ROOT_TWO_PI
            act = (pre * half).astype(jnp.bfloat16)
            dpre = (dact * slope).astype(jnp.bfloat16)
            dpre_out[:, hidden] = dpre
            share = product(act, dbranch[...], TN)
            weighed = share * reduce[hidden, :].astype(jnp.float32)
            rows_out[pl.ds(0, 8), :] += jnp.sum(weighed.reshape(step // 8, 8, channels), axis=0)
            share = share.astype(jnp.bfloat16)
            for place in range(X * Z):
                x, z = place // Z, place % Z
                mine = share[place * per_z : (place + 1) * per_z]
                target[
                    y * X + x, pl.ds(z // 2 * per_z, per_z), pl.ds(z % 2 * narrow, narrow)
                ] = mine[:, :narrow]
                target_z[
                    z, y * (X // 2) + x // 2, :, pl.ds(x % 2 * narrow, narrow)
                ] = mine[:, narrow:]
            share = product(chosen[...], dpre, NN).astype(jnp.bfloat16)
            rows = pl.ds(pl.multiple_of(top + (chunk // wide) * part_x, part_x), part_x)
            lanes = pl.ds(pl.multiple_of((chunk % wide) * step, step), step)
            for place in range(Y * X):
                for back, goal in ((0, sent), (1, kept)):
                    first = back * Y * part + place * part_x
                    goal[place, rows, lanes] = share[first : first + part_x]
        return 0

    lax.fori_loop(0, Y, hidden_block, 0)


def backward_kernel(
    multiplier, dpre, expand, xhat, rstd, padded, rows, dconv_out, out, dconv, small
):
    height, width, channels = dconv_out.shape
    blocks = channels // LANES
    side = 7
    dnormed = product(dpre[...], expand[...], NT)
    for block in range(blocks):
        dconv[block] = dnormed[:, block * LANES : (block + 1) * LANES]
    sums = [jnp.zeros((width, LANES), jnp.float32)] * blocks
    for row in range(height):
        pixels = pl.ds(row * width, width)
        grads = [dconv[block, pixels, :] for block in range(blocks)]
        hats = [xhat[block, pixels, :] for block in range(blocks)]
        sums = [total + grad * hat for total, grad, hat in zip(sums, grads, hats)]
        grads = [grad * rows[pl.ds(8, 1), pl.ds(block * LANES, LANES)] for block, grad in enumerate(grads)]
        mean = jnp.sum(sum(grads), axis=-1, keepdims=True) / channels
        slant = sum(grad * hat for grad, hat in zip(grads, hats))
        slant = jnp.sum(slant, axis=-1, keepdims=True) / channels
        for block in range(blocks):
            value = rstd[pixels, :] * (grads[block] - mean - hats[block] * slant)
            dconv[block, pixels, :] = value
            dconv_out[row, :, pl.ds(block * LANES, LANES)] = value.astype(jnp.bfloat16)
    taps = side * side
    unused = small.shape[0] - taps - 2
    small[pl.ds(taps + 2, unused), :] = jnp.zeros((unused, channels), jnp.float32)
    for block in range(blocks):
        lanes = pl.ds(block * LANES, LANES)
        total = jnp.sum(sums[block], axis=0, keepdims=True)
        small[pl.ds(taps, 1), lanes] = total * multiplier
        total = jnp.sum(rows[pl.ds(0, 8), lanes], axis=0, keepdims=True)
        small[pl.ds(taps + 1, 1), lanes] = total / rows[pl.ds(16, 1), lanes] * multiplier

    def tap_block(block, _):
        lanes = pl.ds(pl.multiple_of(block * LANES, LANES), LANES)
        for second in range(side):
            totals = [jnp.zeros((8, LANES), jnp.float32)] * side
            for first_col in range(0, width, 8):
                grads = [
                    dconv[block, pl.ds(row * width + first_col, 8), :] for row in range(height)
                ]
                columns = pl.ds(LEFT - side // 2 + first_col + second, 8)
                for row in range(height + side - 1):
                    value = padded[block, row, columns, :]
                    for first in range(max(0, row - height + 1), min(side, row + 1)):
                        totals[first] = totals[first] + grads[row - first] * value
            for first, total in enumerate(totals):
                total = jnp.sum(total, axis=0, keepdims=True) * multiplier
                small[pl.ds(first * side + second, 1), lanes] = total
        return 0

    lax.fori_loop(0, blocks, tap_block, 0)
    for place in range(out.shape[0]):
        part = small[pl.ds(place * SMALL, SMALL), :]
        out[place] = jnp.concatenate([part, jnp.zeros_like(part)]).astype(jnp.bfloat16)


def feature_kernel(field, up, down, left, right, taps, cotangent, out, padded):
    height, width, channels = field.shape
    side = 7
    fill(padded, field, up, down, left, right, side // 2)
    for block in range(channels // LANES):
        lanes = pl.ds(block * LANES, LANES)
        for first_col in range(0, width, 8):
            columns = pl.ds(first_col, 8)
            for row, total in enumerate(
                depthwise(padded, taps, block, first_col, height, side, True)
            ):
                total = total + cotangent[row, columns, lanes].astype(jnp.float32)
                out[row, columns, lanes] = total.astype(jnp.bfloat16)


def added(left, right):
    return (left.astype(jnp.float32) + right.astype(jnp.float32)).astype(jnp.bfloat16)


def merge_kernel(kept, came, small, small_came, out):
    rows = kept.shape[1]
    out[:, pl.ds(0, rows), :] = added(kept[...], came[...])
    out[:, pl.ds(rows, small.shape[1]), :] = added(small[...], small_came[...])


def join_kernel(z_ref, kept, came, *outs):
    for step, out in enumerate(outs):
        z = lax.rem(z_ref[0] + step, Z)
        out[...] = added(kept[z], came[z])


def plane_kernel(chunks, out, total):
    total[...] = jnp.sum(chunks[...].astype(jnp.float32), axis=0)
    each = out.shape[1] // 2
    channels = out.shape[2]
    narrow = channels // 2
    top = each * Z // 2
    small = total[pl.ds(total.shape[0] - 2 * SMALL, SMALL), :].astype(jnp.bfloat16)
    small = jnp.concatenate([small[:, :narrow], small[:, narrow:]])
    for z in range(Z):
        parts = [total[pl.ds(top + q * 2 * Z + 2 * z, 2), :] for q in range(each // 2)]
        out[z, pl.ds(0, each), :] = jnp.concatenate(parts).astype(jnp.bfloat16)
        half = total[pl.ds(z // 2 * each, each), pl.ds(z % 2 * narrow, narrow)]
        out[z, pl.ds(each, each), pl.ds(0, narrow)] = half.astype(jnp.bfloat16)
        out[z, pl.ds(each, each), pl.ds(narrow, narrow)] = small


def line_kernel(multiplier, chunks, *refs):
    *came, dexpand, dreduce, out = refs
    total = jnp.sum(chunks[...].astype(jnp.float32), axis=0)
    each = total.shape[0] // 2
    channels = total.shape[1]
    narrow = channels // 2
    for q in range(each // 2):
        dexpand[:, pl.ds(q * channels, channels)] = total[2 * q : 2 * q + 2] * multiplier
    dreduce[...] = total[each:, :narrow] * multiplier
    small = total[each:, narrow:].astype(jnp.bfloat16)
    line = sum(ref[...].astype(jnp.float32) for ref in came).astype(jnp.bfloat16)
    for place in range(out.shape[0]):
        out[place, :, pl.ds(0, narrow)] = line[place // 2][
            :, place % 2 * narrow : (place % 2 + 1) * narrow
        ]
        out[place, :, pl.ds(narrow, narrow)] = small


def last_kernel(multiplier, chunks, half, dreduce, dkernel, dgain, dscale):
    channels = dreduce.shape[1]
    narrow = channels // 2
    dreduce[:, pl.ds(0, narrow)] = half[...]
    total = jnp.sum(chunks[:, :, pl.ds(0, narrow)].astype(jnp.float32), axis=0)
    dreduce[:, pl.ds(narrow, narrow)] = total * multiplier
    side = dkernel.shape[0]
    for place in range(chunks.shape[0]):
        part = chunks[place, :, pl.ds(narrow, narrow)].astype(jnp.float32)
        for row in range(SMALL):
            tap = place * SMALL + row
            for i in range(2):
                lanes = pl.ds(i * narrow, narrow)
                value = part[i * SMALL + row : i * SMALL + row + 1]
                if tap < side * side:
                    dkernel[tap // side, pl.ds(tap % side, 1), lanes] = value
                elif tap == side * side:
                    dgain[:, lanes] = value
                elif tap == side * side + 1:
                    dscale[:, lanes] = value


VMEM = pl.BlockSpec(memory_space=pltpu.VMEM)
HBM = pl.BlockSpec(memory_space=pltpu.HBM)
SMEM = pl.BlockSpec(memory_space=pltpu.SMEM)
PARAMS = pltpu.CompilerParams(vmem_limit_bytes=20 << 20)
GLUE_PARAMS = pltpu.CompilerParams(vmem_limit_bytes=10 << 20)


def in_hbm(value):
    return pltpu.with_memory_space_constraint(value, pltpu.HBM)


def shifted(value, axes, by):
    count = lax.axis_size(axes)
    pairs = [(i, i + by) for i in range(count) if 0 <= i + by < count]
    return lax.ppermute(value, axes, pairs)


def row_borders(field, reach):
    return shifted(field[-reach:], ROW, 1), shifted(field[:reach], ROW, -1)


def column_borders(field, up, down, reach):
    left, right = (
        jnp.concatenate([part[:, columns] for part in (up, field, down)])
        for columns in (slice(-reach, None), slice(0, reach))
    )
    return up, down, shifted(left, COL, 1), shifted(right, COL, -1)


def exchanged(chunks, axes):
    return lax.all_to_all(chunks, axes, 0, 0, tiled=True)


def shards(features, kernel, gain, w_expand, w_reduce, layer_scale, cotangent):
    height, width, channels = features.shape
    hidden = w_reduce.shape[0]
    side = kernel.shape[0]
    reach = side // 2
    blocks = channels // LANES
    pixels = height * width
    multiplier = 1.0 / math.sqrt(pixels * lax.axis_size(ROW) * lax.axis_size(COL))
    gain_row = gain.reshape(1, channels)
    scale_row = layer_scale.reshape(1, channels)
    core = lax.axis_index("core").reshape(1)
    places = Y * X
    rows = hidden // (Y * CORE * X)
    f32, bf16 = jnp.float32, jnp.bfloat16
    shape = jax.ShapeDtypeStruct
    padded_shape = (blocks, height + side - 1, LEFT + width + 8, LANES)

    each = rows // Z
    top = rows // 2
    sent, kept, sent_z, kept_z, dpre, xhat, rstd, padded, row_sums = pl.pallas_call(
        forward_kernel,
        name="forward",
        in_specs=[SMEM, HBM] + [VMEM] * 4 + [HBM] * 6,
        out_specs=[VMEM] * 9,
        out_shape=[shape((places, top + rows, channels), bf16)] * 2
        + [shape((Z, places // 2, each, channels), bf16)] * 2
        + [
            shape((pixels, hidden), bf16),
            shape((blocks, pixels, LANES), f32),
            shape((pixels, LANES), f32),
            shape(padded_shape, f32),
            shape((24, channels), f32),
        ],
        scratch_shapes=[
            pltpu.VMEM((blocks, pixels, LANES), f32),
            pltpu.VMEM((pixels, channels), bf16),
            pltpu.VMEM((pixels, channels), bf16),
            pltpu.VMEM((channels, pixels), bf16),
            pltpu.VMEM((channels, pixels), bf16),
            pltpu.VMEM(features.shape, bf16),
            pltpu.VMEM(kernel.shape, f32),
            pltpu.VMEM((1, channels), f32),
            pltpu.VMEM((channels, hidden), bf16),
            pltpu.VMEM((hidden, channels), bf16),
            pltpu.VMEM((1, channels), f32),
            pltpu.VMEM(cotangent.shape, bf16),
            pltpu.SemaphoreType.DMA((7,)),
        ],
        compiler_params=PARAMS,
    )(
        core, in_hbm(features),
        *column_borders(features, *row_borders(features, reach), reach), in_hbm(kernel), in_hbm(gain_row),
        in_hbm(w_expand), in_hbm(w_reduce), in_hbm(scale_row), in_hbm(cotangent),
    )

    swap = [(0, 1), (1, 0)]
    came = lax.ppermute(sent, "core", swap)
    came_z = lax.ppermute(sent_z, "core", swap)
    dconv, small = pl.pallas_call(
        functools.partial(backward_kernel, multiplier),
        name="backward",
        in_specs=[VMEM] * 6,
        out_specs=[VMEM] * 2,
        out_shape=[
            shape((height, width, channels), bf16),
            shape((places, 2 * SMALL, channels), bf16),
        ],
        scratch_shapes=[
            pltpu.VMEM((blocks, pixels, LANES), f32),
            pltpu.VMEM((places * SMALL, channels), f32),
        ],
        compiler_params=PARAMS,
    )(dpre, w_expand, xhat, rstd, padded, row_sums)

    small_came = lax.ppermute(small, "core", swap)
    whole = top + rows + 2 * SMALL
    chip = pl.pallas_call(
        merge_kernel,
        name="merge",
        grid=(Y,),
        in_specs=[pl.BlockSpec((X, top + rows, channels), lambda i: (i, 0, 0))] * 2
        + [pl.BlockSpec((X, 2 * SMALL, channels), lambda i: (i, 0, 0))] * 2,
        out_specs=pl.BlockSpec((X, whole, channels), lambda i: (i, 0, 0)),
        out_shape=shape((places, whole, channels), bf16),
        compiler_params=GLUE_PARAMS,
    )(kept, came, small, small_came)
    chip, dconv, came_z, rows_came = lax.optimization_barrier(
        (chip, dconv, came_z, row_borders(dconv, reach))
    )
    line = pl.pallas_call(
        join_kernel,
        name="join",
        in_specs=[SMEM] + [VMEM] * 2,
        out_specs=[VMEM] * Z,
        out_shape=[shape(kept_z.shape[1:], bf16)] * Z,
        compiler_params=GLUE_PARAMS,
    )(lax.axis_index("z").reshape(1), kept_z, came_z)
    line = [
        part if step == 0 else lax.ppermute(part, "z", [(i, (i + step) % Z) for i in range(Z)])
        for step, part in enumerate(line)
    ]
    chunks, edges, line = lax.optimization_barrier(
        (exchanged(chip, ("y", "x")), column_borders(dconv, *rows_came, reach), line)
    )
    chunks = pl.pallas_call(
        plane_kernel,
        name="plane",
        in_specs=[VMEM],
        out_specs=VMEM,
        out_shape=shape((Z, 2 * each, channels), bf16),
        scratch_shapes=[pltpu.VMEM((whole, channels), f32)],
        compiler_params=GLUE_PARAMS,
    )(chunks)
    dexpand, half, chunks = pl.pallas_call(
        functools.partial(line_kernel, multiplier),
        name="line",
        in_specs=[VMEM] * (1 + Z),
        out_specs=[VMEM] * 3,
        out_shape=[
            shape((channels * each // hidden, hidden), f32),
            shape((each, channels // 2), f32),
            shape((places, each, channels), bf16),
        ],
        compiler_params=GLUE_PARAMS,
    )(exchanged(chunks, "z"), *line)
    dreduce, dkernel, dgain, dscale = pl.pallas_call(
        functools.partial(last_kernel, multiplier),
        name="last",
        in_specs=[VMEM] * 2,
        out_specs=[VMEM] * 4,
        out_shape=[shape((each, channels), f32), shape((side, side, channels), f32)]
        + [shape((1, channels), f32)] * 2,
        compiler_params=GLUE_PARAMS,
    )(exchanged(chunks, ("y", "x")), half)
    grad_features = pl.pallas_call(
        feature_kernel,
        name="features",
        in_specs=[VMEM] * 7,
        out_specs=VMEM,
        out_shape=shape((height, width, channels), bf16),
        scratch_shapes=[pltpu.VMEM(padded_shape, f32)],
        compiler_params=GLUE_PARAMS,
    )(dconv, *edges, kernel, cotangent)
    return (
        grad_features,
        dkernel,
        dgain.reshape(channels),
        dscale.reshape(channels),
        dexpand,
        dreduce,
    )


def solution(mesh):
    pixels = P(ROW, COL, None)
    return jax.shard_map(
        shards,
        mesh=Mesh(mesh.devices.reshape(Y, CORE, X, Z), (*ROW, *COL)),
        in_specs=(pixels, P(), P(), P(), P(), P(), pixels),
        out_specs=(pixels, P(), P(), P(), P((*ROW, *COL), None), P((*ROW, *COL), None)),
        check_vma=False,
    )
```

```python
import functools
import math

import jax
import jax.numpy as jnp
from jax import lax
from jax.experimental import pallas as pl
from jax.experimental.pallas import tpu as pltpu
from jax.sharding import Mesh
from jax.sharding import PartitionSpec as P

Y, CORE, X, Z = 4, 2, 4, 8
ROW, COL = ("y", "core"), ("x", "z")
INV_ROOT_TWO = 1.0 / math.sqrt(2.0)
INV_ROOT_TWO_PI = 1.0 / math.sqrt(2.0 * math.pi)
LANES = 128
LEFT = 8
SMALL = 4

NN = (((1,), (0,)), ((), ()))
NT = (((1,), (1,)), ((), ()))
TN = (((0,), (0,)), ((), ()))


def product(left, right, dims):
    return lax.dot_general(left, right, dims, preferred_element_type=jnp.float32)


def fill_own(padded, field, up, down, reach):
    height, width, channels = field.shape
    own = pl.ds(LEFT, width)
    for block in range(channels // LANES):
        lanes = pl.ds(block * LANES, LANES)
        padded[block, pl.ds(0, reach), own, :] = up[:, :, lanes].astype(jnp.float32)
        padded[block, pl.ds(reach, height), own, :] = field[:, :, lanes].astype(jnp.float32)
        padded[block, pl.ds(reach + height, reach), own, :] = down[:, :, lanes].astype(jnp.float32)


def fill_sides(padded, left, right, width, reach):
    for block in range(padded.shape[0]):
        lanes = pl.ds(block * LANES, LANES)
        padded[block, :, pl.ds(LEFT - reach, reach), :] = left[:, :, lanes].astype(jnp.float32)
        padded[block, :, pl.ds(LEFT + width, reach), :] = right[:, :, lanes].astype(jnp.float32)


def depthwise(padded, taps, block, first_col, height, side, flip):
    reach = side // 2
    totals = [None] * height
    lanes = pl.ds(pl.multiple_of(block * LANES, LANES), LANES)
    for second in range(side):
        columns = pl.ds(LEFT - reach + first_col + second, 8)
        rows = [padded[block, row, columns, :] for row in range(height + side - 1)]
        for first in range(side):
            if flip:
                weight = taps[side - 1 - first, pl.ds(side - 1 - second, 1), lanes]
            else:
                weight = taps[first, pl.ds(second, 1), lanes]
            for row in range(height):
                term = weight * rows[row + first]
                totals[row] = term if totals[row] is None else totals[row] + term
    return totals


def conv_columns(conv, padded, taps, height, width, starts):
    def conv_block(block, _):
        for first_col in starts:
            totals = depthwise(padded, taps, block, first_col, height, taps.shape[0], False)
            for row, total in enumerate(totals):
                conv[block, pl.ds(row * width + first_col, 8), :] = total
        return 0

    lax.fori_loop(0, padded.shape[0], conv_block, 0)


def prepare_kernel(
    field_h, up, down, taps_h, gain_h, scale_h, cotangent_h, expand_h, reduce_h,
    padded, conv, dbranch, dact, taps, rows_out, expand, reduce,
    field, gain, scale, cotangent, sems,
):
    copies = [
        pltpu.make_async_copy(source, target, sems.at[i])
        for i, (source, target) in enumerate(
            (
                (field_h, field),
                (taps_h, taps),
                (gain_h, gain),
                (scale_h, scale),
                (cotangent_h, cotangent),
                (reduce_h, reduce),
                (expand_h, expand),
            )
        )
    ]
    for copy in copies:
        copy.start()
    for copy in copies[:2]:
        copy.wait()
    height, width, channels = field.shape
    fill_own(padded, field, up, down, taps.shape[0] // 2)
    conv_columns(conv, padded, taps, height, width, range(8, width - 8, 8))
    for copy in copies[2:]:
        copy.wait()
    rows_out[pl.ds(0, 8), :] = jnp.broadcast_to(gain[...], (8, channels))
    rows_out[pl.ds(8, 8), :] = jnp.broadcast_to(scale[...], (8, channels))
    for row in range(height):
        value = cotangent[row].astype(jnp.float32) * scale[...]
        dbranch[pl.ds(row * width, width), :] = value.astype(jnp.bfloat16)
    step = 2 * LANES

    def hidden_block(chunk, _):
        hidden = pl.ds(pl.multiple_of(chunk * step, step), step)
        dact[:, hidden] = product(dbranch[...], reduce[hidden, :], NT)
        return 0

    lax.fori_loop(0, reduce.shape[0] // step, hidden_block, 0)


def forward_kernel(
    core_ref, left, right, padded_in, conv, dbranch, dact, taps, rows_in, expand, reduce,
    sent, kept, sent_z, kept_z, dpre_out, xhat_out, rstd_out, padded, dscale_out,
    normed, turned, chosen,
):
    core = core_ref[0]
    del padded_in
    blocks = padded.shape[0]
    side = taps.shape[0]
    height = padded.shape[1] - side + 1
    width = conv.shape[1] // height
    channels = blocks * LANES
    fill_sides(padded, left, right, width, side // 2)
    conv_columns(conv, padded, taps, height, width, (0, width - 8))
    for row in range(height):
        pixels = pl.ds(row * width, width)
        values = [conv[block, pixels, :] for block in range(blocks)]
        mean = jnp.sum(sum(values), axis=-1, keepdims=True) / channels
        values = [value - mean for value in values]
        spread = jnp.sum(sum(value * value for value in values), axis=-1, keepdims=True) / channels
        rstd = lax.rsqrt(spread + 1e-06)
        rstd_out[pixels, :] = jnp.broadcast_to(rstd, (width, LANES))
        for block, value in enumerate(values):
            lanes = pl.ds(block * LANES, LANES)
            xhat = value * rstd
            xhat_out[block, pixels, :] = xhat
            normed[pixels, lanes] = (xhat * rows_in[pl.ds(0, 1), lanes]).astype(jnp.bfloat16)
    turned[...] = normed[...].T
    part = channels // (Y * CORE)
    for y in range(Y):
        for own in range(CORE):
            owner = core if own else 1 - core
            chosen[pl.ds((own * Y + y) * part, part), :] = turned[
                pl.ds(pl.multiple_of((y * CORE + owner) * part, part), part), :
            ]
    dscale_out[...] = jnp.zeros_like(dscale_out)
    step = reduce.shape[0] // (Y * CORE)
    per_z = step // (X * Z)
    part_x = part // X
    wide = channels // step
    narrow = channels // 2
    top = per_z * Z // 2

    def hidden_block(y, _):
        for own, target, target_z in ((0, sent, sent_z), (1, kept, kept_z)):
            owner = core if own else 1 - core
            chunk = y * CORE + owner
            hidden = pl.ds(pl.multiple_of(chunk * step, step), step)
            pre = product(normed[...], expand[:, hidden], NN)
            half = 0.5 * (1.0 + lax.erf(pre * INV_ROOT_TWO))
            slope = half + pre * jnp.exp(-0.5 * pre * pre) * INV_ROOT_TWO_PI
            act = (pre * half).astype(jnp.bfloat16)
            dpre = (dact[:, hidden] * slope).astype(jnp.bfloat16)
            dpre_out[:, hidden] = dpre
            share = product(act, dbranch[...], TN)
            weighed = share * reduce[hidden, :].astype(jnp.float32)
            dscale_out[...] += jnp.sum(weighed.reshape(step // 8, 8, channels), axis=0)
            share = share.astype(jnp.bfloat16)
            for place in range(X * Z):
                x, z = place // Z, place % Z
                mine = share[place * per_z : (place + 1) * per_z]
                target[
                    y * X + x, pl.ds(z // 2 * per_z, per_z), pl.ds(z % 2 * narrow, narrow)
                ] = mine[:, :narrow]
                target_z[
                    z, y * (X // 2) + x // 2, :, pl.ds(x % 2 * narrow, narrow)
                ] = mine[:, narrow:]
            share = product(chosen[...], dpre, NN).astype(jnp.bfloat16)
            rows = pl.ds(pl.multiple_of(top + (chunk // wide) * part_x, part_x), part_x)
            lanes = pl.ds(pl.multiple_of((chunk % wide) * step, step), step)
            for place in range(Y * X):
                for back, goal in ((0, sent), (1, kept)):
                    first = back * Y * part + place * part_x
                    goal[place, rows, lanes] = share[first : first + part_x]
        return 0

    lax.fori_loop(0, Y, hidden_block, 0)


def backward_kernel(
    multiplier, dpre, expand, xhat, rstd, padded, rows, dscale, dconv_out, out, dconv, small
):
    height, width, channels = dconv_out.shape
    blocks = channels // LANES
    side = 7
    dnormed = product(dpre[...], expand[...], NT)
    for block in range(blocks):
        dconv[block] = dnormed[:, block * LANES : (block + 1) * LANES]
    sums = [jnp.zeros((width, LANES), jnp.float32)] * blocks
    for row in range(height):
        pixels = pl.ds(row * width, width)
        grads = [dconv[block, pixels, :] for block in range(blocks)]
        hats = [xhat[block, pixels, :] for block in range(blocks)]
        sums = [total + grad * hat for total, grad, hat in zip(sums, grads, hats)]
        grads = [grad * rows[pl.ds(0, 1), pl.ds(block * LANES, LANES)] for block, grad in enumerate(grads)]
        mean = jnp.sum(sum(grads), axis=-1, keepdims=True) / channels
        slant = sum(grad * hat for grad, hat in zip(grads, hats))
        slant = jnp.sum(slant, axis=-1, keepdims=True) / channels
        for block in range(blocks):
            value = rstd[pixels, :] * (grads[block] - mean - hats[block] * slant)
            dconv[block, pixels, :] = value
            dconv_out[row, :, pl.ds(block * LANES, LANES)] = value.astype(jnp.bfloat16)
    taps = side * side
    unused = small.shape[0] - taps - 2
    small[pl.ds(taps + 2, unused), :] = jnp.zeros((unused, channels), jnp.float32)
    for block in range(blocks):
        lanes = pl.ds(block * LANES, LANES)
        total = jnp.sum(sums[block], axis=0, keepdims=True)
        small[pl.ds(taps, 1), lanes] = total * multiplier
        total = jnp.sum(dscale[:, lanes], axis=0, keepdims=True)
        small[pl.ds(taps + 1, 1), lanes] = total / rows[pl.ds(8, 1), lanes] * multiplier

    def tap_block(block, _):
        lanes = pl.ds(pl.multiple_of(block * LANES, LANES), LANES)
        for second in range(side):
            totals = [jnp.zeros((8, LANES), jnp.float32)] * side
            for first_col in range(0, width, 8):
                grads = [
                    dconv[block, pl.ds(row * width + first_col, 8), :] for row in range(height)
                ]
                columns = pl.ds(LEFT - side // 2 + first_col + second, 8)
                for row in range(height + side - 1):
                    value = padded[block, row, columns, :]
                    for first in range(max(0, row - height + 1), min(side, row + 1)):
                        totals[first] = totals[first] + grads[row - first] * value
            for first, total in enumerate(totals):
                total = jnp.sum(total, axis=0, keepdims=True) * multiplier
                small[pl.ds(first * side + second, 1), lanes] = total
        return 0

    lax.fori_loop(0, blocks, tap_block, 0)
    for place in range(out.shape[0]):
        part = small[pl.ds(place * SMALL, SMALL), :]
        out[place] = jnp.concatenate([part, jnp.zeros_like(part)]).astype(jnp.bfloat16)


def feature_kernel(field, up, down, left, right, taps, cotangent, out, padded):
    height, width, channels = field.shape
    side = 7
    fill_own(padded, field, up, down, side // 2)
    fill_sides(padded, left, right, width, side // 2)
    for block in range(channels // LANES):
        lanes = pl.ds(block * LANES, LANES)
        for first_col in range(0, width, 8):
            columns = pl.ds(first_col, 8)
            for row, total in enumerate(
                depthwise(padded, taps, block, first_col, height, side, True)
            ):
                total = total + cotangent[row, columns, lanes].astype(jnp.float32)
                out[row, columns, lanes] = total.astype(jnp.bfloat16)


def added(left, right):
    return (left.astype(jnp.float32) + right.astype(jnp.float32)).astype(jnp.bfloat16)


def merge_kernel(kept, came, small, small_came, out):
    rows = kept.shape[1]
    out[:, pl.ds(0, rows), :] = added(kept[...], came[...])
    out[:, pl.ds(rows, small.shape[1]), :] = added(small[...], small_came[...])


def join_kernel(z_ref, kept, came, *outs):
    for step, out in enumerate(outs):
        z = lax.rem(z_ref[0] + step, Z)
        out[...] = added(kept[z], came[z])


def plane_kernel(chunks, out, total):
    total[...] = jnp.sum(chunks[...].astype(jnp.float32), axis=0)
    each = out.shape[1] // 2
    channels = out.shape[2]
    narrow = channels // 2
    top = each * Z // 2
    small = total[pl.ds(total.shape[0] - 2 * SMALL, SMALL), :].astype(jnp.bfloat16)
    small = jnp.concatenate([small[:, :narrow], small[:, narrow:]])
    for z in range(Z):
        parts = [total[pl.ds(top + q * 2 * Z + 2 * z, 2), :] for q in range(each // 2)]
        out[z, pl.ds(0, each), :] = jnp.concatenate(parts).astype(jnp.bfloat16)
        half = total[pl.ds(z // 2 * each, each), pl.ds(z % 2 * narrow, narrow)]
        out[z, pl.ds(each, each), pl.ds(0, narrow)] = half.astype(jnp.bfloat16)
        out[z, pl.ds(each, each), pl.ds(narrow, narrow)] = small


def line_kernel(multiplier, chunks, *refs):
    *came, dexpand, dreduce, out = refs
    total = jnp.sum(chunks[...].astype(jnp.float32), axis=0)
    each = total.shape[0] // 2
    channels = total.shape[1]
    narrow = channels // 2
    for q in range(each // 2):
        dexpand[:, pl.ds(q * channels, channels)] = total[2 * q : 2 * q + 2] * multiplier
    dreduce[...] = total[each:, :narrow] * multiplier
    small = total[each:, narrow:].astype(jnp.bfloat16)
    line = sum(ref[...].astype(jnp.float32) for ref in came).astype(jnp.bfloat16)
    for place in range(out.shape[0]):
        out[place, :, pl.ds(0, narrow)] = line[place // 2][
            :, place % 2 * narrow : (place % 2 + 1) * narrow
        ]
        out[place, :, pl.ds(narrow, narrow)] = small


def last_kernel(multiplier, chunks, half, dreduce, dkernel, dgain, dscale):
    channels = dreduce.shape[1]
    narrow = channels // 2
    dreduce[:, pl.ds(0, narrow)] = half[...]
    total = jnp.sum(chunks[:, :, pl.ds(0, narrow)].astype(jnp.float32), axis=0)
    dreduce[:, pl.ds(narrow, narrow)] = total * multiplier
    side = dkernel.shape[0]
    for place in range(chunks.shape[0]):
        part = chunks[place, :, pl.ds(narrow, narrow)].astype(jnp.float32)
        for row in range(SMALL):
            tap = place * SMALL + row
            for i in range(2):
                lanes = pl.ds(i * narrow, narrow)
                value = part[i * SMALL + row : i * SMALL + row + 1]
                if tap < side * side:
                    dkernel[tap // side, pl.ds(tap % side, 1), lanes] = value
                elif tap == side * side:
                    dgain[:, lanes] = value
                elif tap == side * side + 1:
                    dscale[:, lanes] = value


VMEM = pl.BlockSpec(memory_space=pltpu.VMEM)
HBM = pl.BlockSpec(memory_space=pltpu.HBM)
SMEM = pl.BlockSpec(memory_space=pltpu.SMEM)
PARAMS = pltpu.CompilerParams(vmem_limit_bytes=20 << 20)
GLUE_PARAMS = pltpu.CompilerParams(vmem_limit_bytes=10 << 20)


def in_hbm(value):
    return pltpu.with_memory_space_constraint(value, pltpu.HBM)


def shifted(value, axes, by):
    count = lax.axis_size(axes)
    pairs = [(i, i + by) for i in range(count) if 0 <= i + by < count]
    return lax.ppermute(value, axes, pairs)


def row_borders(field, reach):
    return shifted(field[-reach:], ROW, 1), shifted(field[:reach], ROW, -1)


def column_borders(field, up, down, reach):
    left, right = (
        jnp.concatenate([part[:, columns] for part in (up, field, down)])
        for columns in (slice(-reach, None), slice(0, reach))
    )
    return up, down, shifted(left, COL, 1), shifted(right, COL, -1)


def exchanged(chunks, axes):
    return lax.all_to_all(chunks, axes, 0, 0, tiled=True)


def shards(features, kernel, gain, w_expand, w_reduce, layer_scale, cotangent):
    height, width, channels = features.shape
    hidden = w_reduce.shape[0]
    side = kernel.shape[0]
    reach = side // 2
    blocks = channels // LANES
    pixels = height * width
    multiplier = 1.0 / math.sqrt(pixels * lax.axis_size(ROW) * lax.axis_size(COL))
    gain_row = gain.reshape(1, channels)
    scale_row = layer_scale.reshape(1, channels)
    core = lax.axis_index("core").reshape(1)
    places = Y * X
    rows = hidden // (Y * CORE * X)
    f32, bf16 = jnp.float32, jnp.bfloat16
    shape = jax.ShapeDtypeStruct
    padded_shape = (blocks, height + side - 1, LEFT + width + 8, LANES)

    each = rows // Z
    top = rows // 2
    up, down = row_borders(features, reach)
    left, right = column_borders(features, up, down, reach)[2:]
    padded, conv, dbranch, dact, taps, params, expand, reduce = pl.pallas_call(
        prepare_kernel,
        name="prepare",
        in_specs=[HBM] + [VMEM] * 2 + [HBM] * 6,
        out_specs=[VMEM] * 8,
        out_shape=[
            shape(padded_shape, f32),
            shape((blocks, pixels, LANES), f32),
            shape((pixels, channels), bf16),
            shape((pixels, hidden), f32),
            shape(kernel.shape, f32),
            shape((16, channels), f32),
            shape(w_expand.shape, bf16),
            shape(w_reduce.shape, bf16),
        ],
        scratch_shapes=[
            pltpu.VMEM(features.shape, bf16),
            pltpu.VMEM((1, channels), f32),
            pltpu.VMEM((1, channels), f32),
            pltpu.VMEM(cotangent.shape, bf16),
            pltpu.SemaphoreType.DMA((7,)),
        ],
        compiler_params=PARAMS,
    )(
        in_hbm(features), up, down, in_hbm(kernel), in_hbm(gain_row), in_hbm(scale_row),
        in_hbm(cotangent), in_hbm(w_expand), in_hbm(w_reduce),
    )
    sent, kept, sent_z, kept_z, dpre, xhat, rstd, padded, dscale = pl.pallas_call(
        forward_kernel,
        name="forward",
        in_specs=[SMEM] + [VMEM] * 10,
        out_specs=[VMEM] * 9,
        out_shape=[shape((places, top + rows, channels), bf16)] * 2
        + [shape((Z, places // 2, each, channels), bf16)] * 2
        + [
            shape((pixels, hidden), bf16),
            shape((blocks, pixels, LANES), f32),
            shape((pixels, LANES), f32),
            shape(padded_shape, f32),
            shape((8, channels), f32),
        ],
        scratch_shapes=[
            pltpu.VMEM((pixels, channels), bf16),
            pltpu.VMEM((channels, pixels), bf16),
            pltpu.VMEM((channels, pixels), bf16),
        ],
        input_output_aliases={3: 7},
        compiler_params=PARAMS,
    )(core, left, right, padded, conv, dbranch, dact, taps, params, expand, reduce)

    swap = [(0, 1), (1, 0)]
    came = lax.ppermute(sent, "core", swap)
    came_z = lax.ppermute(sent_z, "core", swap)
    dconv, small = pl.pallas_call(
        functools.partial(backward_kernel, multiplier),
        name="backward",
        in_specs=[VMEM] * 7,
        out_specs=[VMEM] * 2,
        out_shape=[
            shape((height, width, channels), bf16),
            shape((places, 2 * SMALL, channels), bf16),
        ],
        scratch_shapes=[
            pltpu.VMEM((blocks, pixels, LANES), f32),
            pltpu.VMEM((places * SMALL, channels), f32),
        ],
        compiler_params=PARAMS,
    )(dpre, expand, xhat, rstd, padded, params, dscale)

    small_came = lax.ppermute(small, "core", swap)
    whole = top + rows + 2 * SMALL
    chip = pl.pallas_call(
        merge_kernel,
        name="merge",
        grid=(Y,),
        in_specs=[pl.BlockSpec((X, top + rows, channels), lambda i: (i, 0, 0))] * 2
        + [pl.BlockSpec((X, 2 * SMALL, channels), lambda i: (i, 0, 0))] * 2,
        out_specs=pl.BlockSpec((X, whole, channels), lambda i: (i, 0, 0)),
        out_shape=shape((places, whole, channels), bf16),
        compiler_params=GLUE_PARAMS,
    )(kept, came, small, small_came)
    chip, dconv, came_z, rows_came = lax.optimization_barrier(
        (chip, dconv, came_z, row_borders(dconv, reach))
    )
    line = pl.pallas_call(
        join_kernel,
        name="join",
        in_specs=[SMEM] + [VMEM] * 2,
        out_specs=[VMEM] * Z,
        out_shape=[shape(kept_z.shape[1:], bf16)] * Z,
        compiler_params=GLUE_PARAMS,
    )(lax.axis_index("z").reshape(1), kept_z, came_z)
    line = [
        part if step == 0 else lax.ppermute(part, "z", [(i, (i + step) % Z) for i in range(Z)])
        for step, part in enumerate(line)
    ]
    chunks, edges, line = lax.optimization_barrier(
        (exchanged(chip, ("y", "x")), column_borders(dconv, *rows_came, reach), line)
    )
    chunks = pl.pallas_call(
        plane_kernel,
        name="plane",
        in_specs=[VMEM],
        out_specs=VMEM,
        out_shape=shape((Z, 2 * each, channels), bf16),
        scratch_shapes=[pltpu.VMEM((whole, channels), f32)],
        compiler_params=GLUE_PARAMS,
    )(chunks)
    dexpand, half, chunks = pl.pallas_call(
        functools.partial(line_kernel, multiplier),
        name="line",
        in_specs=[VMEM] * (1 + Z),
        out_specs=[VMEM] * 3,
        out_shape=[
            shape((channels * each // hidden, hidden), f32),
            shape((each, channels // 2), f32),
            shape((places, each, channels), bf16),
        ],
        compiler_params=GLUE_PARAMS,
    )(exchanged(chunks, "z"), *line)
    dreduce, dkernel, dgain, dscale = pl.pallas_call(
        functools.partial(last_kernel, multiplier),
        name="last",
        in_specs=[VMEM] * 2,
        out_specs=[VMEM] * 4,
        out_shape=[shape((each, channels), f32), shape((side, side, channels), f32)]
        + [shape((1, channels), f32)] * 2,
        compiler_params=GLUE_PARAMS,
    )(exchanged(chunks, ("y", "x")), half)
    grad_features = pl.pallas_call(
        feature_kernel,
        name="features",
        in_specs=[VMEM] * 7,
        out_specs=VMEM,
        out_shape=shape((height, width, channels), bf16),
        scratch_shapes=[pltpu.VMEM(padded_shape, f32)],
        compiler_params=GLUE_PARAMS,
    )(dconv, *edges, kernel, cotangent)
    return (
        grad_features,
        dkernel,
        dgain.reshape(channels),
        dscale.reshape(channels),
        dexpand,
        dreduce,
    )


def solution(mesh):
    pixels = P(ROW, COL, None)
    return jax.shard_map(
        shards,
        mesh=Mesh(mesh.devices.reshape(Y, CORE, X, Z), (*ROW, *COL)),
        in_specs=(pixels, P(), P(), P(), P(), P(), pixels),
        out_specs=(pixels, P(), P(), P(), P((*ROW, *COL), None), P((*ROW, *COL), None)),
        check_vma=False,
    )
```

```python
import functools
import math

import jax
import jax.numpy as jnp
from jax import lax
from jax.experimental import pallas as pl
from jax.experimental.pallas import tpu as pltpu
from jax.sharding import Mesh
from jax.sharding import PartitionSpec as P

Y, CORE, X, Z = 4, 2, 4, 8
ROW, COL = ("y", "core"), ("x", "z")
INV_ROOT_TWO = 1.0 / math.sqrt(2.0)
INV_ROOT_TWO_PI = 1.0 / math.sqrt(2.0 * math.pi)
LANES = 128
LEFT = 8
SMALL = 32

NN = (((1,), (0,)), ((), ()))
NT = (((1,), (1,)), ((), ()))
TN = (((0,), (0,)), ((), ()))


def product(left, right, dims):
    return lax.dot_general(left, right, dims, preferred_element_type=jnp.float32)


def fill_own(padded, field, up, down, reach):
    height, width, channels = field.shape
    own = pl.ds(LEFT, width)
    for block in range(channels // LANES):
        lanes = pl.ds(block * LANES, LANES)
        padded[block, pl.ds(0, reach), own, :] = up[:, :, lanes].astype(jnp.float32)
        padded[block, pl.ds(reach, height), own, :] = field[:, :, lanes].astype(jnp.float32)
        padded[block, pl.ds(reach + height, reach), own, :] = down[:, :, lanes].astype(jnp.float32)


def fill_sides(padded, left, right, width, reach):
    for block in range(padded.shape[0]):
        lanes = pl.ds(block * LANES, LANES)
        padded[block, :, pl.ds(LEFT - reach, reach), :] = left[:, :, lanes].astype(jnp.float32)
        padded[block, :, pl.ds(LEFT + width, reach), :] = right[:, :, lanes].astype(jnp.float32)


def depthwise(padded, taps, block, first_col, height, side, flip):
    reach = side // 2
    totals = [None] * height
    lanes = pl.ds(pl.multiple_of(block * LANES, LANES), LANES)
    for second in range(side):
        columns = pl.ds(LEFT - reach + first_col + second, 8)
        rows = [padded[block, row, columns, :] for row in range(height + side - 1)]
        for first in range(side):
            if flip:
                weight = taps[side - 1 - first, pl.ds(side - 1 - second, 1), lanes]
            else:
                weight = taps[first, pl.ds(second, 1), lanes]
            for row in range(height):
                term = weight * rows[row + first]
                totals[row] = term if totals[row] is None else totals[row] + term
    return totals


def conv_columns(conv, padded, taps, height, width, starts):
    def conv_block(block, _):
        for first_col in starts:
            totals = depthwise(padded, taps, block, first_col, height, taps.shape[0], False)
            for row, total in enumerate(totals):
                conv[block, pl.ds(row * width + first_col, 8), :] = total
        return 0

    lax.fori_loop(0, padded.shape[0], conv_block, 0)


def prepare_kernel(
    field_h, down, up, taps_h, gain_h, scale_h, cotangent_h, expand_h, reduce_h,
    padded, conv, dbranch, dact, taps, rows_out, expand, reduce,
    field, gain, scale, cotangent, sems,
):
    copies = [
        pltpu.make_async_copy(source, target, sems.at[i])
        for i, (source, target) in enumerate(
            (
                (field_h, field),
                (taps_h, taps),
                (gain_h, gain),
                (scale_h, scale),
                (cotangent_h, cotangent),
                (reduce_h, reduce),
                (expand_h, expand),
            )
        )
    ]
    for copy in copies:
        copy.start()
    for copy in copies[:2]:
        copy.wait()
    height, width, channels = field.shape
    fill_own(padded, field, up, down, taps.shape[0] // 2)
    conv_columns(conv, padded, taps, height, width, range(8, width - 8, 8))
    for copy in copies[2:]:
        copy.wait()
    rows_out[pl.ds(0, 8), :] = jnp.broadcast_to(gain[...], (8, channels))
    rows_out[pl.ds(8, 8), :] = jnp.broadcast_to(scale[...], (8, channels))
    for row in range(height):
        value = cotangent[row].astype(jnp.float32) * scale[...]
        dbranch[pl.ds(row * width, width), :] = value.astype(jnp.bfloat16)
    step = 2 * LANES

    def hidden_block(chunk, _):
        hidden = pl.ds(pl.multiple_of(chunk * step, step), step)
        dact[:, hidden] = product(dbranch[...], reduce[hidden, :], NT)
        return 0

    lax.fori_loop(0, reduce.shape[0] // step, hidden_block, 0)


def forward_kernel(
    core_ref, left, right, padded_in, conv, dbranch, dact, taps, rows_in, expand, reduce,
    sent, kept, dpre_out, xhat_out, rstd_out, padded, dscale_out,
    normed, turned, chosen,
):
    core = core_ref[0]
    del padded_in
    blocks = padded.shape[0]
    side = taps.shape[0]
    height = padded.shape[1] - side + 1
    width = conv.shape[1] // height
    channels = blocks * LANES
    fill_sides(padded, left, right, width, side // 2)
    conv_columns(conv, padded, taps, height, width, (0, width - 8))
    for row in range(height):
        pixels = pl.ds(row * width, width)
        values = [conv[block, pixels, :] for block in range(blocks)]
        mean = jnp.sum(sum(values), axis=-1, keepdims=True) / channels
        values = [value - mean for value in values]
        spread = jnp.sum(sum(value * value for value in values), axis=-1, keepdims=True) / channels
        rstd = lax.rsqrt(spread + 1e-06)
        rstd_out[pixels, :] = jnp.broadcast_to(rstd, (width, LANES))
        for block, value in enumerate(values):
            lanes = pl.ds(block * LANES, LANES)
            xhat = value * rstd
            xhat_out[block, pixels, :] = xhat
            normed[pixels, lanes] = (xhat * rows_in[pl.ds(0, 1), lanes]).astype(jnp.bfloat16)
    turned[...] = normed[...].T
    part = channels // (Y * CORE)
    for y in range(Y):
        for own in range(CORE):
            owner = core if own else 1 - core
            chosen[pl.ds((own * Y + y) * part, part), :] = turned[
                pl.ds(pl.multiple_of((y * CORE + owner) * part, part), part), :
            ]
    dscale_out[...] = jnp.zeros_like(dscale_out)
    step = reduce.shape[0] // (Y * CORE)
    per_z = step // (X * Z)
    part_x = part // X
    wide = channels // step
    top = per_z * Z

    def hidden_block(y, _):
        for own, target in ((0, sent), (1, kept)):
            owner = core if own else 1 - core
            chunk = y * CORE + owner
            hidden = pl.ds(pl.multiple_of(chunk * step, step), step)
            pre = product(normed[...], expand[:, hidden], NN)
            half = 0.5 * (1.0 + lax.erf(pre * INV_ROOT_TWO))
            slope = half + pre * jnp.exp(-0.5 * pre * pre) * INV_ROOT_TWO_PI
            act = (pre * half).astype(jnp.bfloat16)
            dpre = (dact[:, hidden] * slope).astype(jnp.bfloat16)
            dpre_out[:, hidden] = dpre
            share = product(act, dbranch[...], TN)
            weighed = share * reduce[hidden, :].astype(jnp.float32)
            dscale_out[...] += jnp.sum(weighed.reshape(step // 8, 8, channels), axis=0)
            share = share.astype(jnp.bfloat16)
            for x in range(X):
                target[y * X + x, pl.ds(0, top), :] = share[x * top : (x + 1) * top]
            share = product(chosen[...], dpre, NN).astype(jnp.bfloat16)
            rows = pl.ds(pl.multiple_of(top + (chunk // wide) * part_x, part_x), part_x)
            lanes = pl.ds(pl.multiple_of((chunk % wide) * step, step), step)
            for place in range(Y * X):
                for back, goal in ((0, sent), (1, kept)):
                    first = back * Y * part + place * part_x
                    goal[place, rows, lanes] = share[first : first + part_x]
        return 0

    lax.fori_loop(0, Y, hidden_block, 0)


def backward_kernel(
    multiplier, core_ref, dpre, expand, xhat, rstd, padded, rows, dscale,
    dconv_out, sent, kept, dconv, small,
):
    height, width, channels = dconv_out.shape
    blocks = channels // LANES
    side = 7
    dnormed = product(dpre[...], expand[...], NT)
    for block in range(blocks):
        dconv[block] = dnormed[:, block * LANES : (block + 1) * LANES]
    sums = [jnp.zeros((width, LANES), jnp.float32)] * blocks
    for row in range(height):
        pixels = pl.ds(row * width, width)
        grads = [dconv[block, pixels, :] for block in range(blocks)]
        hats = [xhat[block, pixels, :] for block in range(blocks)]
        sums = [total + grad * hat for total, grad, hat in zip(sums, grads, hats)]
        grads = [grad * rows[pl.ds(0, 1), pl.ds(block * LANES, LANES)] for block, grad in enumerate(grads)]
        mean = jnp.sum(sum(grads), axis=-1, keepdims=True) / channels
        slant = sum(grad * hat for grad, hat in zip(grads, hats))
        slant = jnp.sum(slant, axis=-1, keepdims=True) / channels
        for block in range(blocks):
            value = rstd[pixels, :] * (grads[block] - mean - hats[block] * slant)
            dconv[block, pixels, :] = value
            dconv_out[row, :, pl.ds(block * LANES, LANES)] = value.astype(jnp.bfloat16)
    taps = side * side
    unused = small.shape[0] - taps - 2
    small[pl.ds(taps + 2, unused), :] = jnp.zeros((unused, channels), jnp.float32)
    for block in range(blocks):
        lanes = pl.ds(block * LANES, LANES)
        total = jnp.sum(sums[block], axis=0, keepdims=True)
        small[pl.ds(taps, 1), lanes] = total * multiplier
        total = jnp.sum(dscale[:, lanes], axis=0, keepdims=True)
        small[pl.ds(taps + 1, 1), lanes] = total / rows[pl.ds(8, 1), lanes] * multiplier

    def tap_block(block, _):
        lanes = pl.ds(pl.multiple_of(block * LANES, LANES), LANES)
        for second in range(side):
            totals = [jnp.zeros((8, LANES), jnp.float32)] * side
            for first_col in range(0, width, 8):
                grads = [
                    dconv[block, pl.ds(row * width + first_col, 8), :] for row in range(height)
                ]
                columns = pl.ds(LEFT - side // 2 + first_col + second, 8)
                for row in range(height + side - 1):
                    value = padded[block, row, columns, :]
                    for first in range(max(0, row - height + 1), min(side, row + 1)):
                        totals[first] = totals[first] + grads[row - first] * value
            for first, total in enumerate(totals):
                total = jnp.sum(total, axis=0, keepdims=True) * multiplier
                small[pl.ds(first * side + second, 1), lanes] = total
        return 0

    lax.fori_loop(0, blocks, tap_block, 0)
    for out, core in ((sent, 1 - core_ref[0]), (kept, core_ref[0])):
        half = small[pl.ds(pl.multiple_of(core * SMALL, SMALL), SMALL), :]
        out[...] = half.astype(jnp.bfloat16)


def feature_kernel(field, up, down, left, right, taps, cotangent, out, padded):
    height, width, channels = field.shape
    side = 7
    fill_own(padded, field, up, down, side // 2)
    fill_sides(padded, left, right, width, side // 2)
    for block in range(channels // LANES):
        lanes = pl.ds(block * LANES, LANES)
        for first_col in range(0, width, 8):
            columns = pl.ds(first_col, 8)
            for row, total in enumerate(
                depthwise(padded, taps, block, first_col, height, side, True)
            ):
                total = total + cotangent[row, columns, lanes].astype(jnp.float32)
                out[row, columns, lanes] = total.astype(jnp.bfloat16)


def added(left, right):
    return (left.astype(jnp.float32) + right.astype(jnp.float32)).astype(jnp.bfloat16)


def merge_kernel(kept, came, out):
    out[...] = added(kept[...], came[...])


def plane_kernel(chunks, out, total):
    total[...] = jnp.sum(chunks[...].astype(jnp.float32), axis=0)
    each = out.shape[1] // 2
    top = each * Z
    for z in range(Z):
        parts = [total[pl.ds(z * each, each), :]]
        parts += [total[pl.ds(top + q * 2 * Z + 2 * z, 2), :] for q in range(each // 2)]
        out[z] = jnp.concatenate(parts).astype(jnp.bfloat16)


def line_kernel(multiplier, chunks, dreduce, dexpand):
    total = jnp.sum(chunks[...].astype(jnp.float32), axis=0)
    each, channels = dreduce.shape
    dreduce[...] = total[:each] * multiplier
    for q in range(each // 2):
        part = total[each + 2 * q : each + 2 * q + 2]
        dexpand[:, pl.ds(q * channels, channels)] = part * multiplier


def small_kernel(core_ref, own, other, dkernel, dgain, dscale, full):
    full[core_ref[0]] = own[...].astype(jnp.float32)
    full[1 - core_ref[0]] = other[...].astype(jnp.float32)
    side = dkernel.shape[0]
    for tap in range(side * side + 2):
        value = full[tap // SMALL, pl.ds(tap % SMALL, 1), :]
        if tap < side * side:
            dkernel[tap // side, pl.ds(tap % side, 1), :] = value
        elif tap == side * side:
            dgain[...] = value
        else:
            dscale[...] = value


VMEM = pl.BlockSpec(memory_space=pltpu.VMEM)
HBM = pl.BlockSpec(memory_space=pltpu.HBM)
SMEM = pl.BlockSpec(memory_space=pltpu.SMEM)
PARAMS = pltpu.CompilerParams(vmem_limit_bytes=20 << 20)
GLUE_PARAMS = pltpu.CompilerParams(vmem_limit_bytes=10 << 20)


def in_hbm(value):
    return pltpu.with_memory_space_constraint(value, pltpu.HBM)


def shifted(value, axes, by):
    count = lax.axis_size(axes)
    pairs = [(i, i + by) for i in range(count) if 0 <= i + by < count]
    return lax.ppermute(value, axes, pairs)


def row_borders(field, reach):
    down = shifted(field[:reach], ROW, -1)
    return shifted(field[-reach:], ROW, 1), down


def paired(value, axis, apart):
    count = lax.axis_size(axis)
    came = lax.ppermute(value, axis, [(i, i ^ apart) for i in range(count)])
    return added(value, came)


def column_borders(field, up, down, reach):
    left, right = (
        jnp.concatenate([part[:, columns] for part in (up, field, down)])
        for columns in (slice(-reach, None), slice(0, reach))
    )
    right = shifted(right, COL, -1)
    return up, down, shifted(left, COL, 1), right


def exchanged(chunks, axes):
    return lax.all_to_all(chunks, axes, 0, 0, tiled=True)


def shards(features, kernel, gain, w_expand, w_reduce, layer_scale, cotangent):
    height, width, channels = features.shape
    hidden = w_reduce.shape[0]
    side = kernel.shape[0]
    reach = side // 2
    blocks = channels // LANES
    pixels = height * width
    multiplier = 1.0 / math.sqrt(pixels * lax.axis_size(ROW) * lax.axis_size(COL))
    gain_row = gain.reshape(1, channels)
    scale_row = layer_scale.reshape(1, channels)
    core = lax.axis_index("core").reshape(1)
    places = Y * X
    rows = hidden // (Y * CORE * X)
    f32, bf16 = jnp.float32, jnp.bfloat16
    shape = jax.ShapeDtypeStruct
    padded_shape = (blocks, height + side - 1, LEFT + width + 8, LANES)

    each = rows // Z
    up, down = row_borders(features, reach)
    left, right = column_borders(features, up, down, reach)[2:]
    padded, conv, dbranch, dact, taps, params, expand, reduce = pl.pallas_call(
        prepare_kernel,
        name="prepare",
        in_specs=[HBM] + [VMEM] * 2 + [HBM] * 6,
        out_specs=[VMEM] * 8,
        out_shape=[
            shape(padded_shape, f32),
            shape((blocks, pixels, LANES), f32),
            shape((pixels, channels), bf16),
            shape((pixels, hidden), f32),
            shape(kernel.shape, f32),
            shape((16, channels), f32),
            shape(w_expand.shape, bf16),
            shape(w_reduce.shape, bf16),
        ],
        scratch_shapes=[
            pltpu.VMEM(features.shape, bf16),
            pltpu.VMEM((1, channels), f32),
            pltpu.VMEM((1, channels), f32),
            pltpu.VMEM(cotangent.shape, bf16),
            pltpu.SemaphoreType.DMA((7,)),
        ],
        compiler_params=PARAMS,
    )(
        in_hbm(features), down, up, in_hbm(kernel), in_hbm(gain_row), in_hbm(scale_row),
        in_hbm(cotangent), in_hbm(w_expand), in_hbm(w_reduce),
    )
    sent, kept, dpre, xhat, rstd, padded, dscale = pl.pallas_call(
        forward_kernel,
        name="forward",
        in_specs=[SMEM] + [VMEM] * 10,
        out_specs=[VMEM] * 7,
        out_shape=[shape((places, 2 * rows, channels), bf16)] * 2
        + [
            shape((pixels, hidden), bf16),
            shape((blocks, pixels, LANES), f32),
            shape((pixels, LANES), f32),
            shape(padded_shape, f32),
            shape((8, channels), f32),
        ],
        scratch_shapes=[
            pltpu.VMEM((pixels, channels), bf16),
            pltpu.VMEM((channels, pixels), bf16),
            pltpu.VMEM((channels, pixels), bf16),
        ],
        input_output_aliases={3: 5},
        compiler_params=PARAMS,
    )(core, left, right, padded, conv, dbranch, dact, taps, params, expand, reduce)

    swap = [(0, 1), (1, 0)]
    came = lax.ppermute(sent, "core", swap)
    dconv, small_sent, small = pl.pallas_call(
        functools.partial(backward_kernel, multiplier),
        name="backward",
        in_specs=[SMEM] + [VMEM] * 7,
        out_specs=[VMEM] * 3,
        out_shape=[
            shape((height, width, channels), bf16),
            shape((SMALL, channels), bf16),
            shape((SMALL, channels), bf16),
        ],
        scratch_shapes=[
            pltpu.VMEM((blocks, pixels, LANES), f32),
            pltpu.VMEM((CORE * SMALL, channels), f32),
        ],
        compiler_params=PARAMS,
    )(core, dpre, expand, xhat, rstd, padded, params, dscale)

    small_came = lax.ppermute(small_sent, "core", swap)
    block = pl.BlockSpec((X, 2 * rows, channels), lambda i: (i, 0, 0))
    chip = pl.pallas_call(
        merge_kernel,
        name="merge",
        grid=(Y,),
        in_specs=[block] * 2,
        out_specs=block,
        out_shape=shape((places, 2 * rows, channels), bf16),
        compiler_params=GLUE_PARAMS,
    )(kept, came)
    chip, dconv, small, small_came, rows_came = lax.optimization_barrier(
        (chip, dconv, small, small_came, row_borders(dconv, reach))
    )
    small = added(small, small_came)
    for axis, apart in (("z", 1), ("z", 2), ("z", 4), ("x", 1), ("x", 2)):
        small = paired(small, axis, apart)
    chunks, edges, small = lax.optimization_barrier(
        (exchanged(chip, ("y", "x")), column_borders(dconv, *rows_came, reach), small)
    )
    chunks = pl.pallas_call(
        plane_kernel,
        name="plane",
        in_specs=[VMEM],
        out_specs=VMEM,
        out_shape=shape((Z, 2 * each, channels), bf16),
        scratch_shapes=[pltpu.VMEM((2 * rows, channels), f32)],
        compiler_params=GLUE_PARAMS,
    )(chunks)
    chunks, small = lax.optimization_barrier((chunks, small))
    for apart in (1, 2):
        small = paired(small, "y", apart)
    dreduce, dexpand = pl.pallas_call(
        functools.partial(line_kernel, multiplier),
        name="line",
        in_specs=[VMEM],
        out_specs=[VMEM] * 2,
        out_shape=[
            shape((each, channels), f32),
            shape((channels * each // hidden, hidden), f32),
        ],
        compiler_params=GLUE_PARAMS,
    )(exchanged(chunks, "z"))
    dkernel, dgain, dscale = pl.pallas_call(
        small_kernel,
        name="small",
        in_specs=[SMEM] + [VMEM] * 2,
        out_specs=[VMEM] * 3,
        out_shape=[shape((side, side, channels), f32)] + [shape((1, channels), f32)] * 2,
        scratch_shapes=[pltpu.VMEM((CORE, SMALL, channels), f32)],
        compiler_params=GLUE_PARAMS,
    )(core, small, lax.ppermute(small, "core", swap))
    grad_features = pl.pallas_call(
        feature_kernel,
        name="features",
        in_specs=[VMEM] * 7,
        out_specs=VMEM,
        out_shape=shape((height, width, channels), bf16),
        scratch_shapes=[pltpu.VMEM(padded_shape, f32)],
        compiler_params=GLUE_PARAMS,
    )(dconv, *edges, kernel, cotangent)
    return (
        grad_features,
        dkernel,
        dgain.reshape(channels),
        dscale.reshape(channels),
        dexpand,
        dreduce,
    )


def solution(mesh):
    pixels = P(ROW, COL, None)
    return jax.shard_map(
        shards,
        mesh=Mesh(mesh.devices.reshape(Y, CORE, X, Z), (*ROW, *COL)),
        in_specs=(pixels, P(), P(), P(), P(), P(), pixels),
        out_specs=(pixels, P(), P(), P(), P((*ROW, *COL), None), P((*ROW, *COL), None)),
        check_vma=False,
    )
```

```python
import functools
import math

import jax
import jax.numpy as jnp
from jax import lax
from jax.experimental import pallas as pl
from jax.experimental.pallas import tpu as pltpu
from jax.sharding import Mesh
from jax.sharding import PartitionSpec as P

Y, CORE, X, Z = 4, 2, 4, 8
ROW, COL = ("y", "core"), ("x", "z")
INV_ROOT_TWO = 1.0 / math.sqrt(2.0)
INV_ROOT_TWO_PI = 1.0 / math.sqrt(2.0 * math.pi)
LANES = 128
LEFT = 8
SMALL = 4

NN = (((1,), (0,)), ((), ()))
NT = (((1,), (1,)), ((), ()))
TN = (((0,), (0,)), ((), ()))


def product(left, right, dims):
    return lax.dot_general(left, right, dims, preferred_element_type=jnp.float32)


def fill_own(padded, field, up, down, reach):
    height, width, channels = field.shape
    own = pl.ds(LEFT, width)
    for block in range(channels // LANES):
        lanes = pl.ds(block * LANES, LANES)
        padded[block, pl.ds(0, reach), own, :] = up[:, :, lanes].astype(jnp.float32)
        padded[block, pl.ds(reach, height), own, :] = field[:, :, lanes].astype(jnp.float32)
        padded[block, pl.ds(reach + height, reach), own, :] = down[:, :, lanes].astype(jnp.float32)


def fill_sides(padded, left, right, width, reach):
    rows = padded.shape[1]
    places = ((0, rows - reach, reach), (reach, reach, rows - 2 * reach), (rows - reach, 0, reach))
    for block in range(padded.shape[0]):
        lanes = pl.ds(block * LANES, LANES)
        for side, column in ((left, LEFT - reach), (right, LEFT + width)):
            value = side[:, :, lanes].astype(jnp.float32)
            for source, target, count in places:
                padded[block, pl.ds(target, count), pl.ds(column, reach), :] = value[
                    source : source + count
                ]


def depthwise(padded, taps, block, first_col, height, side, flip):
    reach = side // 2
    totals = [None] * height
    lanes = pl.ds(pl.multiple_of(block * LANES, LANES), LANES)
    for second in range(side):
        columns = pl.ds(LEFT - reach + first_col + second, 8)
        rows = [padded[block, row, columns, :] for row in range(height + side - 1)]
        for first in range(side):
            if flip:
                weight = taps[side - 1 - first, pl.ds(side - 1 - second, 1), lanes]
            else:
                weight = taps[first, pl.ds(second, 1), lanes]
            for row in range(height):
                term = weight * rows[row + first]
                totals[row] = term if totals[row] is None else totals[row] + term
    return totals


def conv_columns(conv, padded, taps, height, width, starts):
    def conv_block(block, _):
        for first_col in starts:
            totals = depthwise(padded, taps, block, first_col, height, taps.shape[0], False)
            for row, total in enumerate(totals):
                conv[block, pl.ds(row * width + first_col, 8), :] = total
        return 0

    lax.fori_loop(0, padded.shape[0], conv_block, 0)


def prepare_kernel(
    field_h, up, down, taps_h, gain_h, scale_h, cotangent_h, expand_h, reduce_h,
    padded, conv, dbranch, taps, rows_out, expand, reduce,
    field, gain, scale, cotangent, sems,
):
    copies = [
        pltpu.make_async_copy(source, target, sems.at[i])
        for i, (source, target) in enumerate(
            (
                (field_h, field),
                (taps_h, taps),
                (gain_h, gain),
                (scale_h, scale),
                (cotangent_h, cotangent),
                (reduce_h, reduce),
                (expand_h, expand),
            )
        )
    ]
    for copy in copies:
        copy.start()
    for copy in copies[:2]:
        copy.wait()
    height, width, channels = field.shape
    fill_own(padded, field, up, down, taps.shape[0] // 2)
    conv_columns(conv, padded, taps, height, width, range(8, width - 8, 8))
    for copy in copies[2:5]:
        copy.wait()
    rows_out[pl.ds(0, 8), :] = jnp.broadcast_to(gain[...], (8, channels))
    rows_out[pl.ds(8, 8), :] = jnp.broadcast_to(scale[...], (8, channels))
    for row in range(height):
        value = cotangent[row].astype(jnp.float32) * scale[...]
        dbranch[pl.ds(row * width, width), :] = value.astype(jnp.bfloat16)
    for copy in copies[5:]:
        copy.wait()


def forward_kernel(
    core_ref, left, right, padded_in, conv, dbranch, taps, rows_in, expand, reduce,
    sent, kept, dpre_out, xhat_out, rstd_out, padded, dscale_out,
    normed, turned, chosen,
):
    core = core_ref[0]
    del padded_in
    blocks = padded.shape[0]
    side = taps.shape[0]
    height = padded.shape[1] - side + 1
    width = conv.shape[1] // height
    channels = blocks * LANES
    fill_sides(padded, left, right, width, side // 2)
    conv_columns(conv, padded, taps, height, width, (0, width - 8))
    for row in range(height):
        pixels = pl.ds(row * width, width)
        values = [conv[block, pixels, :] for block in range(blocks)]
        mean = jnp.sum(sum(values), axis=-1, keepdims=True) / channels
        values = [value - mean for value in values]
        spread = jnp.sum(sum(value * value for value in values), axis=-1, keepdims=True) / channels
        rstd = lax.rsqrt(spread + 1e-06)
        rstd_out[pixels, :] = jnp.broadcast_to(rstd, (width, LANES))
        for block, value in enumerate(values):
            lanes = pl.ds(block * LANES, LANES)
            xhat = value * rstd
            xhat_out[block, pixels, :] = xhat
            normed[pixels, lanes] = (xhat * rows_in[pl.ds(0, 1), lanes]).astype(jnp.bfloat16)
    turned[...] = normed[...].T
    part = channels // (Y * CORE)
    for y in range(Y):
        for own in range(CORE):
            owner = core if own else 1 - core
            chosen[pl.ds((own * Y + y) * part, part), :] = turned[
                pl.ds(pl.multiple_of((y * CORE + owner) * part, part), part), :
            ]
    dscale_out[...] = jnp.zeros_like(dscale_out)
    step = reduce.shape[0] // (Y * CORE)
    per_z = step // (X * Z)
    part_x = part // X
    wide = channels // step
    top = per_z * Z

    def hidden_block(y, _):
        for own, target in ((0, sent), (1, kept)):
            owner = core if own else 1 - core
            chunk = y * CORE + owner
            hidden = pl.ds(pl.multiple_of(chunk * step, step), step)
            pre = product(normed[...], expand[:, hidden], NN)
            dact = product(dbranch[...], reduce[hidden, :], NT)
            half = 0.5 * (1.0 + lax.erf(pre * INV_ROOT_TWO))
            slope = half + pre * jnp.exp(-0.5 * pre * pre) * INV_ROOT_TWO_PI
            act = (pre * half).astype(jnp.bfloat16)
            dpre = (dact * slope).astype(jnp.bfloat16)
            dpre_out[:, hidden] = dpre
            share = product(act, dbranch[...], TN)
            weighed = share * reduce[hidden, :].astype(jnp.float32)
            dscale_out[...] += jnp.sum(weighed.reshape(step // 8, 8, channels), axis=0)
            share = share.astype(jnp.bfloat16)
            for x in range(X):
                target[y * X + x, pl.ds(0, top), :] = share[x * top : (x + 1) * top]
            share = product(chosen[...], dpre, NN).astype(jnp.bfloat16)
            rows = pl.ds(pl.multiple_of(top + (chunk // wide) * part_x, part_x), part_x)
            lanes = pl.ds(pl.multiple_of((chunk % wide) * step, step), step)
            for place in range(Y * X):
                for back, goal in ((0, sent), (1, kept)):
                    first = back * Y * part + place * part_x
                    goal[place, rows, lanes] = share[first : first + part_x]
        return 0

    lax.fori_loop(0, Y, hidden_block, 0)


def backward_kernel(
    multiplier, dpre, expand, xhat, rstd, padded, rows, dscale, dconv_out, out, dconv, small
):
    height, width, channels = dconv_out.shape
    blocks = channels // LANES
    side = 7
    dnormed = product(dpre[...], expand[...], NT)
    for block in range(blocks):
        dconv[block] = dnormed[:, block * LANES : (block + 1) * LANES]
    sums = [jnp.zeros((width, LANES), jnp.float32)] * blocks
    for row in range(height):
        pixels = pl.ds(row * width, width)
        grads = [dconv[block, pixels, :] for block in range(blocks)]
        hats = [xhat[block, pixels, :] for block in range(blocks)]
        sums = [total + grad * hat for total, grad, hat in zip(sums, grads, hats)]
        grads = [grad * rows[pl.ds(0, 1), pl.ds(block * LANES, LANES)] for block, grad in enumerate(grads)]
        mean = jnp.sum(sum(grads), axis=-1, keepdims=True) / channels
        slant = sum(grad * hat for grad, hat in zip(grads, hats))
        slant = jnp.sum(slant, axis=-1, keepdims=True) / channels
        for block in range(blocks):
            value = rstd[pixels, :] * (grads[block] - mean - hats[block] * slant)
            dconv[block, pixels, :] = value
            dconv_out[row, :, pl.ds(block * LANES, LANES)] = value.astype(jnp.bfloat16)
    taps = side * side
    unused = small.shape[0] - taps - 2
    small[pl.ds(taps + 2, unused), :] = jnp.zeros((unused, channels), jnp.float32)
    for block in range(blocks):
        lanes = pl.ds(block * LANES, LANES)
        total = jnp.sum(sums[block], axis=0, keepdims=True)
        small[pl.ds(taps, 1), lanes] = total * multiplier
        total = jnp.sum(dscale[:, lanes], axis=0, keepdims=True)
        small[pl.ds(taps + 1, 1), lanes] = total / rows[pl.ds(8, 1), lanes] * multiplier

    def tap_block(block, _):
        lanes = pl.ds(pl.multiple_of(block * LANES, LANES), LANES)
        for second in range(side):
            totals = [jnp.zeros((8, LANES), jnp.float32)] * side
            for first_col in range(0, width, 8):
                grads = [
                    dconv[block, pl.ds(row * width + first_col, 8), :] for row in range(height)
                ]
                columns = pl.ds(LEFT - side // 2 + first_col + second, 8)
                for row in range(height + side - 1):
                    value = padded[block, row, columns, :]
                    for first in range(max(0, row - height + 1), min(side, row + 1)):
                        totals[first] = totals[first] + grads[row - first] * value
            for first, total in enumerate(totals):
                total = jnp.sum(total, axis=0, keepdims=True) * multiplier
                small[pl.ds(first * side + second, 1), lanes] = total
        return 0

    lax.fori_loop(0, blocks, tap_block, 0)
    for place in range(out.shape[0]):
        part = small[pl.ds(place * SMALL, SMALL), :]
        out[place] = jnp.concatenate([part, jnp.zeros_like(part)]).astype(jnp.bfloat16)


def feature_kernel(field, up, down, left, right, taps, cotangent, out, padded):
    height, width, channels = field.shape
    side = 7
    fill_own(padded, field, up, down, side // 2)
    fill_sides(padded, left, right, width, side // 2)
    for block in range(channels // LANES):
        lanes = pl.ds(block * LANES, LANES)
        for first_col in range(0, width, 8):
            columns = pl.ds(first_col, 8)
            for row, total in enumerate(
                depthwise(padded, taps, block, first_col, height, side, True)
            ):
                total = total + cotangent[row, columns, lanes].astype(jnp.float32)
                out[row, columns, lanes] = total.astype(jnp.bfloat16)


def added(left, right):
    return (left.astype(jnp.float32) + right.astype(jnp.float32)).astype(jnp.bfloat16)


def merge_kernel(kept, came, small, small_came, out):
    rows = kept.shape[1]
    out[:, pl.ds(0, rows), :] = added(kept[...], came[...])
    out[:, pl.ds(rows, small.shape[1]), :] = added(small[...], small_came[...])


def plane_kernel(chunks, out, total):
    total[...] = jnp.sum(chunks[...].astype(jnp.float32), axis=0)
    each = (out.shape[1] - 2 * SMALL) // 2
    top = each * Z
    small = total[pl.ds(2 * top, 2 * SMALL), :].astype(jnp.bfloat16)
    for z in range(Z):
        parts = [total[pl.ds(z * each, each), :]]
        parts += [total[pl.ds(top + q * 2 * Z + 2 * z, 2), :] for q in range(each // 2)]
        out[z, pl.ds(0, 2 * each), :] = jnp.concatenate(parts).astype(jnp.bfloat16)
        out[z, pl.ds(2 * each, 2 * SMALL), :] = small


def line_kernel(multiplier, chunks, dreduce, dexpand, out):
    total = jnp.sum(chunks[...].astype(jnp.float32), axis=0)
    each, channels = dreduce.shape
    dreduce[...] = total[:each] * multiplier
    for q in range(each // 2):
        part = total[each + 2 * q : each + 2 * q + 2]
        dexpand[:, pl.ds(q * channels, channels)] = part * multiplier
    small = total[2 * each :].astype(jnp.bfloat16)
    out[...] = jnp.broadcast_to(small[None], out.shape)


def small_kernel(chunks, dkernel, dgain, dscale):
    side = dkernel.shape[0]
    for place in range(chunks.shape[0]):
        part = chunks[place].astype(jnp.float32)
        for row in range(SMALL):
            tap = place * SMALL + row
            value = part[row : row + 1]
            if tap < side * side:
                dkernel[tap // side, pl.ds(tap % side, 1), :] = value
            elif tap == side * side:
                dgain[...] = value
            elif tap == side * side + 1:
                dscale[...] = value


VMEM = pl.BlockSpec(memory_space=pltpu.VMEM)
HBM = pl.BlockSpec(memory_space=pltpu.HBM)
SMEM = pl.BlockSpec(memory_space=pltpu.SMEM)
PARAMS = pltpu.CompilerParams(vmem_limit_bytes=20 << 20)
GLUE_PARAMS = pltpu.CompilerParams(vmem_limit_bytes=10 << 20)


def in_hbm(value):
    return pltpu.with_memory_space_constraint(value, pltpu.HBM)


def shifted(value, axes, by):
    count = lax.axis_size(axes)
    pairs = [(i, i + by) for i in range(count) if 0 <= i + by < count]
    return lax.ppermute(value, axes, pairs)


def row_borders(field, reach):
    return shifted(field[-reach:], ROW, 1), shifted(field[:reach], ROW, -1)


def column_borders(field, up, down, reach):
    left, right = (
        jnp.concatenate([part[:, columns] for part in (down, field, up)])
        for columns in (slice(-reach, None), slice(0, reach))
    )
    return up, down, shifted(left, COL, 1), shifted(right, COL, -1)


def exchanged(chunks, axes):
    return lax.all_to_all(chunks, axes, 0, 0, tiled=True)


def shards(features, kernel, gain, w_expand, w_reduce, layer_scale, cotangent):
    height, width, channels = features.shape
    hidden = w_reduce.shape[0]
    side = kernel.shape[0]
    reach = side // 2
    blocks = channels // LANES
    pixels = height * width
    multiplier = 1.0 / math.sqrt(pixels * lax.axis_size(ROW) * lax.axis_size(COL))
    gain_row = gain.reshape(1, channels)
    scale_row = layer_scale.reshape(1, channels)
    core = lax.axis_index("core").reshape(1)
    places = Y * X
    rows = hidden // (Y * CORE * X)
    f32, bf16 = jnp.float32, jnp.bfloat16
    shape = jax.ShapeDtypeStruct
    padded_shape = (blocks, height + side - 1, LEFT + width + 8, LANES)

    each = rows // Z
    up, down = row_borders(features, reach)
    left, right = column_borders(features, up, down, reach)[2:]
    padded, conv, dbranch, taps, params, expand, reduce = pl.pallas_call(
        prepare_kernel,
        name="prepare",
        in_specs=[HBM] + [VMEM] * 2 + [HBM] * 6,
        out_specs=[VMEM] * 7,
        out_shape=[
            shape(padded_shape, f32),
            shape((blocks, pixels, LANES), f32),
            shape((pixels, channels), bf16),
            shape(kernel.shape, f32),
            shape((16, channels), f32),
            shape(w_expand.shape, bf16),
            shape(w_reduce.shape, bf16),
        ],
        scratch_shapes=[
            pltpu.VMEM(features.shape, bf16),
            pltpu.VMEM((1, channels), f32),
            pltpu.VMEM((1, channels), f32),
            pltpu.VMEM(cotangent.shape, bf16),
            pltpu.SemaphoreType.DMA((7,)),
        ],
        compiler_params=PARAMS,
    )(
        in_hbm(features), up, down, in_hbm(kernel), in_hbm(gain_row), in_hbm(scale_row),
        in_hbm(cotangent), in_hbm(w_expand), in_hbm(w_reduce),
    )
    sent, kept, dpre, xhat, rstd, padded, dscale = pl.pallas_call(
        forward_kernel,
        name="forward",
        in_specs=[SMEM] + [VMEM] * 9,
        out_specs=[VMEM] * 7,
        out_shape=[shape((places, 2 * rows, channels), bf16)] * 2
        + [
            shape((pixels, hidden), bf16),
            shape((blocks, pixels, LANES), f32),
            shape((pixels, LANES), f32),
            shape(padded_shape, f32),
            shape((8, channels), f32),
        ],
        scratch_shapes=[
            pltpu.VMEM((pixels, channels), bf16),
            pltpu.VMEM((channels, pixels), bf16),
            pltpu.VMEM((channels, pixels), bf16),
        ],
        input_output_aliases={3: 5},
        compiler_params=PARAMS,
    )(core, left, right, padded, conv, dbranch, taps, params, expand, reduce)

    swap = [(0, 1), (1, 0)]
    came = lax.ppermute(sent, "core", swap)
    dconv, small = pl.pallas_call(
        functools.partial(backward_kernel, multiplier),
        name="backward",
        in_specs=[VMEM] * 7,
        out_specs=[VMEM] * 2,
        out_shape=[
            shape((height, width, channels), bf16),
            shape((places, 2 * SMALL, channels), bf16),
        ],
        scratch_shapes=[
            pltpu.VMEM((blocks, pixels, LANES), f32),
            pltpu.VMEM((places * SMALL, channels), f32),
        ],
        compiler_params=PARAMS,
    )(dpre, expand, xhat, rstd, padded, params, dscale)

    small_came = lax.ppermute(small, "core", swap)
    whole = 2 * rows + 2 * SMALL
    chip = pl.pallas_call(
        merge_kernel,
        name="merge",
        grid=(Y,),
        in_specs=[pl.BlockSpec((X, 2 * rows, channels), lambda i: (i, 0, 0))] * 2
        + [pl.BlockSpec((X, 2 * SMALL, channels), lambda i: (i, 0, 0))] * 2,
        out_specs=pl.BlockSpec((X, whole, channels), lambda i: (i, 0, 0)),
        out_shape=shape((places, whole, channels), bf16),
        compiler_params=GLUE_PARAMS,
    )(kept, came, small, small_came)
    chip, dconv, rows_came = lax.optimization_barrier((chip, dconv, row_borders(dconv, reach)))
    edges = column_borders(dconv, *rows_came, reach)
    grad_features = pl.pallas_call(
        feature_kernel,
        name="features",
        in_specs=[VMEM] * 7,
        out_specs=VMEM,
        out_shape=shape((height, width, channels), bf16),
        scratch_shapes=[pltpu.VMEM(padded_shape, f32)],
        compiler_params=GLUE_PARAMS,
    )(dconv, *edges, kernel, cotangent)
    chunks, grad_features = lax.optimization_barrier((exchanged(chip, ("y", "x")), grad_features))
    chunks = pl.pallas_call(
        plane_kernel,
        name="plane",
        in_specs=[VMEM],
        out_specs=VMEM,
        out_shape=shape((Z, 2 * each + 2 * SMALL, channels), bf16),
        scratch_shapes=[pltpu.VMEM((whole, channels), f32)],
        compiler_params=GLUE_PARAMS,
    )(chunks)
    dreduce, dexpand, chunks = pl.pallas_call(
        functools.partial(line_kernel, multiplier),
        name="line",
        in_specs=[VMEM],
        out_specs=[VMEM] * 3,
        out_shape=[
            shape((each, channels), f32),
            shape((channels * each // hidden, hidden), f32),
            shape((places, 2 * SMALL, channels), bf16),
        ],
        compiler_params=GLUE_PARAMS,
    )(exchanged(chunks, "z"))
    dkernel, dgain, dscale = pl.pallas_call(
        small_kernel,
        name="small",
        in_specs=[VMEM],
        out_specs=[VMEM] * 3,
        out_shape=[shape((side, side, channels), f32)] + [shape((1, channels), f32)] * 2,
        compiler_params=GLUE_PARAMS,
    )(exchanged(chunks, ("y", "x")))
    return (
        grad_features,
        dkernel,
        dgain.reshape(channels),
        dscale.reshape(channels),
        dexpand,
        dreduce,
    )


def solution(mesh):
    pixels = P(ROW, COL, None)
    return jax.shard_map(
        shards,
        mesh=Mesh(mesh.devices.reshape(Y, CORE, X, Z), (*ROW, *COL)),
        in_specs=(pixels, P(), P(), P(), P(), P(), pixels),
        out_specs=(pixels, P(), P(), P(), P((*ROW, *COL), None), P((*ROW, *COL), None)),
        check_vma=False,
    )
```

```python
import functools
import math

import jax
import jax.numpy as jnp
from jax import lax
from jax.experimental import pallas as pl
from jax.experimental.pallas import tpu as pltpu
from jax.sharding import Mesh
from jax.sharding import PartitionSpec as P

Y, CORE, X, Z = 4, 2, 4, 8
ROW, COL = ("y", "core"), ("x", "z")
INV_ROOT_TWO = 1.0 / math.sqrt(2.0)
INV_ROOT_TWO_PI = 1.0 / math.sqrt(2.0 * math.pi)
LANES = 128
ALONG = 128
LEFT = 8
SMALL = 4

NN = (((1,), (0,)), ((), ()))
NT = (((1,), (1,)), ((), ()))
TN = (((0,), (0,)), ((), ()))


def product(left, right, dims):
    return lax.dot_general(left, right, dims, preferred_element_type=jnp.float32)


def fill_own(padded, field, up, down, reach):
    height, width, channels = field.shape
    own = pl.ds(LEFT, width)
    for block in range(channels // LANES):
        lanes = pl.ds(block * LANES, LANES)
        padded[block, pl.ds(0, reach), own, :] = up[:, :, lanes].astype(jnp.float32)
        padded[block, pl.ds(reach, height), own, :] = field[:, :, lanes].astype(jnp.float32)
        padded[block, pl.ds(reach + height, reach), own, :] = down[:, :, lanes].astype(jnp.float32)


def fill_sides(padded, left, right, width, reach):
    rows = padded.shape[1]
    places = ((0, rows - reach, reach), (reach, reach, rows - 2 * reach), (rows - reach, 0, reach))
    for block in range(padded.shape[0]):
        lanes = pl.ds(block * LANES, LANES)
        for side, column in ((left, LEFT - reach), (right, LEFT + width)):
            value = side[:, :, lanes].astype(jnp.float32)
            for source, target, count in places:
                padded[block, pl.ds(target, count), pl.ds(column, reach), :] = value[
                    source : source + count
                ]


def depthwise(padded, taps, block, first_col, height, side, flip):
    reach = side // 2
    totals = [None] * height
    lanes = pl.ds(pl.multiple_of(block * LANES, LANES), LANES)
    for second in range(side):
        columns = pl.ds(LEFT - reach + first_col + second, 8)
        rows = [padded[block, row, columns, :] for row in range(height + side - 1)]
        for first in range(side):
            if flip:
                weight = taps[side - 1 - first, pl.ds(side - 1 - second, 1), lanes]
            else:
                weight = taps[first, pl.ds(second, 1), lanes]
            for row in range(height):
                term = weight * rows[row + first]
                totals[row] = term if totals[row] is None else totals[row] + term
    return totals


def conv_columns(conv, padded, taps, height, width, starts):
    def conv_block(block, _):
        for first_col in starts:
            totals = depthwise(padded, taps, block, first_col, height, taps.shape[0], False)
            for row, total in enumerate(totals):
                conv[block, pl.ds(row * width + first_col, 8), :] = total
        return 0

    lax.fori_loop(0, padded.shape[0], conv_block, 0)


def slot(index, rows, channels):
    across = channels // LANES
    return pl.ds(index // across * rows, rows), pl.ds(index % across * LANES, LANES)


def prepare_kernel(
    field_h, up, down, taps_h, gain_h, scale_h, cotangent_h, expand_h, reduce_h,
    padded, conv, dbranch, taps, rows_out, expand, reduce,
    field, gain, scale, cotangent, sems,
):
    copies = [
        pltpu.make_async_copy(source, target, sems.at[i])
        for i, (source, target) in enumerate(
            (
                (field_h, field),
                (taps_h, taps),
                (gain_h, gain),
                (scale_h, scale),
                (cotangent_h, cotangent),
                (reduce_h, reduce),
                (expand_h, expand),
            )
        )
    ]
    for copy in copies:
        copy.start()
    for copy in copies[:2]:
        copy.wait()
    height, width, channels = field.shape
    fill_own(padded, field, up, down, taps.shape[0] // 2)
    conv_columns(conv, padded, taps, height, width, range(8, width - 8, 8))
    for copy in copies[2:5]:
        copy.wait()
    rows_out[pl.ds(0, 8), :] = jnp.broadcast_to(gain[...], (8, channels))
    rows_out[pl.ds(8, 8), :] = jnp.broadcast_to(scale[...], (8, channels))
    for row in range(height):
        value = cotangent[row].astype(jnp.float32) * scale[...]
        dbranch[pl.ds(row * width, width), :] = value.astype(jnp.bfloat16)
    for copy in copies[5:]:
        copy.wait()


def forward_kernel(
    core_ref, left, right, padded_in, conv, dbranch, taps, rows_in, expand, reduce,
    sent, kept, sent_z, kept_z, dpre_out, xhat_out, rstd_out, padded, dscale_out,
    normed, turned, chosen,
):
    core = core_ref[0]
    del padded_in
    blocks = padded.shape[0]
    side = taps.shape[0]
    height = padded.shape[1] - side + 1
    width = conv.shape[1] // height
    channels = blocks * LANES
    fill_sides(padded, left, right, width, side // 2)
    conv_columns(conv, padded, taps, height, width, (0, width - 8))
    for row in range(height):
        pixels = pl.ds(row * width, width)
        values = [conv[block, pixels, :] for block in range(blocks)]
        mean = jnp.sum(sum(values), axis=-1, keepdims=True) / channels
        values = [value - mean for value in values]
        spread = jnp.sum(sum(value * value for value in values), axis=-1, keepdims=True) / channels
        rstd = lax.rsqrt(spread + 1e-06)
        rstd_out[pixels, :] = jnp.broadcast_to(rstd, (width, LANES))
        for block, value in enumerate(values):
            lanes = pl.ds(block * LANES, LANES)
            xhat = value * rstd
            xhat_out[block, pixels, :] = xhat
            normed[pixels, lanes] = (xhat * rows_in[pl.ds(0, 1), lanes]).astype(jnp.bfloat16)
    turned[...] = normed[...].T
    part = channels // (Y * CORE)
    for y in range(Y):
        for own in range(CORE):
            owner = core if own else 1 - core
            chosen[pl.ds((own * Y + y) * part, part), :] = turned[
                pl.ds(pl.multiple_of((y * CORE + owner) * part, part), part), :
            ]
    dscale_out[...] = jnp.zeros_like(dscale_out)
    step = reduce.shape[0] // (Y * CORE)
    per_z = step // (X * Z)
    part_x = part // X
    wide = channels // step
    kept_blocks = (channels - ALONG) // LANES
    top = per_z * Z * kept_blocks * LANES // channels

    def hidden_block(y, _):
        for own, target, target_z in ((0, sent, sent_z), (1, kept, kept_z)):
            owner = core if own else 1 - core
            chunk = y * CORE + owner
            hidden = pl.ds(pl.multiple_of(chunk * step, step), step)
            pre = product(normed[...], expand[:, hidden], NN)
            dact = product(dbranch[...], reduce[hidden, :], NT)
            half = 0.5 * (1.0 + lax.erf(pre * INV_ROOT_TWO))
            slope = half + pre * jnp.exp(-0.5 * pre * pre) * INV_ROOT_TWO_PI
            act = (pre * half).astype(jnp.bfloat16)
            dpre = (dact * slope).astype(jnp.bfloat16)
            dpre_out[:, hidden] = dpre
            share = product(act, dbranch[...], TN)
            weighed = share * reduce[hidden, :].astype(jnp.float32)
            dscale_out[...] += jnp.sum(weighed.reshape(step // 8, 8, channels), axis=0)
            share = share.astype(jnp.bfloat16)
            for place in range(X * Z):
                x, z = place // Z, place % Z
                mine = share[place * per_z : (place + 1) * per_z]
                for i in range(kept_blocks):
                    slot_rows, slot_lanes = slot(z * kept_blocks + i, per_z, channels)
                    target[y * X + x, slot_rows, slot_lanes] = mine[
                        :, i * LANES : (i + 1) * LANES
                    ]
                target_z[z, y, :, pl.ds(x * ALONG, ALONG)] = mine[:, kept_blocks * LANES :]
            share = product(chosen[...], dpre, NN).astype(jnp.bfloat16)
            rows = pl.ds(pl.multiple_of(top + (chunk // wide) * part_x, part_x), part_x)
            lanes = pl.ds(pl.multiple_of((chunk % wide) * step, step), step)
            for place in range(Y * X):
                for back, goal in ((0, sent), (1, kept)):
                    first = back * Y * part + place * part_x
                    goal[place, rows, lanes] = share[first : first + part_x]
        return 0

    lax.fori_loop(0, Y, hidden_block, 0)


def backward_kernel(
    multiplier, dpre, expand, xhat, rstd, padded, rows, dscale, dconv_out, out, dconv, small
):
    height, width, channels = dconv_out.shape
    blocks = channels // LANES
    side = 7
    dnormed = product(dpre[...], expand[...], NT)
    for block in range(blocks):
        dconv[block] = dnormed[:, block * LANES : (block + 1) * LANES]
    sums = [jnp.zeros((width, LANES), jnp.float32)] * blocks
    for row in range(height):
        pixels = pl.ds(row * width, width)
        grads = [dconv[block, pixels, :] for block in range(blocks)]
        hats = [xhat[block, pixels, :] for block in range(blocks)]
        sums = [total + grad * hat for total, grad, hat in zip(sums, grads, hats)]
        grads = [grad * rows[pl.ds(0, 1), pl.ds(block * LANES, LANES)] for block, grad in enumerate(grads)]
        mean = jnp.sum(sum(grads), axis=-1, keepdims=True) / channels
        slant = sum(grad * hat for grad, hat in zip(grads, hats))
        slant = jnp.sum(slant, axis=-1, keepdims=True) / channels
        for block in range(blocks):
            value = rstd[pixels, :] * (grads[block] - mean - hats[block] * slant)
            dconv[block, pixels, :] = value
            dconv_out[row, :, pl.ds(block * LANES, LANES)] = value.astype(jnp.bfloat16)
    taps = side * side
    unused = small.shape[0] - taps - 2
    small[pl.ds(taps + 2, unused), :] = jnp.zeros((unused, channels), jnp.float32)
    for block in range(blocks):
        lanes = pl.ds(block * LANES, LANES)
        total = jnp.sum(sums[block], axis=0, keepdims=True)
        small[pl.ds(taps, 1), lanes] = total * multiplier
        total = jnp.sum(dscale[:, lanes], axis=0, keepdims=True)
        small[pl.ds(taps + 1, 1), lanes] = total / rows[pl.ds(8, 1), lanes] * multiplier

    def tap_block(block, _):
        lanes = pl.ds(pl.multiple_of(block * LANES, LANES), LANES)
        for second in range(side):
            totals = [jnp.zeros((8, LANES), jnp.float32)] * side
            for first_col in range(0, width, 8):
                grads = [
                    dconv[block, pl.ds(row * width + first_col, 8), :] for row in range(height)
                ]
                columns = pl.ds(LEFT - side // 2 + first_col + second, 8)
                for row in range(height + side - 1):
                    value = padded[block, row, columns, :]
                    for first in range(max(0, row - height + 1), min(side, row + 1)):
                        totals[first] = totals[first] + grads[row - first] * value
            for first, total in enumerate(totals):
                total = jnp.sum(total, axis=0, keepdims=True) * multiplier
                small[pl.ds(first * side + second, 1), lanes] = total
        return 0

    lax.fori_loop(0, blocks, tap_block, 0)
    for place in range(out.shape[0]):
        part = small[pl.ds(place * SMALL, SMALL), :]
        out[place] = jnp.concatenate([part, jnp.zeros_like(part)]).astype(jnp.bfloat16)


def feature_kernel(field, up, down, left, right, taps, cotangent, out, padded):
    height, width, channels = field.shape
    side = 7
    fill_own(padded, field, up, down, side // 2)
    fill_sides(padded, left, right, width, side // 2)
    for block in range(channels // LANES):
        lanes = pl.ds(block * LANES, LANES)
        for first_col in range(0, width, 8):
            columns = pl.ds(first_col, 8)
            for row, total in enumerate(
                depthwise(padded, taps, block, first_col, height, side, True)
            ):
                total = total + cotangent[row, columns, lanes].astype(jnp.float32)
                out[row, columns, lanes] = total.astype(jnp.bfloat16)


def added(left, right):
    return (left.astype(jnp.float32) + right.astype(jnp.float32)).astype(jnp.bfloat16)


def merge_kernel(kept, came, small, small_came, out):
    rows = kept.shape[1]
    out[:, pl.ds(0, rows), :] = added(kept[...], came[...])
    out[:, pl.ds(rows, small.shape[1]), :] = added(small[...], small_came[...])


def join_kernel(z_ref, kept, came, *outs):
    for step, out in enumerate(outs):
        z = lax.rem(z_ref[0] + step, Z)
        out[...] = added(kept[z], came[z])


def plane_kernel(chunks, out, total):
    total[...] = jnp.sum(chunks[...].astype(jnp.float32), axis=0)
    each = (out.shape[1] - 2 * SMALL) // 2
    channels = out.shape[2]
    top = total.shape[0] - 2 * SMALL - each * Z
    blocks = (channels - ALONG) // LANES
    small = total[pl.ds(total.shape[0] - 2 * SMALL, 2 * SMALL), :].astype(jnp.bfloat16)
    for z in range(Z):
        parts = [total[slot(z * blocks + i, each, channels)] for i in range(blocks)]
        parts.append(jnp.zeros((each, ALONG), jnp.float32))
        out[z, pl.ds(0, each), :] = jnp.concatenate(parts, axis=1).astype(jnp.bfloat16)
        parts = [total[pl.ds(top + q * 2 * Z + 2 * z, 2), :] for q in range(each // 2)]
        out[z, pl.ds(each, each), :] = jnp.concatenate(parts).astype(jnp.bfloat16)
        out[z, pl.ds(2 * each, 2 * SMALL), :] = small


def line_kernel(multiplier, chunks, *refs):
    *came, part_out, dexpand, out = refs
    total = jnp.sum(chunks[...].astype(jnp.float32), axis=0)
    each, channels = part_out.shape
    part_out[...] = total[:each] * multiplier
    for q in range(each // 2):
        part = total[each + 2 * q : each + 2 * q + 2]
        dexpand[:, pl.ds(q * channels, channels)] = part * multiplier
    small = total[2 * each : 2 * each + SMALL]
    half = channels // 2
    small = jnp.concatenate([small[:, :half], small[:, half:]]).astype(jnp.bfloat16)
    line = sum(ref[...].astype(jnp.float32) for ref in came).astype(jnp.bfloat16)
    for place in range(out.shape[0]):
        y, x = place // X, place % X
        out[place, :, pl.ds(0, half)] = small
        out[place, :, pl.ds(half, ALONG)] = line[y][:, x * ALONG : (x + 1) * ALONG]
        out[place, :, pl.ds(half + ALONG, half - ALONG)] = jnp.zeros(
            (each, half - ALONG), jnp.bfloat16
        )


def last_kernel(multiplier, chunks, part, dreduce, dkernel, dgain, dscale):
    channels = dreduce.shape[1]
    half = channels // 2
    own = channels - ALONG
    dreduce[:, pl.ds(0, own)] = part[:, pl.ds(0, own)]
    total = jnp.sum(chunks[:, :, pl.ds(half, ALONG)].astype(jnp.float32), axis=0)
    dreduce[:, pl.ds(own, ALONG)] = total * multiplier
    side = dkernel.shape[0]
    for place in range(chunks.shape[0]):
        small = chunks[place, :, pl.ds(0, half)].astype(jnp.float32)
        for row in range(SMALL):
            tap = place * SMALL + row
            for i in range(2):
                lanes = pl.ds(i * half, half)
                value = small[i * SMALL + row : i * SMALL + row + 1]
                if tap < side * side:
                    dkernel[tap // side, pl.ds(tap % side, 1), lanes] = value
                elif tap == side * side:
                    dgain[:, lanes] = value
                elif tap == side * side + 1:
                    dscale[:, lanes] = value


VMEM = pl.BlockSpec(memory_space=pltpu.VMEM)
HBM = pl.BlockSpec(memory_space=pltpu.HBM)
SMEM = pl.BlockSpec(memory_space=pltpu.SMEM)
PARAMS = pltpu.CompilerParams(vmem_limit_bytes=20 << 20)
GLUE_PARAMS = pltpu.CompilerParams(vmem_limit_bytes=10 << 20)


def in_hbm(value):
    return pltpu.with_memory_space_constraint(value, pltpu.HBM)


def shifted(value, axes, by):
    count = lax.axis_size(axes)
    pairs = [(i, i + by) for i in range(count) if 0 <= i + by < count]
    return lax.ppermute(value, axes, pairs)


def row_borders(field, reach):
    return shifted(field[-reach:], ROW, 1), shifted(field[:reach], ROW, -1)


def column_borders(field, up, down, reach):
    left, right = (
        jnp.concatenate([part[:, columns] for part in (down, field, up)])
        for columns in (slice(-reach, None), slice(0, reach))
    )
    return up, down, shifted(left, COL, 1), shifted(right, COL, -1)


def exchanged(chunks, axes):
    return lax.all_to_all(chunks, axes, 0, 0, tiled=True)


def shards(features, kernel, gain, w_expand, w_reduce, layer_scale, cotangent):
    height, width, channels = features.shape
    hidden = w_reduce.shape[0]
    side = kernel.shape[0]
    reach = side // 2
    blocks = channels // LANES
    pixels = height * width
    multiplier = 1.0 / math.sqrt(pixels * lax.axis_size(ROW) * lax.axis_size(COL))
    gain_row = gain.reshape(1, channels)
    scale_row = layer_scale.reshape(1, channels)
    core = lax.axis_index("core").reshape(1)
    places = Y * X
    rows = hidden // (Y * CORE * X)
    f32, bf16 = jnp.float32, jnp.bfloat16
    shape = jax.ShapeDtypeStruct
    padded_shape = (blocks, height + side - 1, LEFT + width + 8, LANES)

    each = rows // Z
    top = rows * (channels - ALONG) // channels
    up, down = row_borders(features, reach)
    left, right = column_borders(features, up, down, reach)[2:]
    padded, conv, dbranch, taps, params, expand, reduce = pl.pallas_call(
        prepare_kernel,
        name="prepare",
        in_specs=[HBM] + [VMEM] * 2 + [HBM] * 6,
        out_specs=[VMEM] * 7,
        out_shape=[
            shape(padded_shape, f32),
            shape((blocks, pixels, LANES), f32),
            shape((pixels, channels), bf16),
            shape(kernel.shape, f32),
            shape((16, channels), f32),
            shape(w_expand.shape, bf16),
            shape(w_reduce.shape, bf16),
        ],
        scratch_shapes=[
            pltpu.VMEM(features.shape, bf16),
            pltpu.VMEM((1, channels), f32),
            pltpu.VMEM((1, channels), f32),
            pltpu.VMEM(cotangent.shape, bf16),
            pltpu.SemaphoreType.DMA((7,)),
        ],
        compiler_params=PARAMS,
    )(
        in_hbm(features), up, down, in_hbm(kernel), in_hbm(gain_row), in_hbm(scale_row),
        in_hbm(cotangent), in_hbm(w_expand), in_hbm(w_reduce),
    )
    sent, kept, sent_z, kept_z, dpre, xhat, rstd, padded, dscale = pl.pallas_call(
        forward_kernel,
        name="forward",
        in_specs=[SMEM] + [VMEM] * 9,
        out_specs=[VMEM] * 9,
        out_shape=[shape((places, top + rows, channels), bf16)] * 2
        + [shape((Z, Y, each, X * ALONG), bf16)] * 2
        + [
            shape((pixels, hidden), bf16),
            shape((blocks, pixels, LANES), f32),
            shape((pixels, LANES), f32),
            shape(padded_shape, f32),
            shape((8, channels), f32),
        ],
        scratch_shapes=[
            pltpu.VMEM((pixels, channels), bf16),
            pltpu.VMEM((channels, pixels), bf16),
            pltpu.VMEM((channels, pixels), bf16),
        ],
        input_output_aliases={3: 7},
        compiler_params=PARAMS,
    )(core, left, right, padded, conv, dbranch, taps, params, expand, reduce)

    swap = [(0, 1), (1, 0)]
    came = lax.ppermute(sent, "core", swap)
    came_z = lax.ppermute(sent_z, "core", swap)
    dconv, small = pl.pallas_call(
        functools.partial(backward_kernel, multiplier),
        name="backward",
        in_specs=[VMEM] * 7,
        out_specs=[VMEM] * 2,
        out_shape=[
            shape((height, width, channels), bf16),
            shape((places, 2 * SMALL, channels), bf16),
        ],
        scratch_shapes=[
            pltpu.VMEM((blocks, pixels, LANES), f32),
            pltpu.VMEM((places * SMALL, channels), f32),
        ],
        compiler_params=PARAMS,
    )(dpre, expand, xhat, rstd, padded, params, dscale)

    small_came = lax.ppermute(small, "core", swap)
    whole = top + rows + 2 * SMALL
    chip = pl.pallas_call(
        merge_kernel,
        name="merge",
        grid=(Y,),
        in_specs=[pl.BlockSpec((X, top + rows, channels), lambda i: (i, 0, 0))] * 2
        + [pl.BlockSpec((X, 2 * SMALL, channels), lambda i: (i, 0, 0))] * 2,
        out_specs=pl.BlockSpec((X, whole, channels), lambda i: (i, 0, 0)),
        out_shape=shape((places, whole, channels), bf16),
        compiler_params=GLUE_PARAMS,
    )(kept, came, small, small_came)
    chip, dconv, came_z, rows_came = lax.optimization_barrier(
        (chip, dconv, came_z, row_borders(dconv, reach))
    )
    line = pl.pallas_call(
        join_kernel,
        name="join",
        in_specs=[SMEM] + [VMEM] * 2,
        out_specs=[VMEM] * Z,
        out_shape=[shape(kept_z.shape[1:], bf16)] * Z,
        compiler_params=GLUE_PARAMS,
    )(lax.axis_index("z").reshape(1), kept_z, came_z)
    line = [
        part if step == 0 else lax.ppermute(part, "z", [(i, (i + step) % Z) for i in range(Z)])
        for step, part in enumerate(line)
    ]
    chunks, edges, line = lax.optimization_barrier(
        (exchanged(chip, ("y", "x")), column_borders(dconv, *rows_came, reach), line)
    )
    chunks = pl.pallas_call(
        plane_kernel,
        name="plane",
        in_specs=[VMEM],
        out_specs=VMEM,
        out_shape=shape((Z, 2 * each + 2 * SMALL, channels), bf16),
        scratch_shapes=[pltpu.VMEM((whole, channels), f32)],
        compiler_params=GLUE_PARAMS,
    )(chunks)
    part, dexpand, chunks = pl.pallas_call(
        functools.partial(line_kernel, multiplier),
        name="line",
        in_specs=[VMEM] * (1 + Z),
        out_specs=[VMEM] * 3,
        out_shape=[
            shape((each, channels), f32),
            shape((channels * each // hidden, hidden), f32),
            shape((places, each, channels), bf16),
        ],
        compiler_params=GLUE_PARAMS,
    )(exchanged(chunks, "z"), *line)
    dreduce, dkernel, dgain, dscale = pl.pallas_call(
        functools.partial(last_kernel, multiplier),
        name="last",
        in_specs=[VMEM] * 2,
        out_specs=[VMEM] * 4,
        out_shape=[shape((each, channels), f32), shape((side, side, channels), f32)]
        + [shape((1, channels), f32)] * 2,
        compiler_params=GLUE_PARAMS,
    )(exchanged(chunks, ("y", "x")), part)
    grad_features = pl.pallas_call(
        feature_kernel,
        name="features",
        in_specs=[VMEM] * 7,
        out_specs=VMEM,
        out_shape=shape((height, width, channels), bf16),
        scratch_shapes=[pltpu.VMEM(padded_shape, f32)],
        compiler_params=GLUE_PARAMS,
    )(dconv, *edges, kernel, cotangent)
    return (
        grad_features,
        dkernel,
        dgain.reshape(channels),
        dscale.reshape(channels),
        dexpand,
        dreduce,
    )


def solution(mesh):
    pixels = P(ROW, COL, None)
    return jax.shard_map(
        shards,
        mesh=Mesh(mesh.devices.reshape(Y, CORE, X, Z), (*ROW, *COL)),
        in_specs=(pixels, P(), P(), P(), P(), P(), pixels),
        out_specs=(pixels, P(), P(), P(), P((*ROW, *COL), None), P((*ROW, *COL), None)),
        check_vma=False,
    )
```

```python
import functools
import math

import jax
import jax.numpy as jnp
from jax import lax
from jax.experimental import pallas as pl
from jax.experimental.pallas import tpu as pltpu
from jax.sharding import Mesh
from jax.sharding import PartitionSpec as P

Y, CORE, X, Z = 4, 2, 4, 8
ROW, COL = ("y", "core"), ("x", "z")
INV_ROOT_TWO = 1.0 / math.sqrt(2.0)
INV_ROOT_TWO_PI = 1.0 / math.sqrt(2.0 * math.pi)
LANES = 128
ALONG = 128
LEFT = 8
SMALL = 4

NN = (((1,), (0,)), ((), ()))
NT = (((1,), (1,)), ((), ()))
TN = (((0,), (0,)), ((), ()))


def product(left, right, dims):
    return lax.dot_general(left, right, dims, preferred_element_type=jnp.float32)


def in_order(first, inner, outer):
    return jnp.where(first, outer, inner), jnp.where(first, inner, outer)


def fill_own(padded, field, inner, outer, first_row, reach):
    height, width, channels = field.shape
    own = pl.ds(LEFT, width)
    for block in range(channels // LANES):
        lanes = pl.ds(block * LANES, LANES)
        up, down = in_order(
            first_row,
            inner[:, :, lanes].astype(jnp.float32),
            outer[:, :, lanes].astype(jnp.float32),
        )
        padded[block, pl.ds(0, reach), own, :] = up
        padded[block, pl.ds(reach, height), own, :] = field[:, :, lanes].astype(jnp.float32)
        padded[block, pl.ds(reach + height, reach), own, :] = down


def fill_sides(padded, inner, outer, first_row, first_column, width, reach):
    rows = padded.shape[1]
    for block in range(padded.shape[0]):
        lanes = pl.ds(block * LANES, LANES)
        sides = in_order(
            first_column,
            inner[:, :, lanes].astype(jnp.float32),
            outer[:, :, lanes].astype(jnp.float32),
        )
        for value, column in zip(sides, (LEFT - reach, LEFT + width)):
            columns = pl.ds(column, reach)
            up, down = in_order(first_row, value[:reach], value[rows - reach :])
            padded[block, pl.ds(0, reach), columns, :] = up
            padded[block, pl.ds(reach, rows - 2 * reach), columns, :] = value[reach : rows - reach]
            padded[block, pl.ds(rows - reach, reach), columns, :] = down


def depthwise(padded, taps, block, first_col, height, side, flip):
    reach = side // 2
    totals = [None] * height
    lanes = pl.ds(pl.multiple_of(block * LANES, LANES), LANES)
    for second in range(side):
        columns = pl.ds(LEFT - reach + first_col + second, 8)
        rows = [padded[block, row, columns, :] for row in range(height + side - 1)]
        for first in range(side):
            if flip:
                weight = taps[side - 1 - first, pl.ds(side - 1 - second, 1), lanes]
            else:
                weight = taps[first, pl.ds(second, 1), lanes]
            for row in range(height):
                term = weight * rows[row + first]
                totals[row] = term if totals[row] is None else totals[row] + term
    return totals


def conv_columns(conv, padded, taps, height, width, starts):
    def conv_block(block, _):
        for first_col in starts:
            totals = depthwise(padded, taps, block, first_col, height, taps.shape[0], False)
            for row, total in enumerate(totals):
                conv[block, pl.ds(row * width + first_col, 8), :] = total
        return 0

    lax.fori_loop(0, padded.shape[0], conv_block, 0)


def slot(index, rows, channels):
    across = channels // LANES
    return pl.ds(index // across * rows, rows), pl.ds(index % across * LANES, LANES)


def prepare_kernel(
    place_ref, field_h, inner, outer, taps_h, gain_h, scale_h, cotangent_h, expand_h, reduce_h,
    padded, conv, dbranch, taps, rows_out, expand, reduce,
    field, gain, scale, cotangent, sems,
):
    copies = [
        pltpu.make_async_copy(source, target, sems.at[i])
        for i, (source, target) in enumerate(
            (
                (field_h, field),
                (taps_h, taps),
                (gain_h, gain),
                (scale_h, scale),
                (cotangent_h, cotangent),
                (reduce_h, reduce),
                (expand_h, expand),
            )
        )
    ]
    for copy in copies:
        copy.start()
    for copy in copies[:2]:
        copy.wait()
    height, width, channels = field.shape
    fill_own(padded, field, inner, outer, place_ref[0] == 0, taps.shape[0] // 2)
    conv_columns(conv, padded, taps, height, width, range(8, width - 8, 8))
    for copy in copies[2:5]:
        copy.wait()
    rows_out[pl.ds(0, 8), :] = jnp.broadcast_to(gain[...], (8, channels))
    rows_out[pl.ds(8, 8), :] = jnp.broadcast_to(scale[...], (8, channels))
    for row in range(height):
        value = cotangent[row].astype(jnp.float32) * scale[...]
        dbranch[pl.ds(row * width, width), :] = value.astype(jnp.bfloat16)
    for copy in copies[5:]:
        copy.wait()


def forward_kernel(
    place_ref, inner, outer, padded_in, conv, dbranch, taps, rows_in, expand, reduce,
    sent, kept, sent_z, kept_z, dpre_out, xhat_out, rstd_out, padded, dscale_out,
    normed, turned, chosen,
):
    core = place_ref[0]
    first_column = lax.rem(place_ref[1], 2) == 0
    del padded_in
    blocks = padded.shape[0]
    side = taps.shape[0]
    height = padded.shape[1] - side + 1
    width = conv.shape[1] // height
    channels = blocks * LANES
    fill_sides(padded, inner, outer, core == 0, first_column, width, side // 2)
    conv_columns(conv, padded, taps, height, width, (0, width - 8))
    for row in range(height):
        pixels = pl.ds(row * width, width)
        values = [conv[block, pixels, :] for block in range(blocks)]
        mean = jnp.sum(sum(values), axis=-1, keepdims=True) / channels
        values = [value - mean for value in values]
        spread = jnp.sum(sum(value * value for value in values), axis=-1, keepdims=True) / channels
        rstd = lax.rsqrt(spread + 1e-06)
        rstd_out[pixels, :] = jnp.broadcast_to(rstd, (width, LANES))
        for block, value in enumerate(values):
            lanes = pl.ds(block * LANES, LANES)
            xhat = value * rstd
            xhat_out[block, pixels, :] = xhat
            normed[pixels, lanes] = (xhat * rows_in[pl.ds(0, 1), lanes]).astype(jnp.bfloat16)
    turned[...] = normed[...].T
    part = channels // (Y * CORE)
    for y in range(Y):
        for own in range(CORE):
            owner = core if own else 1 - core
            chosen[pl.ds((own * Y + y) * part, part), :] = turned[
                pl.ds(pl.multiple_of((y * CORE + owner) * part, part), part), :
            ]
    dscale_out[...] = jnp.zeros_like(dscale_out)
    step = reduce.shape[0] // (Y * CORE)
    per_z = step // (X * Z)
    part_x = part // X
    wide = channels // step
    kept_blocks = (channels - ALONG) // LANES
    top = per_z * Z * kept_blocks * LANES // channels

    def hidden_block(y, _):
        for own, target, target_z in ((0, sent, sent_z), (1, kept, kept_z)):
            owner = core if own else 1 - core
            chunk = y * CORE + owner
            hidden = pl.ds(pl.multiple_of(chunk * step, step), step)
            pre = product(normed[...], expand[:, hidden], NN)
            dact = product(dbranch[...], reduce[hidden, :], NT)
            half = 0.5 * (1.0 + lax.erf(pre * INV_ROOT_TWO))
            slope = half + pre * jnp.exp(-0.5 * pre * pre) * INV_ROOT_TWO_PI
            act = (pre * half).astype(jnp.bfloat16)
            dpre = (dact * slope).astype(jnp.bfloat16)
            dpre_out[:, hidden] = dpre
            share = product(act, dbranch[...], TN)
            weighed = share * reduce[hidden, :].astype(jnp.float32)
            dscale_out[...] += jnp.sum(weighed.reshape(step // 8, 8, channels), axis=0)
            share = share.astype(jnp.bfloat16)
            for place in range(X * Z):
                x, z = place // Z, place % Z
                mine = share[place * per_z : (place + 1) * per_z]
                for i in range(kept_blocks):
                    slot_rows, slot_lanes = slot(z * kept_blocks + i, per_z, channels)
                    target[y * X + x, slot_rows, slot_lanes] = mine[
                        :, i * LANES : (i + 1) * LANES
                    ]
                target_z[z, y, :, pl.ds(x * ALONG, ALONG)] = mine[:, kept_blocks * LANES :]
            share = product(chosen[...], dpre, NN).astype(jnp.bfloat16)
            rows = pl.ds(pl.multiple_of(top + (chunk // wide) * part_x, part_x), part_x)
            lanes = pl.ds(pl.multiple_of((chunk % wide) * step, step), step)
            for place in range(Y * X):
                for back, goal in ((0, sent), (1, kept)):
                    first = back * Y * part + place * part_x
                    goal[place, rows, lanes] = share[first : first + part_x]
        return 0

    lax.fori_loop(0, Y, hidden_block, 0)


def backward_kernel(
    multiplier, dpre, expand, xhat, rstd, padded, rows, dscale, dconv_out, out, dconv, small
):
    height, width, channels = dconv_out.shape
    blocks = channels // LANES
    side = 7
    dnormed = product(dpre[...], expand[...], NT)
    for block in range(blocks):
        dconv[block] = dnormed[:, block * LANES : (block + 1) * LANES]
    sums = [jnp.zeros((width, LANES), jnp.float32)] * blocks
    for row in range(height):
        pixels = pl.ds(row * width, width)
        grads = [dconv[block, pixels, :] for block in range(blocks)]
        hats = [xhat[block, pixels, :] for block in range(blocks)]
        sums = [total + grad * hat for total, grad, hat in zip(sums, grads, hats)]
        grads = [grad * rows[pl.ds(0, 1), pl.ds(block * LANES, LANES)] for block, grad in enumerate(grads)]
        mean = jnp.sum(sum(grads), axis=-1, keepdims=True) / channels
        slant = sum(grad * hat for grad, hat in zip(grads, hats))
        slant = jnp.sum(slant, axis=-1, keepdims=True) / channels
        for block in range(blocks):
            value = rstd[pixels, :] * (grads[block] - mean - hats[block] * slant)
            dconv[block, pixels, :] = value
            dconv_out[row, :, pl.ds(block * LANES, LANES)] = value.astype(jnp.bfloat16)
    taps = side * side
    unused = small.shape[0] - taps - 2
    small[pl.ds(taps + 2, unused), :] = jnp.zeros((unused, channels), jnp.float32)
    for block in range(blocks):
        lanes = pl.ds(block * LANES, LANES)
        total = jnp.sum(sums[block], axis=0, keepdims=True)
        small[pl.ds(taps, 1), lanes] = total * multiplier
        total = jnp.sum(dscale[:, lanes], axis=0, keepdims=True)
        small[pl.ds(taps + 1, 1), lanes] = total / rows[pl.ds(8, 1), lanes] * multiplier

    def tap_block(block, _):
        lanes = pl.ds(pl.multiple_of(block * LANES, LANES), LANES)
        for second in range(side):
            totals = [jnp.zeros((8, LANES), jnp.float32)] * side
            for first_col in range(0, width, 8):
                grads = [
                    dconv[block, pl.ds(row * width + first_col, 8), :] for row in range(height)
                ]
                columns = pl.ds(LEFT - side // 2 + first_col + second, 8)
                for row in range(height + side - 1):
                    value = padded[block, row, columns, :]
                    for first in range(max(0, row - height + 1), min(side, row + 1)):
                        totals[first] = totals[first] + grads[row - first] * value
            for first, total in enumerate(totals):
                total = jnp.sum(total, axis=0, keepdims=True) * multiplier
                small[pl.ds(first * side + second, 1), lanes] = total
        return 0

    lax.fori_loop(0, blocks, tap_block, 0)
    for place in range(out.shape[0]):
        part = small[pl.ds(place * SMALL, SMALL), :]
        out[place] = jnp.concatenate([part, jnp.zeros_like(part)]).astype(jnp.bfloat16)


def feature_kernel(
    place_ref, field, row_inner, row_outer, inner, outer, taps, cotangent, out, padded
):
    height, width, channels = field.shape
    side = 7
    first_row = place_ref[0] == 0
    first_column = lax.rem(place_ref[1], 2) == 0
    fill_own(padded, field, row_inner, row_outer, first_row, side // 2)
    fill_sides(padded, inner, outer, first_row, first_column, width, side // 2)
    for block in range(channels // LANES):
        lanes = pl.ds(block * LANES, LANES)
        for first_col in range(0, width, 8):
            columns = pl.ds(first_col, 8)
            for row, total in enumerate(
                depthwise(padded, taps, block, first_col, height, side, True)
            ):
                total = total + cotangent[row, columns, lanes].astype(jnp.float32)
                out[row, columns, lanes] = total.astype(jnp.bfloat16)


def added(left, right):
    return (left.astype(jnp.float32) + right.astype(jnp.float32)).astype(jnp.bfloat16)


def merge_kernel(kept, came, small, small_came, out):
    rows = kept.shape[1]
    out[:, pl.ds(0, rows), :] = added(kept[...], came[...])
    out[:, pl.ds(rows, small.shape[1]), :] = added(small[...], small_came[...])


def join_kernel(place_ref, kept, came, *outs):
    for step, out in enumerate(outs):
        z = lax.rem(place_ref[1] + step, Z)
        out[...] = added(kept[z], came[z])


def plane_kernel(chunks, out, total):
    total[...] = jnp.sum(chunks[...].astype(jnp.float32), axis=0)
    each = (out.shape[1] - 2 * SMALL) // 2
    channels = out.shape[2]
    top = total.shape[0] - 2 * SMALL - each * Z
    blocks = (channels - ALONG) // LANES
    small = total[pl.ds(total.shape[0] - 2 * SMALL, 2 * SMALL), :].astype(jnp.bfloat16)
    for z in range(Z):
        parts = [total[slot(z * blocks + i, each, channels)] for i in range(blocks)]
        parts.append(jnp.zeros((each, ALONG), jnp.float32))
        out[z, pl.ds(0, each), :] = jnp.concatenate(parts, axis=1).astype(jnp.bfloat16)
        parts = [total[pl.ds(top + q * 2 * Z + 2 * z, 2), :] for q in range(each // 2)]
        out[z, pl.ds(each, each), :] = jnp.concatenate(parts).astype(jnp.bfloat16)
        out[z, pl.ds(2 * each, 2 * SMALL), :] = small


def line_kernel(multiplier, chunks, *refs):
    *came, part_out, dexpand, out = refs
    total = jnp.sum(chunks[...].astype(jnp.float32), axis=0)
    each, channels = part_out.shape
    part_out[...] = total[:each] * multiplier
    for q in range(each // 2):
        part = total[each + 2 * q : each + 2 * q + 2]
        dexpand[:, pl.ds(q * channels, channels)] = part * multiplier
    small = total[2 * each : 2 * each + SMALL]
    half = channels // 2
    small = jnp.concatenate([small[:, :half], small[:, half:]]).astype(jnp.bfloat16)
    line = sum(ref[...].astype(jnp.float32) for ref in came).astype(jnp.bfloat16)
    for place in range(out.shape[0]):
        y, x = place // X, place % X
        out[place, :, pl.ds(0, half)] = small
        out[place, :, pl.ds(half, ALONG)] = line[y][:, x * ALONG : (x + 1) * ALONG]
        out[place, :, pl.ds(half + ALONG, half - ALONG)] = jnp.zeros(
            (each, half - ALONG), jnp.bfloat16
        )


def last_kernel(multiplier, chunks, part, dreduce, dkernel, dgain, dscale):
    channels = dreduce.shape[1]
    half = channels // 2
    own = channels - ALONG
    dreduce[:, pl.ds(0, own)] = part[:, pl.ds(0, own)]
    total = jnp.sum(chunks[:, :, pl.ds(half, ALONG)].astype(jnp.float32), axis=0)
    dreduce[:, pl.ds(own, ALONG)] = total * multiplier
    side = dkernel.shape[0]
    for place in range(chunks.shape[0]):
        small = chunks[place, :, pl.ds(0, half)].astype(jnp.float32)
        for row in range(SMALL):
            tap = place * SMALL + row
            for i in range(2):
                lanes = pl.ds(i * half, half)
                value = small[i * SMALL + row : i * SMALL + row + 1]
                if tap < side * side:
                    dkernel[tap // side, pl.ds(tap % side, 1), lanes] = value
                elif tap == side * side:
                    dgain[:, lanes] = value
                elif tap == side * side + 1:
                    dscale[:, lanes] = value


VMEM = pl.BlockSpec(memory_space=pltpu.VMEM)
HBM = pl.BlockSpec(memory_space=pltpu.HBM)
SMEM = pl.BlockSpec(memory_space=pltpu.SMEM)
PARAMS = pltpu.CompilerParams(vmem_limit_bytes=20 << 20)
GLUE_PARAMS = pltpu.CompilerParams(vmem_limit_bytes=10 << 20)


def in_hbm(value):
    return pltpu.with_memory_space_constraint(value, pltpu.HBM)


def swapped(low, high, axes, first):
    count = lax.axis_size(axes)
    inner = [(i, i ^ 1) for i in range(count)]
    outer = [(i, i + 1 if i % 2 else i - 1) for i in range(1, count - 1)]
    return (
        lax.ppermute(jnp.where(first, high, low), axes, inner),
        lax.ppermute(jnp.where(first, low, high), axes, outer),
    )


def row_borders(field, reach):
    return swapped(field[:reach], field[-reach:], ROW, lax.axis_index("core") == 0)


def column_borders(field, inner, outer, reach):
    low, high = (
        jnp.concatenate([part[:, columns] for part in (inner, field, outer)])
        for columns in (slice(0, reach), slice(-reach, None))
    )
    return inner, outer, *swapped(low, high, COL, lax.axis_index("z") % 2 == 0)


def exchanged(chunks, axes):
    return lax.all_to_all(chunks, axes, 0, 0, tiled=True)


def shards(features, kernel, gain, w_expand, w_reduce, layer_scale, cotangent):
    height, width, channels = features.shape
    hidden = w_reduce.shape[0]
    side = kernel.shape[0]
    reach = side // 2
    blocks = channels // LANES
    pixels = height * width
    multiplier = 1.0 / math.sqrt(pixels * lax.axis_size(ROW) * lax.axis_size(COL))
    gain_row = gain.reshape(1, channels)
    scale_row = layer_scale.reshape(1, channels)
    place = jnp.stack([lax.axis_index("core"), lax.axis_index("z")])
    places = Y * X
    rows = hidden // (Y * CORE * X)
    f32, bf16 = jnp.float32, jnp.bfloat16
    shape = jax.ShapeDtypeStruct
    padded_shape = (blocks, height + side - 1, LEFT + width + 8, LANES)

    each = rows // Z
    top = rows * (channels - ALONG) // channels
    row_inner, row_outer, inner, outer = column_borders(
        features, *row_borders(features, reach), reach
    )
    padded, conv, dbranch, taps, params, expand, reduce = pl.pallas_call(
        prepare_kernel,
        name="prepare",
        in_specs=[SMEM, HBM] + [VMEM] * 2 + [HBM] * 6,
        out_specs=[VMEM] * 7,
        out_shape=[
            shape(padded_shape, f32),
            shape((blocks, pixels, LANES), f32),
            shape((pixels, channels), bf16),
            shape(kernel.shape, f32),
            shape((16, channels), f32),
            shape(w_expand.shape, bf16),
            shape(w_reduce.shape, bf16),
        ],
        scratch_shapes=[
            pltpu.VMEM(features.shape, bf16),
            pltpu.VMEM((1, channels), f32),
            pltpu.VMEM((1, channels), f32),
            pltpu.VMEM(cotangent.shape, bf16),
            pltpu.SemaphoreType.DMA((7,)),
        ],
        compiler_params=PARAMS,
    )(
        place, in_hbm(features), row_inner, row_outer, in_hbm(kernel), in_hbm(gain_row),
        in_hbm(scale_row), in_hbm(cotangent), in_hbm(w_expand), in_hbm(w_reduce),
    )
    sent, kept, sent_z, kept_z, dpre, xhat, rstd, padded, dscale = pl.pallas_call(
        forward_kernel,
        name="forward",
        in_specs=[SMEM] + [VMEM] * 9,
        out_specs=[VMEM] * 9,
        out_shape=[shape((places, top + rows, channels), bf16)] * 2
        + [shape((Z, Y, each, X * ALONG), bf16)] * 2
        + [
            shape((pixels, hidden), bf16),
            shape((blocks, pixels, LANES), f32),
            shape((pixels, LANES), f32),
            shape(padded_shape, f32),
            shape((8, channels), f32),
        ],
        scratch_shapes=[
            pltpu.VMEM((pixels, channels), bf16),
            pltpu.VMEM((channels, pixels), bf16),
            pltpu.VMEM((channels, pixels), bf16),
        ],
        input_output_aliases={3: 7},
        compiler_params=PARAMS,
    )(place, inner, outer, padded, conv, dbranch, taps, params, expand, reduce)

    swap = [(0, 1), (1, 0)]
    came = lax.ppermute(sent, "core", swap)
    came_z = lax.ppermute(sent_z, "core", swap)
    dconv, small = pl.pallas_call(
        functools.partial(backward_kernel, multiplier),
        name="backward",
        in_specs=[VMEM] * 7,
        out_specs=[VMEM] * 2,
        out_shape=[
            shape((height, width, channels), bf16),
            shape((places, 2 * SMALL, channels), bf16),
        ],
        scratch_shapes=[
            pltpu.VMEM((blocks, pixels, LANES), f32),
            pltpu.VMEM((places * SMALL, channels), f32),
        ],
        compiler_params=PARAMS,
    )(dpre, expand, xhat, rstd, padded, params, dscale)

    small_came = lax.ppermute(small, "core", swap)
    whole = top + rows + 2 * SMALL
    chip = pl.pallas_call(
        merge_kernel,
        name="merge",
        grid=(Y,),
        in_specs=[pl.BlockSpec((X, top + rows, channels), lambda i: (i, 0, 0))] * 2
        + [pl.BlockSpec((X, 2 * SMALL, channels), lambda i: (i, 0, 0))] * 2,
        out_specs=pl.BlockSpec((X, whole, channels), lambda i: (i, 0, 0)),
        out_shape=shape((places, whole, channels), bf16),
        compiler_params=GLUE_PARAMS,
    )(kept, came, small, small_came)
    chip, dconv, came_z, rows_came = lax.optimization_barrier(
        (chip, dconv, came_z, row_borders(dconv, reach))
    )
    line = pl.pallas_call(
        join_kernel,
        name="join",
        in_specs=[SMEM] + [VMEM] * 2,
        out_specs=[VMEM] * Z,
        out_shape=[shape(kept_z.shape[1:], bf16)] * Z,
        compiler_params=GLUE_PARAMS,
    )(place, kept_z, came_z)
    line = [
        part if step == 0 else lax.ppermute(part, "z", [(i, (i + step) % Z) for i in range(Z)])
        for step, part in enumerate(line)
    ]
    chunks, edges, line = lax.optimization_barrier(
        (exchanged(chip, ("y", "x")), column_borders(dconv, *rows_came, reach), line)
    )
    chunks = pl.pallas_call(
        plane_kernel,
        name="plane",
        in_specs=[VMEM],
        out_specs=VMEM,
        out_shape=shape((Z, 2 * each + 2 * SMALL, channels), bf16),
        scratch_shapes=[pltpu.VMEM((whole, channels), f32)],
        compiler_params=GLUE_PARAMS,
    )(chunks)
    part, dexpand, chunks = pl.pallas_call(
        functools.partial(line_kernel, multiplier),
        name="line",
        in_specs=[VMEM] * (1 + Z),
        out_specs=[VMEM] * 3,
        out_shape=[
            shape((each, channels), f32),
            shape((channels * each // hidden, hidden), f32),
            shape((places, each, channels), bf16),
        ],
        compiler_params=GLUE_PARAMS,
    )(exchanged(chunks, "z"), *line)
    dreduce, dkernel, dgain, dscale = pl.pallas_call(
        functools.partial(last_kernel, multiplier),
        name="last",
        in_specs=[VMEM] * 2,
        out_specs=[VMEM] * 4,
        out_shape=[shape((each, channels), f32), shape((side, side, channels), f32)]
        + [shape((1, channels), f32)] * 2,
        compiler_params=GLUE_PARAMS,
    )(exchanged(chunks, ("y", "x")), part)
    grad_features = pl.pallas_call(
        feature_kernel,
        name="features",
        in_specs=[SMEM] + [VMEM] * 7,
        out_specs=VMEM,
        out_shape=shape((height, width, channels), bf16),
        scratch_shapes=[pltpu.VMEM(padded_shape, f32)],
        compiler_params=GLUE_PARAMS,
    )(place, dconv, *edges, kernel, cotangent)
    return (
        grad_features,
        dkernel,
        dgain.reshape(channels),
        dscale.reshape(channels),
        dexpand,
        dreduce,
    )


def solution(mesh):
    pixels = P(ROW, COL, None)
    return jax.shard_map(
        shards,
        mesh=Mesh(mesh.devices.reshape(Y, CORE, X, Z), (*ROW, *COL)),
        in_specs=(pixels, P(), P(), P(), P(), P(), pixels),
        out_specs=(pixels, P(), P(), P(), P((*ROW, *COL), None), P((*ROW, *COL), None)),
        check_vma=False,
    )
```

```python
import functools
import math

import jax
import jax.numpy as jnp
from jax import lax
from jax.experimental import pallas as pl
from jax.experimental.pallas import tpu as pltpu
from jax.sharding import Mesh
from jax.sharding import PartitionSpec as P

Y, CORE, X, Z = 4, 2, 4, 8
ROW, COL = ("y", "core"), ("x", "z")
INV_ROOT_TWO = 1.0 / math.sqrt(2.0)
INV_ROOT_TWO_PI = 1.0 / math.sqrt(2.0 * math.pi)
LANES = 128
ALONG = 256
LEFT = 8
SMALL = 4

NN = (((1,), (0,)), ((), ()))
NT = (((1,), (1,)), ((), ()))
TN = (((0,), (0,)), ((), ()))


def product(left, right, dims):
    return lax.dot_general(left, right, dims, preferred_element_type=jnp.float32)


def border_rows(first, rows, reach):
    return jnp.where(first, rows - reach, 0), jnp.where(first, 0, rows - reach)


def fill_own(padded, field, inner, outer, first_row, reach):
    height, width, channels = field.shape
    own = pl.ds(LEFT, width)
    starts = border_rows(first_row, height + 2 * reach, reach)
    for block in range(channels // LANES):
        lanes = pl.ds(block * LANES, LANES)
        padded[block, pl.ds(reach, height), own, :] = field[:, :, lanes].astype(jnp.float32)
        for border, start in zip((inner, outer), starts):
            padded[block, pl.ds(start, reach), own, :] = border[:, :, lanes].astype(jnp.float32)


def fill_sides(padded, inner, outer, first_row, first_column, width, reach):
    rows = padded.shape[1]
    before, after = border_rows(first_row, rows, reach)

    def fill(left, right):
        for block in range(padded.shape[0]):
            lanes = pl.ds(block * LANES, LANES)
            for side, column in ((left, LEFT - reach), (right, LEFT + width)):
                value = side[:, :, lanes].astype(jnp.float32)
                columns = pl.ds(column, reach)
                padded[block, pl.ds(before, reach), columns, :] = value[:reach]
                padded[block, pl.ds(reach, rows - 2 * reach), columns, :] = value[
                    reach : rows - reach
                ]
                padded[block, pl.ds(after, reach), columns, :] = value[rows - reach :]

    @pl.when(first_column)
    def _():
        fill(outer, inner)

    @pl.when(jnp.logical_not(first_column))
    def _():
        fill(inner, outer)


def depthwise(padded, taps, block, first_col, height, side, flip):
    reach = side // 2
    totals = [None] * height
    lanes = pl.ds(pl.multiple_of(block * LANES, LANES), LANES)
    for second in range(side):
        columns = pl.ds(LEFT - reach + first_col + second, 8)
        rows = [padded[block, row, columns, :] for row in range(height + side - 1)]
        for first in range(side):
            if flip:
                weight = taps[side - 1 - first, pl.ds(side - 1 - second, 1), lanes]
            else:
                weight = taps[first, pl.ds(second, 1), lanes]
            for row in range(height):
                term = weight * rows[row + first]
                totals[row] = term if totals[row] is None else totals[row] + term
    return totals


def conv_columns(conv, padded, taps, height, width, starts):
    def conv_block(block, _):
        for first_col in starts:
            totals = depthwise(padded, taps, block, first_col, height, taps.shape[0], False)
            for row, total in enumerate(totals):
                conv[block, pl.ds(row * width + first_col, 8), :] = total
        return 0

    lax.fori_loop(0, padded.shape[0], conv_block, 0)


def slot(index, rows, channels):
    across = channels // LANES
    return pl.ds(index // across * rows, rows), pl.ds(index % across * LANES, LANES)


def prepare_kernel(
    place_ref, field_h, inner, outer, taps_h, gain_h, scale_h, cotangent_h, expand_h, reduce_h,
    padded, conv, dbranch, taps, rows_out, expand, reduce,
    field, gain, scale, cotangent, sems,
):
    copies = [
        pltpu.make_async_copy(source, target, sems.at[i])
        for i, (source, target) in enumerate(
            (
                (field_h, field),
                (taps_h, taps),
                (gain_h, gain),
                (scale_h, scale),
                (cotangent_h, cotangent),
                (reduce_h, reduce),
                (expand_h, expand),
            )
        )
    ]
    for copy in copies:
        copy.start()
    for copy in copies[:2]:
        copy.wait()
    height, width, channels = field.shape
    fill_own(padded, field, inner, outer, place_ref[0] == 0, taps.shape[0] // 2)
    conv_columns(conv, padded, taps, height, width, range(8, width - 8, 8))
    for copy in copies[2:5]:
        copy.wait()
    rows_out[pl.ds(0, 8), :] = jnp.broadcast_to(gain[...], (8, channels))
    rows_out[pl.ds(8, 8), :] = jnp.broadcast_to(scale[...], (8, channels))
    for row in range(height):
        value = cotangent[row].astype(jnp.float32) * scale[...]
        dbranch[pl.ds(row * width, width), :] = value.astype(jnp.bfloat16)
    for copy in copies[5:]:
        copy.wait()


def forward_kernel(
    place_ref, inner, outer, padded_in, conv, dbranch, taps, rows_in, expand, reduce,
    sent, kept, sent_z, kept_z, dpre_out, xhat_out, rstd_out, padded, dscale_out,
    normed, turned, chosen,
):
    core = place_ref[0]
    first_column = lax.rem(place_ref[1], 2) == 0
    del padded_in
    blocks = padded.shape[0]
    side = taps.shape[0]
    height = padded.shape[1] - side + 1
    width = conv.shape[1] // height
    channels = blocks * LANES
    fill_sides(padded, inner, outer, core == 0, first_column, width, side // 2)
    conv_columns(conv, padded, taps, height, width, (0, width - 8))
    for row in range(height):
        pixels = pl.ds(row * width, width)
        values = [conv[block, pixels, :] for block in range(blocks)]
        mean = jnp.sum(sum(values), axis=-1, keepdims=True) / channels
        values = [value - mean for value in values]
        spread = jnp.sum(sum(value * value for value in values), axis=-1, keepdims=True) / channels
        rstd = lax.rsqrt(spread + 1e-06)
        rstd_out[pixels, :] = jnp.broadcast_to(rstd, (width, LANES))
        for block, value in enumerate(values):
            lanes = pl.ds(block * LANES, LANES)
            xhat = value * rstd
            xhat_out[block, pixels, :] = xhat
            normed[pixels, lanes] = (xhat * rows_in[pl.ds(0, 1), lanes]).astype(jnp.bfloat16)
    turned[...] = normed[...].T
    part = channels // (Y * CORE)
    for y in range(Y):
        for own in range(CORE):
            owner = core if own else 1 - core
            chosen[pl.ds((own * Y + y) * part, part), :] = turned[
                pl.ds(pl.multiple_of((y * CORE + owner) * part, part), part), :
            ]
    dscale_out[...] = jnp.zeros_like(dscale_out)
    step = reduce.shape[0] // (Y * CORE)
    per_z = step // (X * Z)
    part_x = part // X
    wide = channels // step
    kept_blocks = (channels - ALONG) // LANES
    top = per_z * Z * kept_blocks * LANES // channels

    def hidden_block(y, _):
        for own, target, target_z in ((0, sent, sent_z), (1, kept, kept_z)):
            owner = core if own else 1 - core
            chunk = y * CORE + owner
            hidden = pl.ds(pl.multiple_of(chunk * step, step), step)
            pre = product(normed[...], expand[:, hidden], NN)
            dact = product(dbranch[...], reduce[hidden, :], NT)
            half = 0.5 * (1.0 + lax.erf(pre * INV_ROOT_TWO))
            slope = half + pre * jnp.exp(-0.5 * pre * pre) * INV_ROOT_TWO_PI
            act = (pre * half).astype(jnp.bfloat16)
            dpre = (dact * slope).astype(jnp.bfloat16)
            dpre_out[:, hidden] = dpre
            share = product(act, dbranch[...], TN)
            weighed = share * reduce[hidden, :].astype(jnp.float32)
            dscale_out[...] += jnp.sum(weighed.reshape(step // 8, 8, channels), axis=0)
            share = share.astype(jnp.bfloat16)
            for place in range(X * Z):
                x, z = place // Z, place % Z
                mine = share[place * per_z : (place + 1) * per_z]
                for i in range(kept_blocks):
                    slot_rows, slot_lanes = slot(z * kept_blocks + i, per_z, channels)
                    target[y * X + x, slot_rows, slot_lanes] = mine[
                        :, i * LANES : (i + 1) * LANES
                    ]
                target_z[z, y, :, pl.ds(x * ALONG, ALONG)] = mine[:, kept_blocks * LANES :]
            share = product(chosen[...], dpre, NN).astype(jnp.bfloat16)
            rows = pl.ds(pl.multiple_of(top + (chunk // wide) * part_x, part_x), part_x)
            lanes = pl.ds(pl.multiple_of((chunk % wide) * step, step), step)
            for place in range(Y * X):
                for back, goal in ((0, sent), (1, kept)):
                    first = back * Y * part + place * part_x
                    goal[place, rows, lanes] = share[first : first + part_x]
        return 0

    lax.fori_loop(0, Y, hidden_block, 0)


def backward_kernel(
    multiplier, dpre, expand, xhat, rstd, padded, rows, dscale, dconv_out, out, dconv, small
):
    height, width, channels = dconv_out.shape
    blocks = channels // LANES
    side = 7
    dnormed = product(dpre[...], expand[...], NT)
    for block in range(blocks):
        dconv[block] = dnormed[:, block * LANES : (block + 1) * LANES]
    sums = [jnp.zeros((width, LANES), jnp.float32)] * blocks
    for row in range(height):
        pixels = pl.ds(row * width, width)
        grads = [dconv[block, pixels, :] for block in range(blocks)]
        hats = [xhat[block, pixels, :] for block in range(blocks)]
        sums = [total + grad * hat for total, grad, hat in zip(sums, grads, hats)]
        grads = [grad * rows[pl.ds(0, 1), pl.ds(block * LANES, LANES)] for block, grad in enumerate(grads)]
        mean = jnp.sum(sum(grads), axis=-1, keepdims=True) / channels
        slant = sum(grad * hat for grad, hat in zip(grads, hats))
        slant = jnp.sum(slant, axis=-1, keepdims=True) / channels
        for block in range(blocks):
            value = rstd[pixels, :] * (grads[block] - mean - hats[block] * slant)
            dconv[block, pixels, :] = value
            dconv_out[row, :, pl.ds(block * LANES, LANES)] = value.astype(jnp.bfloat16)
    taps = side * side
    unused = small.shape[0] - taps - 2
    small[pl.ds(taps + 2, unused), :] = jnp.zeros((unused, channels), jnp.float32)
    for block in range(blocks):
        lanes = pl.ds(block * LANES, LANES)
        total = jnp.sum(sums[block], axis=0, keepdims=True)
        small[pl.ds(taps, 1), lanes] = total * multiplier
        total = jnp.sum(dscale[:, lanes], axis=0, keepdims=True)
        small[pl.ds(taps + 1, 1), lanes] = total / rows[pl.ds(8, 1), lanes] * multiplier

    def tap_block(block, _):
        lanes = pl.ds(pl.multiple_of(block * LANES, LANES), LANES)
        for second in range(side):
            totals = [jnp.zeros((8, LANES), jnp.float32)] * side
            for first_col in range(0, width, 8):
                grads = [
                    dconv[block, pl.ds(row * width + first_col, 8), :] for row in range(height)
                ]
                columns = pl.ds(LEFT - side // 2 + first_col + second, 8)
                for row in range(height + side - 1):
                    value = padded[block, row, columns, :]
                    for first in range(max(0, row - height + 1), min(side, row + 1)):
                        totals[first] = totals[first] + grads[row - first] * value
            for first, total in enumerate(totals):
                total = jnp.sum(total, axis=0, keepdims=True) * multiplier
                small[pl.ds(first * side + second, 1), lanes] = total
        return 0

    lax.fori_loop(0, blocks, tap_block, 0)
    for place in range(out.shape[0]):
        part = small[pl.ds(place * SMALL, SMALL), :]
        out[place] = jnp.concatenate([part, jnp.zeros_like(part)]).astype(jnp.bfloat16)


def feature_kernel(
    place_ref, field, row_inner, row_outer, inner, outer, taps, cotangent, out, padded
):
    height, width, channels = field.shape
    side = 7
    first_row = place_ref[0] == 0
    first_column = lax.rem(place_ref[1], 2) == 0
    fill_own(padded, field, row_inner, row_outer, first_row, side // 2)
    fill_sides(padded, inner, outer, first_row, first_column, width, side // 2)
    for block in range(channels // LANES):
        lanes = pl.ds(block * LANES, LANES)
        for first_col in range(0, width, 8):
            columns = pl.ds(first_col, 8)
            for row, total in enumerate(
                depthwise(padded, taps, block, first_col, height, side, True)
            ):
                total = total + cotangent[row, columns, lanes].astype(jnp.float32)
                out[row, columns, lanes] = total.astype(jnp.bfloat16)


def added(left, right):
    return (left.astype(jnp.float32) + right.astype(jnp.float32)).astype(jnp.bfloat16)


def merge_kernel(kept, came, small, small_came, out):
    rows = kept.shape[1]
    out[:, pl.ds(0, rows), :] = added(kept[...], came[...])
    out[:, pl.ds(rows, small.shape[1]), :] = added(small[...], small_came[...])


def join_kernel(place_ref, kept, came, *outs):
    for step, out in enumerate(outs):
        z = place_ref[1] ^ step
        out[...] = added(kept[z], came[z])


def plane_kernel(chunks, out, total):
    total[...] = jnp.sum(chunks[...].astype(jnp.float32), axis=0)
    each = (out.shape[1] - 2 * SMALL) // 2
    channels = out.shape[2]
    top = total.shape[0] - 2 * SMALL - each * Z
    blocks = (channels - ALONG) // LANES
    small = total[pl.ds(total.shape[0] - 2 * SMALL, 2 * SMALL), :].astype(jnp.bfloat16)
    for z in range(Z):
        parts = [total[slot(z * blocks + i, each, channels)] for i in range(blocks)]
        parts.append(jnp.zeros((each, ALONG), jnp.float32))
        out[z, pl.ds(0, each), :] = jnp.concatenate(parts, axis=1).astype(jnp.bfloat16)
        parts = [total[pl.ds(top + q * 2 * Z + 2 * z, 2), :] for q in range(each // 2)]
        out[z, pl.ds(each, each), :] = jnp.concatenate(parts).astype(jnp.bfloat16)
        out[z, pl.ds(2 * each, 2 * SMALL), :] = small


def line_kernel(multiplier, chunks, *refs):
    *came, part_out, dexpand, out = refs
    total = jnp.sum(chunks[...].astype(jnp.float32), axis=0)
    each, channels = part_out.shape
    part_out[...] = total[:each] * multiplier
    for q in range(each // 2):
        part = total[each + 2 * q : each + 2 * q + 2]
        dexpand[:, pl.ds(q * channels, channels)] = part * multiplier
    small = total[2 * each : 2 * each + SMALL]
    half = channels // 2
    small = jnp.concatenate([small[:, :half], small[:, half:]]).astype(jnp.bfloat16)
    line = sum(ref[...].astype(jnp.float32) for ref in came).astype(jnp.bfloat16)
    for place in range(out.shape[0]):
        y, x = place // X, place % X
        out[place, :, pl.ds(0, half)] = small
        out[place, :, pl.ds(half, ALONG)] = line[y][:, x * ALONG : (x + 1) * ALONG]


def last_kernel(multiplier, chunks, part, dreduce, dkernel, dgain, dscale):
    channels = dreduce.shape[1]
    half = channels // 2
    own = channels - ALONG
    dreduce[:, pl.ds(0, own)] = part[:, pl.ds(0, own)]
    total = jnp.sum(chunks[:, :, pl.ds(half, ALONG)].astype(jnp.float32), axis=0)
    dreduce[:, pl.ds(own, ALONG)] = total * multiplier
    side = dkernel.shape[0]
    for place in range(chunks.shape[0]):
        small = chunks[place, :, pl.ds(0, half)].astype(jnp.float32)
        for row in range(SMALL):
            tap = place * SMALL + row
            for i in range(2):
                lanes = pl.ds(i * half, half)
                value = small[i * SMALL + row : i * SMALL + row + 1]
                if tap < side * side:
                    dkernel[tap // side, pl.ds(tap % side, 1), lanes] = value
                elif tap == side * side:
                    dgain[:, lanes] = value
                elif tap == side * side + 1:
                    dscale[:, lanes] = value


VMEM = pl.BlockSpec(memory_space=pltpu.VMEM)
HBM = pl.BlockSpec(memory_space=pltpu.HBM)
SMEM = pl.BlockSpec(memory_space=pltpu.SMEM)
PARAMS = pltpu.CompilerParams(vmem_limit_bytes=20 << 20)
GLUE_PARAMS = pltpu.CompilerParams(vmem_limit_bytes=10 << 20)


def in_hbm(value):
    return pltpu.with_memory_space_constraint(value, pltpu.HBM)


def swapped(low, high, axes, first):
    count = lax.axis_size(axes)
    inner = [(i, i ^ 1) for i in range(count)]
    outer = [(i, i + 1 if i % 2 else i - 1) for i in range(1, count - 1)]
    return (
        lax.ppermute(jnp.where(first, high, low), axes, inner),
        lax.ppermute(jnp.where(first, low, high), axes, outer),
    )


def row_borders(field, reach):
    return swapped(field[:reach], field[-reach:], ROW, lax.axis_index("core") == 0)


def column_borders(field, inner, outer, reach):
    low, high = (
        jnp.concatenate([part[:, columns] for part in (inner, field, outer)])
        for columns in (slice(0, reach), slice(-reach, None))
    )
    return inner, outer, *swapped(low, high, COL, lax.axis_index("z") % 2 == 0)


def exchanged(chunks, axes):
    return lax.all_to_all(chunks, axes, 0, 0, tiled=True)


def shards(features, kernel, gain, w_expand, w_reduce, layer_scale, cotangent):
    height, width, channels = features.shape
    hidden = w_reduce.shape[0]
    side = kernel.shape[0]
    reach = side // 2
    blocks = channels // LANES
    pixels = height * width
    multiplier = 1.0 / math.sqrt(pixels * lax.axis_size(ROW) * lax.axis_size(COL))
    gain_row = gain.reshape(1, channels)
    scale_row = layer_scale.reshape(1, channels)
    place = jnp.stack([lax.axis_index("core"), lax.axis_index("z")])
    places = Y * X
    rows = hidden // (Y * CORE * X)
    f32, bf16 = jnp.float32, jnp.bfloat16
    shape = jax.ShapeDtypeStruct
    padded_shape = (blocks, height + side - 1, LEFT + width + 8, LANES)

    each = rows // Z
    top = rows * (channels - ALONG) // channels
    row_inner, row_outer, inner, outer = column_borders(
        features, *row_borders(features, reach), reach
    )
    padded, conv, dbranch, taps, params, expand, reduce = pl.pallas_call(
        prepare_kernel,
        name="prepare",
        in_specs=[SMEM, HBM] + [VMEM] * 2 + [HBM] * 6,
        out_specs=[VMEM] * 7,
        out_shape=[
            shape(padded_shape, f32),
            shape((blocks, pixels, LANES), f32),
            shape((pixels, channels), bf16),
            shape(kernel.shape, f32),
            shape((16, channels), f32),
            shape(w_expand.shape, bf16),
            shape(w_reduce.shape, bf16),
        ],
        scratch_shapes=[
            pltpu.VMEM(features.shape, bf16),
            pltpu.VMEM((1, channels), f32),
            pltpu.VMEM((1, channels), f32),
            pltpu.VMEM(cotangent.shape, bf16),
            pltpu.SemaphoreType.DMA((7,)),
        ],
        compiler_params=PARAMS,
    )(
        place, in_hbm(features), row_inner, row_outer, in_hbm(kernel), in_hbm(gain_row),
        in_hbm(scale_row), in_hbm(cotangent), in_hbm(w_expand), in_hbm(w_reduce),
    )
    sent, kept, sent_z, kept_z, dpre, xhat, rstd, padded, dscale = pl.pallas_call(
        forward_kernel,
        name="forward",
        in_specs=[SMEM] + [VMEM] * 9,
        out_specs=[VMEM] * 9,
        out_shape=[shape((places, top + rows, channels), bf16)] * 2
        + [shape((Z, Y, each, X * ALONG), bf16)] * 2
        + [
            shape((pixels, hidden), bf16),
            shape((blocks, pixels, LANES), f32),
            shape((pixels, LANES), f32),
            shape(padded_shape, f32),
            shape((8, channels), f32),
        ],
        scratch_shapes=[
            pltpu.VMEM((pixels, channels), bf16),
            pltpu.VMEM((channels, pixels), bf16),
            pltpu.VMEM((channels, pixels), bf16),
        ],
        input_output_aliases={3: 7},
        compiler_params=PARAMS,
    )(place, inner, outer, padded, conv, dbranch, taps, params, expand, reduce)

    swap = [(0, 1), (1, 0)]
    came = lax.ppermute(sent, "core", swap)
    came_z = lax.ppermute(sent_z, "core", swap)
    dconv, small = pl.pallas_call(
        functools.partial(backward_kernel, multiplier),
        name="backward",
        in_specs=[VMEM] * 7,
        out_specs=[VMEM] * 2,
        out_shape=[
            shape((height, width, channels), bf16),
            shape((places, 2 * SMALL, channels), bf16),
        ],
        scratch_shapes=[
            pltpu.VMEM((blocks, pixels, LANES), f32),
            pltpu.VMEM((places * SMALL, channels), f32),
        ],
        compiler_params=PARAMS,
    )(dpre, expand, xhat, rstd, padded, params, dscale)

    small_came = lax.ppermute(small, "core", swap)
    whole = top + rows + 2 * SMALL
    chip = pl.pallas_call(
        merge_kernel,
        name="merge",
        grid=(Y,),
        in_specs=[pl.BlockSpec((X, top + rows, channels), lambda i: (i, 0, 0))] * 2
        + [pl.BlockSpec((X, 2 * SMALL, channels), lambda i: (i, 0, 0))] * 2,
        out_specs=pl.BlockSpec((X, whole, channels), lambda i: (i, 0, 0)),
        out_shape=shape((places, whole, channels), bf16),
        compiler_params=GLUE_PARAMS,
    )(kept, came, small, small_came)
    chip, dconv, came_z, rows_came = lax.optimization_barrier(
        (chip, dconv, came_z, row_borders(dconv, reach))
    )
    line = pl.pallas_call(
        join_kernel,
        name="join",
        in_specs=[SMEM] + [VMEM] * 2,
        out_specs=[VMEM] * Z,
        out_shape=[shape(kept_z.shape[1:], bf16)] * Z,
        compiler_params=GLUE_PARAMS,
    )(place, kept_z, came_z)
    line = [
        part if step == 0 else lax.ppermute(part, "z", [(i, i ^ step) for i in range(Z)])
        for step, part in enumerate(line)
    ]
    chunks, edges, line = lax.optimization_barrier(
        (exchanged(chip, ("y", "x")), column_borders(dconv, *rows_came, reach), line)
    )
    chunks = pl.pallas_call(
        plane_kernel,
        name="plane",
        in_specs=[VMEM],
        out_specs=VMEM,
        out_shape=shape((Z, 2 * each + 2 * SMALL, channels), bf16),
        scratch_shapes=[pltpu.VMEM((whole, channels), f32)],
        compiler_params=GLUE_PARAMS,
    )(chunks)
    part, dexpand, chunks = pl.pallas_call(
        functools.partial(line_kernel, multiplier),
        name="line",
        in_specs=[VMEM] * (1 + Z),
        out_specs=[VMEM] * 3,
        out_shape=[
            shape((each, channels), f32),
            shape((channels * each // hidden, hidden), f32),
            shape((places, each, channels), bf16),
        ],
        compiler_params=GLUE_PARAMS,
    )(exchanged(chunks, "z"), *line)
    dreduce, dkernel, dgain, dscale = pl.pallas_call(
        functools.partial(last_kernel, multiplier),
        name="last",
        in_specs=[VMEM] * 2,
        out_specs=[VMEM] * 4,
        out_shape=[shape((each, channels), f32), shape((side, side, channels), f32)]
        + [shape((1, channels), f32)] * 2,
        compiler_params=GLUE_PARAMS,
    )(exchanged(chunks, ("y", "x")), part)
    grad_features = pl.pallas_call(
        feature_kernel,
        name="features",
        in_specs=[SMEM] + [VMEM] * 7,
        out_specs=VMEM,
        out_shape=shape((height, width, channels), bf16),
        scratch_shapes=[pltpu.VMEM(padded_shape, f32)],
        compiler_params=GLUE_PARAMS,
    )(place, dconv, *edges, kernel, cotangent)
    return (
        grad_features,
        dkernel,
        dgain.reshape(channels),
        dscale.reshape(channels),
        dexpand,
        dreduce,
    )


def solution(mesh):
    pixels = P(ROW, COL, None)
    return jax.shard_map(
        shards,
        mesh=Mesh(mesh.devices.reshape(Y, CORE, X, Z), (*ROW, *COL)),
        in_specs=(pixels, P(), P(), P(), P(), P(), pixels),
        out_specs=(pixels, P(), P(), P(), P((*ROW, *COL), None), P((*ROW, *COL), None)),
        check_vma=False,
    )
```

```python
import functools
import math

import jax
import jax.numpy as jnp
from jax import lax
from jax.experimental import pallas as pl
from jax.experimental.pallas import tpu as pltpu
from jax.sharding import Mesh
from jax.sharding import PartitionSpec as P

Y, CORE, X, Z = 4, 2, 4, 8
ROW, COL = ("y", "core"), ("x", "z")
INV_ROOT_TWO = 1.0 / math.sqrt(2.0)
INV_ROOT_TWO_PI = 1.0 / math.sqrt(2.0 * math.pi)
LANES = 128
ALONG = 256
LEFT = 8
SMALL = 4

NN = (((1,), (0,)), ((), ()))
NT = (((1,), (1,)), ((), ()))
TN = (((0,), (0,)), ((), ()))


def product(left, right, dims):
    return lax.dot_general(left, right, dims, preferred_element_type=jnp.float32)


def border_rows(first, rows, reach):
    return jnp.where(first, rows - reach, 0), jnp.where(first, 0, rows - reach)


def fill_own(padded, field, inner, outer, first_row, reach):
    height, width, channels = field.shape
    own = pl.ds(LEFT, width)
    starts = border_rows(first_row, height + 2 * reach, reach)
    for block in range(channels // LANES):
        lanes = pl.ds(block * LANES, LANES)
        padded[block, pl.ds(reach, height), own, :] = field[:, :, lanes].astype(jnp.float32)
        for border, start in zip((inner, outer), starts):
            padded[block, pl.ds(start, reach), own, :] = border[:, :, lanes].astype(jnp.float32)


def fill_sides(padded, inner, outer, first_row, first_column, width, reach):
    rows = padded.shape[1]
    before, after = border_rows(first_row, rows, reach)

    def fill(left, right):
        for block in range(padded.shape[0]):
            lanes = pl.ds(block * LANES, LANES)
            for side, column in ((left, LEFT - reach), (right, LEFT + width)):
                value = side[:, :, lanes].astype(jnp.float32)
                columns = pl.ds(column, reach)
                padded[block, pl.ds(before, reach), columns, :] = value[:reach]
                padded[block, pl.ds(reach, rows - 2 * reach), columns, :] = value[
                    reach : rows - reach
                ]
                padded[block, pl.ds(after, reach), columns, :] = value[rows - reach :]

    @pl.when(first_column)
    def _():
        fill(outer, inner)

    @pl.when(jnp.logical_not(first_column))
    def _():
        fill(inner, outer)


def depthwise(padded, taps, block, first_col, height, side, flip):
    reach = side // 2
    totals = [None] * height
    lanes = pl.ds(pl.multiple_of(block * LANES, LANES), LANES)
    for second in range(side):
        columns = pl.ds(LEFT - reach + first_col + second, 8)
        rows = [padded[block, row, columns, :] for row in range(height + side - 1)]
        for first in range(side):
            if flip:
                weight = taps[side - 1 - first, pl.ds(side - 1 - second, 1), lanes]
            else:
                weight = taps[first, pl.ds(second, 1), lanes]
            for row in range(height):
                term = weight * rows[row + first]
                totals[row] = term if totals[row] is None else totals[row] + term
    return totals


def conv_columns(conv, padded, taps, height, width, starts):
    def conv_block(block, _):
        for first_col in starts:
            totals = depthwise(padded, taps, block, first_col, height, taps.shape[0], False)
            for row, total in enumerate(totals):
                conv[block, pl.ds(row * width + first_col, 8), :] = total
        return 0

    lax.fori_loop(0, padded.shape[0], conv_block, 0)


def slot(index, rows, channels):
    across = channels // LANES
    return pl.ds(index // across * rows, rows), pl.ds(index % across * LANES, LANES)


def prepare_kernel(
    place_ref, field_h, inner, outer, taps_h, gain_h, scale_h, cotangent_h, expand_h, reduce_h,
    padded, conv, dbranch, taps, rows_out, expand, reduce,
    field, gain, scale, cotangent, sems,
):
    copies = [
        pltpu.make_async_copy(source, target, sems.at[i])
        for i, (source, target) in enumerate(
            (
                (field_h, field),
                (taps_h, taps),
                (gain_h, gain),
                (scale_h, scale),
                (cotangent_h, cotangent),
                (reduce_h, reduce),
                (expand_h, expand),
            )
        )
    ]
    for copy in copies:
        copy.start()
    for copy in copies[:2]:
        copy.wait()
    height, width, channels = field.shape
    fill_own(padded, field, inner, outer, place_ref[0] == 0, taps.shape[0] // 2)
    conv_columns(conv, padded, taps, height, width, range(8, width - 8, 8))
    for copy in copies[2:5]:
        copy.wait()
    rows_out[pl.ds(0, 8), :] = jnp.broadcast_to(gain[...], (8, channels))
    rows_out[pl.ds(8, 8), :] = jnp.broadcast_to(scale[...], (8, channels))
    for row in range(height):
        value = cotangent[row].astype(jnp.float32) * scale[...]
        dbranch[pl.ds(row * width, width), :] = value.astype(jnp.bfloat16)
    for copy in copies[5:]:
        copy.wait()


def forward_kernel(
    place_ref, inner, outer, padded_in, conv, dbranch, taps, rows_in, expand, reduce,
    sent, kept, sent_z, kept_z, dpre_out, xhat_out, rstd_out, padded, dscale_out,
    normed, turned, chosen,
):
    core = place_ref[0]
    first_column = lax.rem(place_ref[1], 2) == 0
    del padded_in
    blocks = padded.shape[0]
    side = taps.shape[0]
    height = padded.shape[1] - side + 1
    width = conv.shape[1] // height
    channels = blocks * LANES
    fill_sides(padded, inner, outer, core == 0, first_column, width, side // 2)
    conv_columns(conv, padded, taps, height, width, (0, width - 8))
    for row in range(height):
        pixels = pl.ds(row * width, width)
        values = [conv[block, pixels, :] for block in range(blocks)]
        mean = jnp.sum(sum(values), axis=-1, keepdims=True) / channels
        values = [value - mean for value in values]
        spread = jnp.sum(sum(value * value for value in values), axis=-1, keepdims=True) / channels
        rstd = lax.rsqrt(spread + 1e-06)
        rstd_out[pixels, :] = jnp.broadcast_to(rstd, (width, LANES))
        for block, value in enumerate(values):
            lanes = pl.ds(block * LANES, LANES)
            xhat = value * rstd
            xhat_out[block, pixels, :] = xhat
            normed[pixels, lanes] = (xhat * rows_in[pl.ds(0, 1), lanes]).astype(jnp.bfloat16)
    turned[...] = normed[...].T
    part = channels // (Y * CORE)
    for y in range(Y):
        for own in range(CORE):
            owner = core if own else 1 - core
            chosen[pl.ds((own * Y + y) * part, part), :] = turned[
                pl.ds(pl.multiple_of((y * CORE + owner) * part, part), part), :
            ]
    dscale_out[...] = jnp.zeros_like(dscale_out)
    step = reduce.shape[0] // (Y * CORE)
    per_z = step // (X * Z)
    part_x = part // X
    wide = channels // step
    kept_blocks = (channels - ALONG) // LANES
    top = per_z * Z * kept_blocks * LANES // channels

    def hidden_block(y, _):
        for own, target, target_z in ((0, sent, sent_z), (1, kept, kept_z)):
            owner = core if own else 1 - core
            chunk = y * CORE + owner
            hidden = pl.ds(pl.multiple_of(chunk * step, step), step)
            pre = product(normed[...], expand[:, hidden], NN)
            dact = product(dbranch[...], reduce[hidden, :], NT)
            half = 0.5 * (1.0 + lax.erf(pre * INV_ROOT_TWO))
            slope = half + pre * jnp.exp(-0.5 * pre * pre) * INV_ROOT_TWO_PI
            act = (pre * half).astype(jnp.bfloat16)
            dpre = (dact * slope).astype(jnp.bfloat16)
            dpre_out[:, hidden] = dpre
            share = product(act, dbranch[...], TN)
            weighed = share * reduce[hidden, :].astype(jnp.float32)
            dscale_out[...] += jnp.sum(weighed.reshape(step // 8, 8, channels), axis=0)
            share = share.astype(jnp.bfloat16)
            for place in range(X * Z):
                x, z = place // Z, place % Z
                mine = share[place * per_z : (place + 1) * per_z]
                for i in range(kept_blocks):
                    slot_rows, slot_lanes = slot(z * kept_blocks + i, per_z, channels)
                    target[y * X + x, slot_rows, slot_lanes] = mine[
                        :, i * LANES : (i + 1) * LANES
                    ]
                target_z[z, y, :, pl.ds(x * ALONG, ALONG)] = mine[:, kept_blocks * LANES :]
            share = product(chosen[...], dpre, NN).astype(jnp.bfloat16)
            rows = pl.ds(pl.multiple_of(top + (chunk // wide) * part_x, part_x), part_x)
            lanes = pl.ds(pl.multiple_of((chunk % wide) * step, step), step)
            for place in range(Y * X):
                for back, goal in ((0, sent), (1, kept)):
                    first = back * Y * part + place * part_x
                    goal[place, rows, lanes] = share[first : first + part_x]
        return 0

    lax.fori_loop(0, Y, hidden_block, 0)


def backward_kernel(
    multiplier, dpre, expand, xhat, rstd, padded, rows, dscale, dconv_out, out, dconv, small
):
    height, width, channels = dconv_out.shape
    blocks = channels // LANES
    side = 7
    dnormed = product(dpre[...], expand[...], NT)
    for block in range(blocks):
        dconv[block] = dnormed[:, block * LANES : (block + 1) * LANES]
    sums = [jnp.zeros((width, LANES), jnp.float32)] * blocks
    for row in range(height):
        pixels = pl.ds(row * width, width)
        grads = [dconv[block, pixels, :] for block in range(blocks)]
        hats = [xhat[block, pixels, :] for block in range(blocks)]
        sums = [total + grad * hat for total, grad, hat in zip(sums, grads, hats)]
        grads = [grad * rows[pl.ds(0, 1), pl.ds(block * LANES, LANES)] for block, grad in enumerate(grads)]
        mean = jnp.sum(sum(grads), axis=-1, keepdims=True) / channels
        slant = sum(grad * hat for grad, hat in zip(grads, hats))
        slant = jnp.sum(slant, axis=-1, keepdims=True) / channels
        for block in range(blocks):
            value = rstd[pixels, :] * (grads[block] - mean - hats[block] * slant)
            dconv[block, pixels, :] = value
            dconv_out[row, :, pl.ds(block * LANES, LANES)] = value.astype(jnp.bfloat16)
    taps = side * side
    unused = small.shape[0] - taps - 2
    small[pl.ds(taps + 2, unused), :] = jnp.zeros((unused, channels), jnp.float32)
    for block in range(blocks):
        lanes = pl.ds(block * LANES, LANES)
        total = jnp.sum(sums[block], axis=0, keepdims=True)
        small[pl.ds(taps, 1), lanes] = total * multiplier
        total = jnp.sum(dscale[:, lanes], axis=0, keepdims=True)
        small[pl.ds(taps + 1, 1), lanes] = total / rows[pl.ds(8, 1), lanes] * multiplier

    def tap_block(block, _):
        lanes = pl.ds(pl.multiple_of(block * LANES, LANES), LANES)
        for second in range(side):
            totals = [jnp.zeros((8, LANES), jnp.float32)] * side
            for first_col in range(0, width, 8):
                grads = [
                    dconv[block, pl.ds(row * width + first_col, 8), :] for row in range(height)
                ]
                columns = pl.ds(LEFT - side // 2 + first_col + second, 8)
                for row in range(height + side - 1):
                    value = padded[block, row, columns, :]
                    for first in range(max(0, row - height + 1), min(side, row + 1)):
                        totals[first] = totals[first] + grads[row - first] * value
            for first, total in enumerate(totals):
                total = jnp.sum(total, axis=0, keepdims=True) * multiplier
                small[pl.ds(first * side + second, 1), lanes] = total
        return 0

    lax.fori_loop(0, blocks, tap_block, 0)
    for place in range(out.shape[0]):
        part = small[pl.ds(place * SMALL, SMALL), :]
        out[place] = jnp.concatenate([part, jnp.zeros_like(part)]).astype(jnp.bfloat16)


def feature_kernel(
    place_ref, field, row_inner, row_outer, inner, outer, taps, cotangent, out, padded
):
    height, width, channels = field.shape
    side = 7
    first_row = place_ref[0] == 0
    first_column = lax.rem(place_ref[1], 2) == 0
    fill_own(padded, field, row_inner, row_outer, first_row, side // 2)
    fill_sides(padded, inner, outer, first_row, first_column, width, side // 2)
    for block in range(channels // LANES):
        lanes = pl.ds(block * LANES, LANES)
        for first_col in range(0, width, 8):
            columns = pl.ds(first_col, 8)
            for row, total in enumerate(
                depthwise(padded, taps, block, first_col, height, side, True)
            ):
                total = total + cotangent[row, columns, lanes].astype(jnp.float32)
                out[row, columns, lanes] = total.astype(jnp.bfloat16)


def added(left, right):
    return (left.astype(jnp.float32) + right.astype(jnp.float32)).astype(jnp.bfloat16)


def merge_kernel(kept, came, small, small_came, out):
    rows = kept.shape[1]
    out[:, pl.ds(0, rows), :] = added(kept[...], came[...])
    out[:, pl.ds(rows, small.shape[1]), :] = added(small[...], small_came[...])


def join_kernel(place_ref, kept, came, *outs):
    for step, out in enumerate(outs):
        z = place_ref[1] ^ step
        out[...] = added(kept[z], came[z])


def plane_kernel(place_ref, chunks, *refs):
    *outs, out, total = refs
    total[...] = jnp.sum(chunks[...].astype(jnp.float32), axis=0)
    each = (out.shape[1] - 2 * SMALL) // 2
    channels = total.shape[1]
    top = total.shape[0] - 2 * SMALL - each * Z
    blocks = (channels - ALONG) // LANES
    small = total[pl.ds(total.shape[0] - 2 * SMALL, 2 * SMALL), :].astype(jnp.bfloat16)
    for z in range(Z):
        parts = [total[slot(z * blocks + i, each, channels)] for i in range(blocks)]
        parts.append(jnp.zeros((each, ALONG), jnp.float32))
        out[z, pl.ds(0, each), :] = jnp.concatenate(parts, axis=1).astype(jnp.bfloat16)
        parts = [total[pl.ds(top + q * 2 * Z + 2 * z, 2), :] for q in range(each // 2)]
        out[z, pl.ds(each, each), :] = jnp.concatenate(parts).astype(jnp.bfloat16)
        out[z, pl.ds(2 * each, 2 * SMALL), :] = small
    for step, target in enumerate(outs):
        target[...] = out[place_ref[1] ^ step]


def line_kernel(multiplier, *refs):
    *came, part_out, dexpand, out = refs
    chunks, came = came[:Z], came[Z:]
    total = sum(ref[...].astype(jnp.float32) for ref in chunks)
    each, channels = part_out.shape
    part_out[...] = total[:each] * multiplier
    for q in range(each // 2):
        part = total[each + 2 * q : each + 2 * q + 2]
        dexpand[:, pl.ds(q * channels, channels)] = part * multiplier
    small = total[2 * each : 2 * each + SMALL]
    half = channels // 2
    small = jnp.concatenate([small[:, :half], small[:, half:]]).astype(jnp.bfloat16)
    line = sum(ref[...].astype(jnp.float32) for ref in came).astype(jnp.bfloat16)
    for place in range(out.shape[0]):
        y, x = place // X, place % X
        out[place, :, pl.ds(0, half)] = small
        out[place, :, pl.ds(half, ALONG)] = line[y][:, x * ALONG : (x + 1) * ALONG]


def last_kernel(multiplier, chunks, part, dreduce, dkernel, dgain, dscale):
    channels = dreduce.shape[1]
    half = channels // 2
    own = channels - ALONG
    dreduce[:, pl.ds(0, own)] = part[:, pl.ds(0, own)]
    total = jnp.sum(chunks[:, :, pl.ds(half, ALONG)].astype(jnp.float32), axis=0)
    dreduce[:, pl.ds(own, ALONG)] = total * multiplier
    side = dkernel.shape[0]
    for place in range(chunks.shape[0]):
        small = chunks[place, :, pl.ds(0, half)].astype(jnp.float32)
        for row in range(SMALL):
            tap = place * SMALL + row
            for i in range(2):
                lanes = pl.ds(i * half, half)
                value = small[i * SMALL + row : i * SMALL + row + 1]
                if tap < side * side:
                    dkernel[tap // side, pl.ds(tap % side, 1), lanes] = value
                elif tap == side * side:
                    dgain[:, lanes] = value
                elif tap == side * side + 1:
                    dscale[:, lanes] = value


VMEM = pl.BlockSpec(memory_space=pltpu.VMEM)
HBM = pl.BlockSpec(memory_space=pltpu.HBM)
SMEM = pl.BlockSpec(memory_space=pltpu.SMEM)
PARAMS = pltpu.CompilerParams(vmem_limit_bytes=20 << 20)
GLUE_PARAMS = pltpu.CompilerParams(vmem_limit_bytes=10 << 20)


def in_hbm(value):
    return pltpu.with_memory_space_constraint(value, pltpu.HBM)


def swapped(low, high, axes, first):
    count = lax.axis_size(axes)
    inner = [(i, i ^ 1) for i in range(count)]
    outer = [(i, i + 1 if i % 2 else i - 1) for i in range(1, count - 1)]
    return (
        lax.ppermute(jnp.where(first, high, low), axes, inner),
        lax.ppermute(jnp.where(first, low, high), axes, outer),
    )


def row_borders(field, reach):
    return swapped(field[:reach], field[-reach:], ROW, lax.axis_index("core") == 0)


def column_borders(field, inner, outer, reach):
    low, high = (
        jnp.concatenate([part[:, columns] for part in (inner, field, outer)])
        for columns in (slice(0, reach), slice(-reach, None))
    )
    return inner, outer, *swapped(low, high, COL, lax.axis_index("z") % 2 == 0)


def along_z(parts):
    return [
        part if step == 0 else lax.ppermute(part, "z", [(i, i ^ step) for i in range(Z)])
        for step, part in enumerate(parts)
    ]


def exchanged(chunks, axes):
    return lax.all_to_all(chunks, axes, 0, 0, tiled=True)


def shards(features, kernel, gain, w_expand, w_reduce, layer_scale, cotangent):
    height, width, channels = features.shape
    hidden = w_reduce.shape[0]
    side = kernel.shape[0]
    reach = side // 2
    blocks = channels // LANES
    pixels = height * width
    multiplier = 1.0 / math.sqrt(pixels * lax.axis_size(ROW) * lax.axis_size(COL))
    gain_row = gain.reshape(1, channels)
    scale_row = layer_scale.reshape(1, channels)
    place = jnp.stack([lax.axis_index("core"), lax.axis_index("z")])
    places = Y * X
    rows = hidden // (Y * CORE * X)
    f32, bf16 = jnp.float32, jnp.bfloat16
    shape = jax.ShapeDtypeStruct
    padded_shape = (blocks, height + side - 1, LEFT + width + 8, LANES)

    each = rows // Z
    top = rows * (channels - ALONG) // channels
    row_inner, row_outer, inner, outer = column_borders(
        features, *row_borders(features, reach), reach
    )
    padded, conv, dbranch, taps, params, expand, reduce = pl.pallas_call(
        prepare_kernel,
        name="prepare",
        in_specs=[SMEM, HBM] + [VMEM] * 2 + [HBM] * 6,
        out_specs=[VMEM] * 7,
        out_shape=[
            shape(padded_shape, f32),
            shape((blocks, pixels, LANES), f32),
            shape((pixels, channels), bf16),
            shape(kernel.shape, f32),
            shape((16, channels), f32),
            shape(w_expand.shape, bf16),
            shape(w_reduce.shape, bf16),
        ],
        scratch_shapes=[
            pltpu.VMEM(features.shape, bf16),
            pltpu.VMEM((1, channels), f32),
            pltpu.VMEM((1, channels), f32),
            pltpu.VMEM(cotangent.shape, bf16),
            pltpu.SemaphoreType.DMA((7,)),
        ],
        compiler_params=PARAMS,
    )(
        place, in_hbm(features), row_inner, row_outer, in_hbm(kernel), in_hbm(gain_row),
        in_hbm(scale_row), in_hbm(cotangent), in_hbm(w_expand), in_hbm(w_reduce),
    )
    sent, kept, sent_z, kept_z, dpre, xhat, rstd, padded, dscale = pl.pallas_call(
        forward_kernel,
        name="forward",
        in_specs=[SMEM] + [VMEM] * 9,
        out_specs=[VMEM] * 9,
        out_shape=[shape((places, top + rows, channels), bf16)] * 2
        + [shape((Z, Y, each, X * ALONG), bf16)] * 2
        + [
            shape((pixels, hidden), bf16),
            shape((blocks, pixels, LANES), f32),
            shape((pixels, LANES), f32),
            shape(padded_shape, f32),
            shape((8, channels), f32),
        ],
        scratch_shapes=[
            pltpu.VMEM((pixels, channels), bf16),
            pltpu.VMEM((channels, pixels), bf16),
            pltpu.VMEM((channels, pixels), bf16),
        ],
        input_output_aliases={3: 7},
        compiler_params=PARAMS,
    )(place, inner, outer, padded, conv, dbranch, taps, params, expand, reduce)

    swap = [(0, 1), (1, 0)]
    came = lax.ppermute(sent, "core", swap)
    came_z = lax.ppermute(sent_z, "core", swap)
    dconv, small = pl.pallas_call(
        functools.partial(backward_kernel, multiplier),
        name="backward",
        in_specs=[VMEM] * 7,
        out_specs=[VMEM] * 2,
        out_shape=[
            shape((height, width, channels), bf16),
            shape((places, 2 * SMALL, channels), bf16),
        ],
        scratch_shapes=[
            pltpu.VMEM((blocks, pixels, LANES), f32),
            pltpu.VMEM((places * SMALL, channels), f32),
        ],
        compiler_params=PARAMS,
    )(dpre, expand, xhat, rstd, padded, params, dscale)

    small_came = lax.ppermute(small, "core", swap)
    whole = top + rows + 2 * SMALL
    chip = pl.pallas_call(
        merge_kernel,
        name="merge",
        grid=(Y,),
        in_specs=[pl.BlockSpec((X, top + rows, channels), lambda i: (i, 0, 0))] * 2
        + [pl.BlockSpec((X, 2 * SMALL, channels), lambda i: (i, 0, 0))] * 2,
        out_specs=pl.BlockSpec((X, whole, channels), lambda i: (i, 0, 0)),
        out_shape=shape((places, whole, channels), bf16),
        compiler_params=GLUE_PARAMS,
    )(kept, came, small, small_came)
    chip, dconv, came_z, rows_came = lax.optimization_barrier(
        (chip, dconv, came_z, row_borders(dconv, reach))
    )
    line = pl.pallas_call(
        join_kernel,
        name="join",
        in_specs=[SMEM] + [VMEM] * 2,
        out_specs=[VMEM] * Z,
        out_shape=[shape(kept_z.shape[1:], bf16)] * Z,
        compiler_params=GLUE_PARAMS,
    )(place, kept_z, came_z)
    line = along_z(line)
    chunks, edges, line = lax.optimization_barrier(
        (exchanged(chip, ("y", "x")), column_borders(dconv, *rows_came, reach), line)
    )
    per_z = 2 * each + 2 * SMALL
    chunks = pl.pallas_call(
        plane_kernel,
        name="plane",
        in_specs=[SMEM, VMEM],
        out_specs=[VMEM] * Z,
        out_shape=[shape((per_z, channels), bf16)] * Z,
        scratch_shapes=[
            pltpu.VMEM((Z, per_z, channels), bf16),
            pltpu.VMEM((whole, channels), f32),
        ],
        compiler_params=GLUE_PARAMS,
    )(place, chunks)
    part, dexpand, chunks = pl.pallas_call(
        functools.partial(line_kernel, multiplier),
        name="line",
        in_specs=[VMEM] * (2 * Z),
        out_specs=[VMEM] * 3,
        out_shape=[
            shape((each, channels), f32),
            shape((channels * each // hidden, hidden), f32),
            shape((places, each, channels), bf16),
        ],
        compiler_params=GLUE_PARAMS,
    )(*along_z(chunks), *line)
    dreduce, dkernel, dgain, dscale = pl.pallas_call(
        functools.partial(last_kernel, multiplier),
        name="last",
        in_specs=[VMEM] * 2,
        out_specs=[VMEM] * 4,
        out_shape=[shape((each, channels), f32), shape((side, side, channels), f32)]
        + [shape((1, channels), f32)] * 2,
        compiler_params=GLUE_PARAMS,
    )(exchanged(chunks, ("y", "x")), part)
    grad_features = pl.pallas_call(
        feature_kernel,
        name="features",
        in_specs=[SMEM] + [VMEM] * 7,
        out_specs=VMEM,
        out_shape=shape((height, width, channels), bf16),
        scratch_shapes=[pltpu.VMEM(padded_shape, f32)],
        compiler_params=GLUE_PARAMS,
    )(place, dconv, *edges, kernel, cotangent)
    return (
        grad_features,
        dkernel,
        dgain.reshape(channels),
        dscale.reshape(channels),
        dexpand,
        dreduce,
    )


def solution(mesh):
    pixels = P(ROW, COL, None)
    return jax.shard_map(
        shards,
        mesh=Mesh(mesh.devices.reshape(Y, CORE, X, Z), (*ROW, *COL)),
        in_specs=(pixels, P(), P(), P(), P(), P(), pixels),
        out_specs=(pixels, P(), P(), P(), P((*ROW, *COL), None), P((*ROW, *COL), None)),
        check_vma=False,
    )
```

```python
import functools
import math

import jax
import jax.numpy as jnp
from jax import lax
from jax.experimental import pallas as pl
from jax.experimental.pallas import tpu as pltpu
from jax.sharding import Mesh
from jax.sharding import PartitionSpec as P

Y, CORE, X, Z = 4, 2, 4, 8
ROW, COL = ("y", "core"), ("x", "z")
INV_ROOT_TWO = 1.0 / math.sqrt(2.0)
INV_ROOT_TWO_PI = 1.0 / math.sqrt(2.0 * math.pi)
LANES = 128
ALONG = 256
LEFT = 8
SMALL = 4

NN = (((1,), (0,)), ((), ()))
NT = (((1,), (1,)), ((), ()))
TN = (((0,), (0,)), ((), ()))


def product(left, right, dims):
    return lax.dot_general(left, right, dims, preferred_element_type=jnp.float32)


def border_rows(first, rows, reach):
    return jnp.where(first, rows - reach, 0), jnp.where(first, 0, rows - reach)


def fill_own(padded, field, inner, outer, first_row, reach):
    height, width, channels = field.shape
    own = pl.ds(LEFT, width)
    starts = border_rows(first_row, height + 2 * reach, reach)
    for block in range(channels // LANES):
        lanes = pl.ds(block * LANES, LANES)
        padded[block, pl.ds(reach, height), own, :] = field[:, :, lanes].astype(jnp.float32)
        for border, start in zip((inner, outer), starts):
            padded[block, pl.ds(start, reach), own, :] = border[:, :, lanes].astype(jnp.float32)


def fill_sides(padded, inner, outer, first_row, first_column, width, reach):
    rows = padded.shape[1]
    before, after = border_rows(first_row, rows, reach)

    def fill(left, right):
        for block in range(padded.shape[0]):
            lanes = pl.ds(block * LANES, LANES)
            for side, column in ((left, LEFT - reach), (right, LEFT + width)):
                value = side[:, :, lanes].astype(jnp.float32)
                columns = pl.ds(column, reach)
                padded[block, pl.ds(before, reach), columns, :] = value[:reach]
                padded[block, pl.ds(reach, rows - 2 * reach), columns, :] = value[
                    reach : rows - reach
                ]
                padded[block, pl.ds(after, reach), columns, :] = value[rows - reach :]

    @pl.when(first_column)
    def _():
        fill(outer, inner)

    @pl.when(jnp.logical_not(first_column))
    def _():
        fill(inner, outer)


def depthwise(padded, taps, block, first_col, height, side, flip):
    reach = side // 2
    totals = [None] * height
    lanes = pl.ds(pl.multiple_of(block * LANES, LANES), LANES)
    for second in range(side):
        columns = pl.ds(LEFT - reach + first_col + second, 8)
        rows = [padded[block, row, columns, :] for row in range(height + side - 1)]
        for first in range(side):
            if flip:
                weight = taps[side - 1 - first, pl.ds(side - 1 - second, 1), lanes]
            else:
                weight = taps[first, pl.ds(second, 1), lanes]
            for row in range(height):
                term = weight * rows[row + first]
                totals[row] = term if totals[row] is None else totals[row] + term
    return totals


def conv_columns(conv, padded, taps, height, width, starts):
    def conv_block(block, _):
        for first_col in starts:
            totals = depthwise(padded, taps, block, first_col, height, taps.shape[0], False)
            for row, total in enumerate(totals):
                conv[block, pl.ds(row * width + first_col, 8), :] = total
        return 0

    lax.fori_loop(0, padded.shape[0], conv_block, 0)


def slot(index, rows, channels):
    across = channels // LANES
    return pl.ds(index // across * rows, rows), pl.ds(index % across * LANES, LANES)


def prepare_kernel(
    field_h, inner, outer, taps_h, gain_h, scale_h, cotangent_h, expand_h, reduce_h,
    padded, conv, dbranch, taps, rows_out, expand, reduce,
    field, gain, scale, cotangent, sems,
):
    copies = [
        pltpu.make_async_copy(source, target, sems.at[i])
        for i, (source, target) in enumerate(
            (
                (field_h, field),
                (taps_h, taps),
                (gain_h, gain),
                (scale_h, scale),
                (cotangent_h, cotangent),
                (reduce_h, reduce),
                (expand_h, expand),
            )
        )
    ]
    for copy in copies:
        copy.start()
    for copy in copies[:2]:
        copy.wait()
    height, width, channels = field.shape
    fill_own(padded, field, inner, outer, lax.axis_index("core") == 0, taps.shape[0] // 2)
    conv_columns(conv, padded, taps, height, width, range(8, width - 8, 8))
    for copy in copies[2:5]:
        copy.wait()
    rows_out[pl.ds(0, 8), :] = jnp.broadcast_to(gain[...], (8, channels))
    rows_out[pl.ds(8, 8), :] = jnp.broadcast_to(scale[...], (8, channels))
    for row in range(height):
        value = cotangent[row].astype(jnp.float32) * scale[...]
        dbranch[pl.ds(row * width, width), :] = value.astype(jnp.bfloat16)
    for copy in copies[5:]:
        copy.wait()


def forward_kernel(
    inner, outer, padded_in, conv, dbranch, taps, rows_in, expand, reduce,
    sent, kept, sent_z, kept_z, dpre_out, xhat_out, rstd_out, padded, dscale_out,
    normed, turned, chosen,
):
    core = lax.axis_index("core")
    first_column = lax.rem(lax.axis_index("z"), 2) == 0
    del padded_in
    blocks = padded.shape[0]
    side = taps.shape[0]
    height = padded.shape[1] - side + 1
    width = conv.shape[1] // height
    channels = blocks * LANES
    fill_sides(padded, inner, outer, core == 0, first_column, width, side // 2)
    conv_columns(conv, padded, taps, height, width, (0, width - 8))
    for row in range(height):
        pixels = pl.ds(row * width, width)
        values = [conv[block, pixels, :] for block in range(blocks)]
        mean = jnp.sum(sum(values), axis=-1, keepdims=True) / channels
        values = [value - mean for value in values]
        spread = jnp.sum(sum(value * value for value in values), axis=-1, keepdims=True) / channels
        rstd = lax.rsqrt(spread + 1e-06)
        rstd_out[pixels, :] = jnp.broadcast_to(rstd, (width, LANES))
        for block, value in enumerate(values):
            lanes = pl.ds(block * LANES, LANES)
            xhat = value * rstd
            xhat_out[block, pixels, :] = xhat
            normed[pixels, lanes] = (xhat * rows_in[pl.ds(0, 1), lanes]).astype(jnp.bfloat16)
    turned[...] = normed[...].T
    part = channels // (Y * CORE)
    for y in range(Y):
        for own in range(CORE):
            owner = core if own else 1 - core
            chosen[pl.ds((own * Y + y) * part, part), :] = turned[
                pl.ds(pl.multiple_of((y * CORE + owner) * part, part), part), :
            ]
    dscale_out[...] = jnp.zeros_like(dscale_out)
    step = reduce.shape[0] // (Y * CORE)
    per_z = step // (X * Z)
    part_x = part // X
    wide = channels // step
    kept_blocks = (channels - ALONG) // LANES
    top = per_z * Z * kept_blocks * LANES // channels

    def hidden_block(y, _):
        for own, target, target_z in ((0, sent, sent_z), (1, kept, kept_z)):
            owner = core if own else 1 - core
            chunk = y * CORE + owner
            hidden = pl.ds(pl.multiple_of(chunk * step, step), step)
            pre = product(normed[...], expand[:, hidden], NN)
            dact = product(dbranch[...], reduce[hidden, :], NT)
            half = 0.5 * (1.0 + lax.erf(pre * INV_ROOT_TWO))
            slope = half + pre * jnp.exp(-0.5 * pre * pre) * INV_ROOT_TWO_PI
            act = (pre * half).astype(jnp.bfloat16)
            dpre = (dact * slope).astype(jnp.bfloat16)
            dpre_out[:, hidden] = dpre
            share = product(act, dbranch[...], TN)
            weighed = share * reduce[hidden, :].astype(jnp.float32)
            dscale_out[...] += jnp.sum(weighed.reshape(step // 8, 8, channels), axis=0)
            share = share.astype(jnp.bfloat16)
            for place in range(X * Z):
                x, z = place // Z, place % Z
                mine = share[place * per_z : (place + 1) * per_z]
                for i in range(kept_blocks):
                    slot_rows, slot_lanes = slot(z * kept_blocks + i, per_z, channels)
                    target[y * X + x, slot_rows, slot_lanes] = mine[
                        :, i * LANES : (i + 1) * LANES
                    ]
                target_z[z, y, :, pl.ds(x * ALONG, ALONG)] = mine[:, kept_blocks * LANES :]
            share = product(chosen[...], dpre, NN).astype(jnp.bfloat16)
            rows = pl.ds(pl.multiple_of(top + (chunk // wide) * part_x, part_x), part_x)
            lanes = pl.ds(pl.multiple_of((chunk % wide) * step, step), step)
            for place in range(Y * X):
                for back, goal in ((0, sent), (1, kept)):
                    first = back * Y * part + place * part_x
                    goal[place, rows, lanes] = share[first : first + part_x]
        return 0

    lax.fori_loop(0, Y, hidden_block, 0)


def backward_kernel(
    multiplier, dpre, expand, xhat, rstd, padded, rows, dscale, dconv_out, out, dconv, small
):
    height, width, channels = dconv_out.shape
    blocks = channels // LANES
    side = 7
    dnormed = product(dpre[...], expand[...], NT)
    for block in range(blocks):
        dconv[block] = dnormed[:, block * LANES : (block + 1) * LANES]
    sums = [jnp.zeros((width, LANES), jnp.float32)] * blocks
    for row in range(height):
        pixels = pl.ds(row * width, width)
        grads = [dconv[block, pixels, :] for block in range(blocks)]
        hats = [xhat[block, pixels, :] for block in range(blocks)]
        sums = [total + grad * hat for total, grad, hat in zip(sums, grads, hats)]
        grads = [grad * rows[pl.ds(0, 1), pl.ds(block * LANES, LANES)] for block, grad in enumerate(grads)]
        mean = jnp.sum(sum(grads), axis=-1, keepdims=True) / channels
        slant = sum(grad * hat for grad, hat in zip(grads, hats))
        slant = jnp.sum(slant, axis=-1, keepdims=True) / channels
        for block in range(blocks):
            value = rstd[pixels, :] * (grads[block] - mean - hats[block] * slant)
            dconv[block, pixels, :] = value
            dconv_out[row, :, pl.ds(block * LANES, LANES)] = value.astype(jnp.bfloat16)
    taps = side * side
    unused = small.shape[0] - taps - 2
    small[pl.ds(taps + 2, unused), :] = jnp.zeros((unused, channels), jnp.float32)
    for block in range(blocks):
        lanes = pl.ds(block * LANES, LANES)
        total = jnp.sum(sums[block], axis=0, keepdims=True)
        small[pl.ds(taps, 1), lanes] = total * multiplier
        total = jnp.sum(dscale[:, lanes], axis=0, keepdims=True)
        small[pl.ds(taps + 1, 1), lanes] = total / rows[pl.ds(8, 1), lanes] * multiplier

    def tap_block(block, _):
        lanes = pl.ds(pl.multiple_of(block * LANES, LANES), LANES)
        for second in range(side):
            totals = [jnp.zeros((8, LANES), jnp.float32)] * side
            for first_col in range(0, width, 8):
                grads = [
                    dconv[block, pl.ds(row * width + first_col, 8), :] for row in range(height)
                ]
                columns = pl.ds(LEFT - side // 2 + first_col + second, 8)
                for row in range(height + side - 1):
                    value = padded[block, row, columns, :]
                    for first in range(max(0, row - height + 1), min(side, row + 1)):
                        totals[first] = totals[first] + grads[row - first] * value
            for first, total in enumerate(totals):
                total = jnp.sum(total, axis=0, keepdims=True) * multiplier
                small[pl.ds(first * side + second, 1), lanes] = total
        return 0

    lax.fori_loop(0, blocks, tap_block, 0)
    for place in range(out.shape[0]):
        part = small[pl.ds(place * SMALL, SMALL), :]
        out[place] = jnp.concatenate([part, jnp.zeros_like(part)]).astype(jnp.bfloat16)


def feature_kernel(
    field, row_inner, row_outer, inner, outer, taps, cotangent, out, padded
):
    height, width, channels = field.shape
    side = 7
    first_row = lax.axis_index("core") == 0
    first_column = lax.rem(lax.axis_index("z"), 2) == 0
    fill_own(padded, field, row_inner, row_outer, first_row, side // 2)
    fill_sides(padded, inner, outer, first_row, first_column, width, side // 2)
    for block in range(channels // LANES):
        lanes = pl.ds(block * LANES, LANES)
        for first_col in range(0, width, 8):
            columns = pl.ds(first_col, 8)
            for row, total in enumerate(
                depthwise(padded, taps, block, first_col, height, side, True)
            ):
                total = total + cotangent[row, columns, lanes].astype(jnp.float32)
                out[row, columns, lanes] = total.astype(jnp.bfloat16)


def added(left, right):
    return (left.astype(jnp.float32) + right.astype(jnp.float32)).astype(jnp.bfloat16)


def merge_kernel(kept, came, small, small_came, out):
    rows = kept.shape[1]
    out[:, pl.ds(0, rows), :] = added(kept[...], came[...])
    out[:, pl.ds(rows, small.shape[1]), :] = added(small[...], small_came[...])


def join_kernel(kept, came, *outs):
    for step, out in enumerate(outs):
        z = lax.axis_index("z") ^ step
        out[...] = added(kept[z], came[z])


def plane_kernel(chunks, out, total):
    total[...] = jnp.sum(chunks[...].astype(jnp.float32), axis=0)
    each = (out.shape[1] - 2 * SMALL) // 2
    channels = out.shape[2]
    top = total.shape[0] - 2 * SMALL - each * Z
    blocks = (channels - ALONG) // LANES
    small = total[pl.ds(total.shape[0] - 2 * SMALL, 2 * SMALL), :].astype(jnp.bfloat16)
    for z in range(Z):
        parts = [total[slot(z * blocks + i, each, channels)] for i in range(blocks)]
        parts.append(jnp.zeros((each, ALONG), jnp.float32))
        out[z, pl.ds(0, each), :] = jnp.concatenate(parts, axis=1).astype(jnp.bfloat16)
        parts = [total[pl.ds(top + q * 2 * Z + 2 * z, 2), :] for q in range(each // 2)]
        out[z, pl.ds(each, each), :] = jnp.concatenate(parts).astype(jnp.bfloat16)
        out[z, pl.ds(2 * each, 2 * SMALL), :] = small


def line_kernel(multiplier, chunks, *refs):
    *came, part_out, dexpand, out = refs
    total = jnp.sum(chunks[...].astype(jnp.float32), axis=0)
    each, channels = part_out.shape
    part_out[...] = total[:each] * multiplier
    for q in range(each // 2):
        part = total[each + 2 * q : each + 2 * q + 2]
        dexpand[:, pl.ds(q * channels, channels)] = part * multiplier
    small = total[2 * each : 2 * each + SMALL]
    half = channels // 2
    small = jnp.concatenate([small[:, :half], small[:, half:]]).astype(jnp.bfloat16)
    line = sum(ref[...].astype(jnp.float32) for ref in came).astype(jnp.bfloat16)
    for place in range(out.shape[0]):
        y, x = place // X, place % X
        out[place, :, pl.ds(0, half)] = small
        out[place, :, pl.ds(half, ALONG)] = line[y][:, x * ALONG : (x + 1) * ALONG]


def last_kernel(multiplier, chunks, part, dreduce, dkernel, dgain, dscale):
    channels = dreduce.shape[1]
    half = channels // 2
    own = channels - ALONG
    dreduce[:, pl.ds(0, own)] = part[:, pl.ds(0, own)]
    total = jnp.sum(chunks[:, :, pl.ds(half, ALONG)].astype(jnp.float32), axis=0)
    dreduce[:, pl.ds(own, ALONG)] = total * multiplier
    side = dkernel.shape[0]
    for place in range(chunks.shape[0]):
        small = chunks[place, :, pl.ds(0, half)].astype(jnp.float32)
        for row in range(SMALL):
            tap = place * SMALL + row
            for i in range(2):
                lanes = pl.ds(i * half, half)
                value = small[i * SMALL + row : i * SMALL + row + 1]
                if tap < side * side:
                    dkernel[tap // side, pl.ds(tap % side, 1), lanes] = value
                elif tap == side * side:
                    dgain[:, lanes] = value
                elif tap == side * side + 1:
                    dscale[:, lanes] = value


VMEM = pl.BlockSpec(memory_space=pltpu.VMEM)
HBM = pl.BlockSpec(memory_space=pltpu.HBM)
PARAMS = pltpu.CompilerParams(vmem_limit_bytes=20 << 20)
GLUE_PARAMS = pltpu.CompilerParams(vmem_limit_bytes=10 << 20)


def in_hbm(value):
    return pltpu.with_memory_space_constraint(value, pltpu.HBM)


def swapped(low, high, axes, first):
    count = lax.axis_size(axes)
    inner = [(i, i ^ 1) for i in range(count)]
    outer = [(i, i + 1 if i % 2 else i - 1) for i in range(1, count - 1)]
    return (
        lax.ppermute(jnp.where(first, high, low), axes, inner),
        lax.ppermute(jnp.where(first, low, high), axes, outer),
    )


def row_borders(field, reach):
    return swapped(field[:reach], field[-reach:], ROW, lax.axis_index("core") == 0)


def column_borders(field, inner, outer, reach):
    low, high = (
        jnp.concatenate([part[:, columns] for part in (inner, field, outer)])
        for columns in (slice(0, reach), slice(-reach, None))
    )
    return inner, outer, *swapped(low, high, COL, lax.axis_index("z") % 2 == 0)


def exchanged(chunks, axes):
    return lax.all_to_all(chunks, axes, 0, 0, tiled=True)


def shards(features, kernel, gain, w_expand, w_reduce, layer_scale, cotangent):
    height, width, channels = features.shape
    hidden = w_reduce.shape[0]
    side = kernel.shape[0]
    reach = side // 2
    blocks = channels // LANES
    pixels = height * width
    multiplier = 1.0 / math.sqrt(pixels * lax.axis_size(ROW) * lax.axis_size(COL))
    gain_row = gain.reshape(1, channels)
    scale_row = layer_scale.reshape(1, channels)
    places = Y * X
    rows = hidden // (Y * CORE * X)
    f32, bf16 = jnp.float32, jnp.bfloat16
    shape = jax.ShapeDtypeStruct
    padded_shape = (blocks, height + side - 1, LEFT + width + 8, LANES)

    each = rows // Z
    top = rows * (channels - ALONG) // channels
    row_inner, row_outer, inner, outer = column_borders(
        features, *row_borders(features, reach), reach
    )
    padded, conv, dbranch, taps, params, expand, reduce = pl.pallas_call(
        prepare_kernel,
        name="prepare",
        in_specs=[HBM] + [VMEM] * 2 + [HBM] * 6,
        out_specs=[VMEM] * 7,
        out_shape=[
            shape(padded_shape, f32),
            shape((blocks, pixels, LANES), f32),
            shape((pixels, channels), bf16),
            shape(kernel.shape, f32),
            shape((16, channels), f32),
            shape(w_expand.shape, bf16),
            shape(w_reduce.shape, bf16),
        ],
        scratch_shapes=[
            pltpu.VMEM(features.shape, bf16),
            pltpu.VMEM((1, channels), f32),
            pltpu.VMEM((1, channels), f32),
            pltpu.VMEM(cotangent.shape, bf16),
            pltpu.SemaphoreType.DMA((7,)),
        ],
        compiler_params=PARAMS,
    )(
        in_hbm(features), row_inner, row_outer, in_hbm(kernel), in_hbm(gain_row),
        in_hbm(scale_row), in_hbm(cotangent), in_hbm(w_expand), in_hbm(w_reduce),
    )
    sent, kept, sent_z, kept_z, dpre, xhat, rstd, padded, dscale = pl.pallas_call(
        forward_kernel,
        name="forward",
        in_specs=[VMEM] * 9,
        out_specs=[VMEM] * 9,
        out_shape=[shape((places, top + rows, channels), bf16)] * 2
        + [shape((Z, Y, each, X * ALONG), bf16)] * 2
        + [
            shape((pixels, hidden), bf16),
            shape((blocks, pixels, LANES), f32),
            shape((pixels, LANES), f32),
            shape(padded_shape, f32),
            shape((8, channels), f32),
        ],
        scratch_shapes=[
            pltpu.VMEM((pixels, channels), bf16),
            pltpu.VMEM((channels, pixels), bf16),
            pltpu.VMEM((channels, pixels), bf16),
        ],
        input_output_aliases={2: 7},
        compiler_params=PARAMS,
    )(inner, outer, padded, conv, dbranch, taps, params, expand, reduce)

    swap = [(0, 1), (1, 0)]
    came = lax.ppermute(sent, "core", swap)
    came_z = lax.ppermute(sent_z, "core", swap)
    dconv, small = pl.pallas_call(
        functools.partial(backward_kernel, multiplier),
        name="backward",
        in_specs=[VMEM] * 7,
        out_specs=[VMEM] * 2,
        out_shape=[
            shape((height, width, channels), bf16),
            shape((places, 2 * SMALL, channels), bf16),
        ],
        scratch_shapes=[
            pltpu.VMEM((blocks, pixels, LANES), f32),
            pltpu.VMEM((places * SMALL, channels), f32),
        ],
        compiler_params=PARAMS,
    )(dpre, expand, xhat, rstd, padded, params, dscale)

    small_came = lax.ppermute(small, "core", swap)
    whole = top + rows + 2 * SMALL
    chip = pl.pallas_call(
        merge_kernel,
        name="merge",
        grid=(Y,),
        in_specs=[pl.BlockSpec((X, top + rows, channels), lambda i: (i, 0, 0))] * 2
        + [pl.BlockSpec((X, 2 * SMALL, channels), lambda i: (i, 0, 0))] * 2,
        out_specs=pl.BlockSpec((X, whole, channels), lambda i: (i, 0, 0)),
        out_shape=shape((places, whole, channels), bf16),
        compiler_params=GLUE_PARAMS,
    )(kept, came, small, small_came)
    chip, dconv, came_z, rows_came = lax.optimization_barrier(
        (chip, dconv, came_z, row_borders(dconv, reach))
    )
    line = pl.pallas_call(
        join_kernel,
        name="join",
        in_specs=[VMEM] * 2,
        out_specs=[VMEM] * Z,
        out_shape=[shape(kept_z.shape[1:], bf16)] * Z,
        compiler_params=GLUE_PARAMS,
    )(kept_z, came_z)
    line = [
        part if step == 0 else lax.ppermute(part, "z", [(i, i ^ step) for i in range(Z)])
        for step, part in enumerate(line)
    ]
    chunks, edges, line = lax.optimization_barrier(
        (exchanged(chip, ("y", "x")), column_borders(dconv, *rows_came, reach), line)
    )
    chunks = pl.pallas_call(
        plane_kernel,
        name="plane",
        in_specs=[VMEM],
        out_specs=VMEM,
        out_shape=shape((Z, 2 * each + 2 * SMALL, channels), bf16),
        scratch_shapes=[pltpu.VMEM((whole, channels), f32)],
        compiler_params=GLUE_PARAMS,
    )(chunks)
    part, dexpand, chunks = pl.pallas_call(
        functools.partial(line_kernel, multiplier),
        name="line",
        in_specs=[VMEM] * (1 + Z),
        out_specs=[VMEM] * 3,
        out_shape=[
            shape((each, channels), f32),
            shape((channels * each // hidden, hidden), f32),
            shape((places, each, channels), bf16),
        ],
        compiler_params=GLUE_PARAMS,
    )(exchanged(chunks, "z"), *line)
    dreduce, dkernel, dgain, dscale = pl.pallas_call(
        functools.partial(last_kernel, multiplier),
        name="last",
        in_specs=[VMEM] * 2,
        out_specs=[VMEM] * 4,
        out_shape=[shape((each, channels), f32), shape((side, side, channels), f32)]
        + [shape((1, channels), f32)] * 2,
        compiler_params=GLUE_PARAMS,
    )(exchanged(chunks, ("y", "x")), part)
    grad_features = pl.pallas_call(
        feature_kernel,
        name="features",
        in_specs=[VMEM] * 7,
        out_specs=VMEM,
        out_shape=shape((height, width, channels), bf16),
        scratch_shapes=[pltpu.VMEM(padded_shape, f32)],
        compiler_params=GLUE_PARAMS,
    )(dconv, *edges, kernel, cotangent)
    return (
        grad_features,
        dkernel,
        dgain.reshape(channels),
        dscale.reshape(channels),
        dexpand,
        dreduce,
    )


def solution(mesh):
    pixels = P(ROW, COL, None)
    return jax.shard_map(
        shards,
        mesh=Mesh(mesh.devices.reshape(Y, CORE, X, Z), (*ROW, *COL)),
        in_specs=(pixels, P(), P(), P(), P(), P(), pixels),
        out_specs=(pixels, P(), P(), P(), P((*ROW, *COL), None), P((*ROW, *COL), None)),
        check_vma=False,
    )
```

```python
import functools
import math

import jax
import jax.numpy as jnp
from jax import lax
from jax.experimental import pallas as pl
from jax.experimental.pallas import tpu as pltpu
from jax.sharding import Mesh
from jax.sharding import PartitionSpec as P

Y, CORE, X, Z = 4, 2, 4, 8
ROW, COL = ("y", "core"), ("x", "z")
INV_ROOT_TWO = 1.0 / math.sqrt(2.0)
INV_ROOT_TWO_PI = 1.0 / math.sqrt(2.0 * math.pi)
LANES = 128
ALONG = 256
LEFT = 8
SMALL = 4

NN = (((1,), (0,)), ((), ()))
NT = (((1,), (1,)), ((), ()))
TN = (((0,), (0,)), ((), ()))


def product(left, right, dims):
    return lax.dot_general(left, right, dims, preferred_element_type=jnp.float32)


def border_rows(first, rows, reach):
    return jnp.where(first, rows - reach, 0), jnp.where(first, 0, rows - reach)


def fill_own(padded, field, inner, outer, first_row, reach):
    height, width, channels = field.shape
    own = pl.ds(LEFT, width)
    starts = border_rows(first_row, height + 2 * reach, reach)
    for block in range(channels // LANES):
        lanes = pl.ds(block * LANES, LANES)
        padded[block, pl.ds(reach, height), own, :] = field[:, :, lanes].astype(jnp.float32)
        for border, start in zip((inner, outer), starts):
            padded[block, pl.ds(start, reach), own, :] = border[:, :, lanes].astype(jnp.float32)


def fill_sides(padded, inner, outer, first_row, first_column, width, reach):
    rows = padded.shape[1]
    before, after = border_rows(first_row, rows, reach)

    def fill(left, right):
        for block in range(padded.shape[0]):
            lanes = pl.ds(block * LANES, LANES)
            for side, column in ((left, LEFT - reach), (right, LEFT + width)):
                value = side[:, :, lanes].astype(jnp.float32)
                columns = pl.ds(column, reach)
                padded[block, pl.ds(before, reach), columns, :] = value[:reach]
                padded[block, pl.ds(reach, rows - 2 * reach), columns, :] = value[
                    reach : rows - reach
                ]
                padded[block, pl.ds(after, reach), columns, :] = value[rows - reach :]

    @pl.when(first_column)
    def _():
        fill(outer, inner)

    @pl.when(jnp.logical_not(first_column))
    def _():
        fill(inner, outer)


def depthwise(padded, taps, block, first_col, height, side, flip):
    reach = side // 2
    totals = [None] * height
    lanes = pl.ds(pl.multiple_of(block * LANES, LANES), LANES)
    for second in range(side):
        columns = pl.ds(LEFT - reach + first_col + second, 8)
        rows = [padded[block, row, columns, :] for row in range(height + side - 1)]
        for first in range(side):
            if flip:
                weight = taps[side - 1 - first, pl.ds(side - 1 - second, 1), lanes]
            else:
                weight = taps[first, pl.ds(second, 1), lanes]
            for row in range(height):
                term = weight * rows[row + first]
                totals[row] = term if totals[row] is None else totals[row] + term
    return totals


def conv_columns(conv, padded, taps, height, width, starts):
    def conv_block(block, _):
        for first_col in starts:
            totals = depthwise(padded, taps, block, first_col, height, taps.shape[0], False)
            for row, total in enumerate(totals):
                conv[block, pl.ds(row * width + first_col, 8), :] = total
        return 0

    lax.fori_loop(0, padded.shape[0], conv_block, 0)


def slot(index, rows, channels):
    across = channels // LANES
    return pl.ds(index // across * rows, rows), pl.ds(index % across * LANES, LANES)


def prepare_kernel(
    field_h, inner, outer, taps_h, gain_h, scale_h, cotangent_h, expand_h, reduce_h,
    padded, conv, dbranch, taps, rows_out, expand, reduce,
    field, gain, scale, cotangent, sems,
):
    copies = [
        pltpu.make_async_copy(source, target, sems.at[i])
        for i, (source, target) in enumerate(
            (
                (field_h, field),
                (taps_h, taps),
                (gain_h, gain),
                (scale_h, scale),
                (cotangent_h, cotangent),
                (reduce_h, reduce),
                (expand_h, expand),
            )
        )
    ]
    for copy in copies:
        copy.start()
    for copy in copies[:2]:
        copy.wait()
    height, width, channels = field.shape
    fill_own(padded, field, inner, outer, lax.axis_index("core") == 0, taps.shape[0] // 2)
    conv_columns(conv, padded, taps, height, width, range(8, width - 8, 8))
    for copy in copies[2:5]:
        copy.wait()
    rows_out[pl.ds(0, 8), :] = jnp.broadcast_to(gain[...], (8, channels))
    rows_out[pl.ds(8, 8), :] = jnp.broadcast_to(scale[...], (8, channels))
    for row in range(height):
        value = cotangent[row].astype(jnp.float32) * scale[...]
        dbranch[pl.ds(row * width, width), :] = value.astype(jnp.bfloat16)
    for copy in copies[5:]:
        copy.wait()


def forward_kernel(
    inner, outer, padded_in, conv, dbranch, taps, rows_in, expand, reduce,
    sent, kept, sent_z, kept_z, dpre_out, xhat_out, rstd_out, padded, dscale_out,
    normed, turned, chosen,
):
    core = lax.axis_index("core")
    first_column = lax.rem(lax.axis_index("z"), 2) == 0
    del padded_in
    blocks = padded.shape[0]
    side = taps.shape[0]
    height = padded.shape[1] - side + 1
    width = conv.shape[1] // height
    channels = blocks * LANES
    fill_sides(padded, inner, outer, core == 0, first_column, width, side // 2)
    conv_columns(conv, padded, taps, height, width, (0, width - 8))
    for row in range(height):
        pixels = pl.ds(row * width, width)
        values = [conv[block, pixels, :] for block in range(blocks)]
        mean = jnp.sum(sum(values), axis=-1, keepdims=True) / channels
        values = [value - mean for value in values]
        spread = jnp.sum(sum(value * value for value in values), axis=-1, keepdims=True) / channels
        rstd = lax.rsqrt(spread + 1e-06)
        rstd_out[pixels, :] = jnp.broadcast_to(rstd, (width, LANES))
        for block, value in enumerate(values):
            lanes = pl.ds(block * LANES, LANES)
            xhat = value * rstd
            xhat_out[block, pixels, :] = xhat
            normed[pixels, lanes] = (xhat * rows_in[pl.ds(0, 1), lanes]).astype(jnp.bfloat16)
    turned[...] = normed[...].T
    part = channels // (Y * CORE)
    for y in range(Y):
        for own in range(CORE):
            owner = core if own else 1 - core
            chosen[pl.ds((own * Y + y) * part, part), :] = turned[
                pl.ds(pl.multiple_of((y * CORE + owner) * part, part), part), :
            ]
    dscale_out[...] = jnp.zeros_like(dscale_out)
    step = reduce.shape[0] // (Y * CORE)
    per_z = step // (X * Z)
    part_x = part // X
    wide = channels // step
    kept_blocks = (channels - ALONG) // LANES
    top = per_z * Z * kept_blocks * LANES // channels

    def hidden_block(y, _):
        for own, target, target_z in ((0, sent, sent_z), (1, kept, kept_z)):
            owner = core if own else 1 - core
            chunk = y * CORE + owner
            hidden = pl.ds(pl.multiple_of(chunk * step, step), step)
            pre = product(normed[...], expand[:, hidden], NN)
            dact = product(dbranch[...], reduce[hidden, :], NT)
            half = 0.5 * (1.0 + lax.erf(pre * INV_ROOT_TWO))
            slope = half + pre * jnp.exp(-0.5 * pre * pre) * INV_ROOT_TWO_PI
            act = (pre * half).astype(jnp.bfloat16)
            dpre = (dact * slope).astype(jnp.bfloat16)
            dpre_out[:, hidden] = dpre
            share = product(act, dbranch[...], TN)
            weighed = share * reduce[hidden, :].astype(jnp.float32)
            dscale_out[...] += jnp.sum(weighed.reshape(step // 8, 8, channels), axis=0)
            share = share.astype(jnp.bfloat16)
            for place in range(X * Z):
                x, z = place // Z, place % Z
                mine = share[place * per_z : (place + 1) * per_z]
                for i in range(kept_blocks):
                    slot_rows, slot_lanes = slot(z * kept_blocks + i, per_z, channels)
                    target[y * X + x, slot_rows, slot_lanes] = mine[
                        :, i * LANES : (i + 1) * LANES
                    ]
                target_z[z, y, :, pl.ds(x * ALONG, ALONG)] = mine[:, kept_blocks * LANES :]
            share = product(chosen[...], dpre, NN).astype(jnp.bfloat16)
            rows = pl.ds(pl.multiple_of(top + (chunk // wide) * part_x, part_x), part_x)
            lanes = pl.ds(pl.multiple_of((chunk % wide) * step, step), step)
            for place in range(Y * X):
                for back, goal in ((0, sent), (1, kept)):
                    first = back * Y * part + place * part_x
                    goal[place, rows, lanes] = share[first : first + part_x]
        return 0

    lax.fori_loop(0, Y, hidden_block, 0)


def backward_kernel(
    multiplier, dpre, expand, xhat, rstd, padded, rows, dscale, dconv_out, out, dconv, small
):
    height, width, channels = dconv_out.shape
    blocks = channels // LANES
    side = 7
    dnormed = product(dpre[...], expand[...], NT)
    for block in range(blocks):
        dconv[block] = dnormed[:, block * LANES : (block + 1) * LANES]
    sums = [jnp.zeros((width, LANES), jnp.float32)] * blocks
    for row in range(height):
        pixels = pl.ds(row * width, width)
        grads = [dconv[block, pixels, :] for block in range(blocks)]
        hats = [xhat[block, pixels, :] for block in range(blocks)]
        sums = [total + grad * hat for total, grad, hat in zip(sums, grads, hats)]
        grads = [grad * rows[pl.ds(0, 1), pl.ds(block * LANES, LANES)] for block, grad in enumerate(grads)]
        mean = jnp.sum(sum(grads), axis=-1, keepdims=True) / channels
        slant = sum(grad * hat for grad, hat in zip(grads, hats))
        slant = jnp.sum(slant, axis=-1, keepdims=True) / channels
        for block in range(blocks):
            value = rstd[pixels, :] * (grads[block] - mean - hats[block] * slant)
            dconv[block, pixels, :] = value
            dconv_out[row, :, pl.ds(block * LANES, LANES)] = value.astype(jnp.bfloat16)
    taps = side * side
    unused = small.shape[0] - taps - 2
    small[pl.ds(taps + 2, unused), :] = jnp.zeros((unused, channels), jnp.float32)
    for block in range(blocks):
        lanes = pl.ds(block * LANES, LANES)
        total = jnp.sum(sums[block], axis=0, keepdims=True)
        small[pl.ds(taps, 1), lanes] = total * multiplier
        total = jnp.sum(dscale[:, lanes], axis=0, keepdims=True)
        small[pl.ds(taps + 1, 1), lanes] = total / rows[pl.ds(8, 1), lanes] * multiplier

    def tap_block(block, _):
        lanes = pl.ds(pl.multiple_of(block * LANES, LANES), LANES)
        for second in range(side):
            totals = [jnp.zeros((8, LANES), jnp.float32)] * side
            for first_col in range(0, width, 8):
                grads = [
                    dconv[block, pl.ds(row * width + first_col, 8), :] for row in range(height)
                ]
                columns = pl.ds(LEFT - side // 2 + first_col + second, 8)
                for row in range(height + side - 1):
                    value = padded[block, row, columns, :]
                    for first in range(max(0, row - height + 1), min(side, row + 1)):
                        totals[first] = totals[first] + grads[row - first] * value
            for first, total in enumerate(totals):
                total = jnp.sum(total, axis=0, keepdims=True) * multiplier
                small[pl.ds(first * side + second, 1), lanes] = total
        return 0

    lax.fori_loop(0, blocks, tap_block, 0)
    for place in range(out.shape[0]):
        part = small[pl.ds(place * SMALL, SMALL), :]
        out[place] = jnp.concatenate([part, jnp.zeros_like(part)]).astype(jnp.bfloat16)


def feature_kernel(
    field, row_inner, row_outer, inner, outer, taps, cotangent, out, padded
):
    height, width, channels = field.shape
    side = 7
    first_row = lax.axis_index("core") == 0
    first_column = lax.rem(lax.axis_index("z"), 2) == 0
    fill_own(padded, field, row_inner, row_outer, first_row, side // 2)
    fill_sides(padded, inner, outer, first_row, first_column, width, side // 2)
    for block in range(channels // LANES):
        lanes = pl.ds(block * LANES, LANES)
        for first_col in range(0, width, 8):
            columns = pl.ds(first_col, 8)
            for row, total in enumerate(
                depthwise(padded, taps, block, first_col, height, side, True)
            ):
                total = total + cotangent[row, columns, lanes].astype(jnp.float32)
                out[row, columns, lanes] = total.astype(jnp.bfloat16)


def added(left, right):
    return (left.astype(jnp.float32) + right.astype(jnp.float32)).astype(jnp.bfloat16)


def merge_kernel(kept, came, small, small_came, out):
    rows = kept.shape[1]
    out[:, pl.ds(0, rows), :] = added(kept[...], came[...])
    out[:, pl.ds(rows, small.shape[1]), :] = added(small[...], small_came[...])


def join_kernel(kept, came, *outs):
    for step, out in enumerate(outs):
        z = lax.axis_index("z") ^ step
        out[...] = added(kept[z], came[z])


def plane_kernel(chunks, out, total):
    total[...] = jnp.sum(chunks[...].astype(jnp.float32), axis=0)
    each = out.shape[1] // 2
    channels = out.shape[2]
    top = total.shape[0] - 2 * SMALL - each * Z
    blocks = (channels - ALONG) // LANES
    small = total[pl.ds(total.shape[0] - 2 * SMALL, SMALL), :]
    small = jnp.concatenate([small[:, :ALONG], small[:, ALONG:]])
    for z in range(Z):
        parts = [total[slot(z * blocks + i, each, channels)] for i in range(blocks)]
        parts.append(small)
        out[z, pl.ds(0, each), :] = jnp.concatenate(parts, axis=1).astype(jnp.bfloat16)
        parts = [total[pl.ds(top + q * 2 * Z + 2 * z, 2), :] for q in range(each // 2)]
        out[z, pl.ds(each, each), :] = jnp.concatenate(parts).astype(jnp.bfloat16)


def line_kernel(multiplier, chunks, *refs):
    *came, part_out, dexpand, out = refs
    total = jnp.sum(chunks[...].astype(jnp.float32), axis=0)
    each, channels = part_out.shape
    part_out[...] = total[:each] * multiplier
    for q in range(each // 2):
        part = total[each + 2 * q : each + 2 * q + 2]
        dexpand[:, pl.ds(q * channels, channels)] = part * multiplier
    half = channels // 2
    small = total[:each, half:].astype(jnp.bfloat16)
    line = sum(ref[...].astype(jnp.float32) for ref in came).astype(jnp.bfloat16)
    for place in range(out.shape[0]):
        y, x = place // X, place % X
        out[place, :, pl.ds(0, half)] = small
        out[place, :, pl.ds(half, ALONG)] = line[y][:, x * ALONG : (x + 1) * ALONG]


def last_kernel(multiplier, chunks, part, dreduce, dkernel, dgain, dscale):
    channels = dreduce.shape[1]
    half = channels // 2
    own = channels - ALONG
    dreduce[:, pl.ds(0, own)] = part[:, pl.ds(0, own)]
    total = jnp.sum(chunks[:, :, pl.ds(half, ALONG)].astype(jnp.float32), axis=0)
    dreduce[:, pl.ds(own, ALONG)] = total * multiplier
    side = dkernel.shape[0]
    for place in range(chunks.shape[0]):
        small = chunks[place, :, pl.ds(0, half)].astype(jnp.float32)
        for row in range(SMALL):
            tap = place * SMALL + row
            for i in range(2):
                lanes = pl.ds(i * half, half)
                value = small[i * SMALL + row : i * SMALL + row + 1]
                if tap < side * side:
                    dkernel[tap // side, pl.ds(tap % side, 1), lanes] = value
                elif tap == side * side:
                    dgain[:, lanes] = value
                elif tap == side * side + 1:
                    dscale[:, lanes] = value


VMEM = pl.BlockSpec(memory_space=pltpu.VMEM)
HBM = pl.BlockSpec(memory_space=pltpu.HBM)
PARAMS = pltpu.CompilerParams(vmem_limit_bytes=20 << 20)
GLUE_PARAMS = pltpu.CompilerParams(vmem_limit_bytes=10 << 20)


def in_hbm(value):
    return pltpu.with_memory_space_constraint(value, pltpu.HBM)


def swapped(low, high, axes, first):
    count = lax.axis_size(axes)
    inner = [(i, i ^ 1) for i in range(count)]
    outer = [(i, i + 1 if i % 2 else i - 1) for i in range(1, count - 1)]
    return (
        lax.ppermute(jnp.where(first, high, low), axes, inner),
        lax.ppermute(jnp.where(first, low, high), axes, outer),
    )


def row_borders(field, reach):
    return swapped(field[:reach], field[-reach:], ROW, lax.axis_index("core") == 0)


def column_borders(field, inner, outer, reach):
    low, high = (
        jnp.concatenate([part[:, columns] for part in (inner, field, outer)])
        for columns in (slice(0, reach), slice(-reach, None))
    )
    return inner, outer, *swapped(low, high, COL, lax.axis_index("z") % 2 == 0)


def exchanged(chunks, axes):
    return lax.all_to_all(chunks, axes, 0, 0, tiled=True)


def shards(features, kernel, gain, w_expand, w_reduce, layer_scale, cotangent):
    height, width, channels = features.shape
    hidden = w_reduce.shape[0]
    side = kernel.shape[0]
    reach = side // 2
    blocks = channels // LANES
    pixels = height * width
    multiplier = 1.0 / math.sqrt(pixels * lax.axis_size(ROW) * lax.axis_size(COL))
    gain_row = gain.reshape(1, channels)
    scale_row = layer_scale.reshape(1, channels)
    places = Y * X
    rows = hidden // (Y * CORE * X)
    f32, bf16 = jnp.float32, jnp.bfloat16
    shape = jax.ShapeDtypeStruct
    padded_shape = (blocks, height + side - 1, LEFT + width + 8, LANES)

    each = rows // Z
    top = rows * (channels - ALONG) // channels
    row_inner, row_outer, inner, outer = column_borders(
        features, *row_borders(features, reach), reach
    )
    padded, conv, dbranch, taps, params, expand, reduce = pl.pallas_call(
        prepare_kernel,
        name="prepare",
        in_specs=[HBM] + [VMEM] * 2 + [HBM] * 6,
        out_specs=[VMEM] * 7,
        out_shape=[
            shape(padded_shape, f32),
            shape((blocks, pixels, LANES), f32),
            shape((pixels, channels), bf16),
            shape(kernel.shape, f32),
            shape((16, channels), f32),
            shape(w_expand.shape, bf16),
            shape(w_reduce.shape, bf16),
        ],
        scratch_shapes=[
            pltpu.VMEM(features.shape, bf16),
            pltpu.VMEM((1, channels), f32),
            pltpu.VMEM((1, channels), f32),
            pltpu.VMEM(cotangent.shape, bf16),
            pltpu.SemaphoreType.DMA((7,)),
        ],
        compiler_params=PARAMS,
    )(
        in_hbm(features), row_inner, row_outer, in_hbm(kernel), in_hbm(gain_row),
        in_hbm(scale_row), in_hbm(cotangent), in_hbm(w_expand), in_hbm(w_reduce),
    )
    sent, kept, sent_z, kept_z, dpre, xhat, rstd, padded, dscale = pl.pallas_call(
        forward_kernel,
        name="forward",
        in_specs=[VMEM] * 9,
        out_specs=[VMEM] * 9,
        out_shape=[shape((places, top + rows, channels), bf16)] * 2
        + [shape((Z, Y, each, X * ALONG), bf16)] * 2
        + [
            shape((pixels, hidden), bf16),
            shape((blocks, pixels, LANES), f32),
            shape((pixels, LANES), f32),
            shape(padded_shape, f32),
            shape((8, channels), f32),
        ],
        scratch_shapes=[
            pltpu.VMEM((pixels, channels), bf16),
            pltpu.VMEM((channels, pixels), bf16),
            pltpu.VMEM((channels, pixels), bf16),
        ],
        input_output_aliases={2: 7},
        compiler_params=PARAMS,
    )(inner, outer, padded, conv, dbranch, taps, params, expand, reduce)

    swap = [(0, 1), (1, 0)]
    came = lax.ppermute(sent, "core", swap)
    came_z = lax.ppermute(sent_z, "core", swap)
    dconv, small = pl.pallas_call(
        functools.partial(backward_kernel, multiplier),
        name="backward",
        in_specs=[VMEM] * 7,
        out_specs=[VMEM] * 2,
        out_shape=[
            shape((height, width, channels), bf16),
            shape((places, 2 * SMALL, channels), bf16),
        ],
        scratch_shapes=[
            pltpu.VMEM((blocks, pixels, LANES), f32),
            pltpu.VMEM((places * SMALL, channels), f32),
        ],
        compiler_params=PARAMS,
    )(dpre, expand, xhat, rstd, padded, params, dscale)

    small_came = lax.ppermute(small, "core", swap)
    whole = top + rows + 2 * SMALL
    chip = pl.pallas_call(
        merge_kernel,
        name="merge",
        grid=(Y,),
        in_specs=[pl.BlockSpec((X, top + rows, channels), lambda i: (i, 0, 0))] * 2
        + [pl.BlockSpec((X, 2 * SMALL, channels), lambda i: (i, 0, 0))] * 2,
        out_specs=pl.BlockSpec((X, whole, channels), lambda i: (i, 0, 0)),
        out_shape=shape((places, whole, channels), bf16),
        compiler_params=GLUE_PARAMS,
    )(kept, came, small, small_came)
    chip, dconv, came_z, rows_came = lax.optimization_barrier(
        (chip, dconv, came_z, row_borders(dconv, reach))
    )
    line = pl.pallas_call(
        join_kernel,
        name="join",
        in_specs=[VMEM] * 2,
        out_specs=[VMEM] * Z,
        out_shape=[shape(kept_z.shape[1:], bf16)] * Z,
        compiler_params=GLUE_PARAMS,
    )(kept_z, came_z)
    line = [
        part if step == 0 else lax.ppermute(part, "z", [(i, i ^ step) for i in range(Z)])
        for step, part in enumerate(line)
    ]
    chunks, edges, line = lax.optimization_barrier(
        (exchanged(chip, ("y", "x")), column_borders(dconv, *rows_came, reach), line)
    )
    chunks = pl.pallas_call(
        plane_kernel,
        name="plane",
        in_specs=[VMEM],
        out_specs=VMEM,
        out_shape=shape((Z, 2 * each, channels), bf16),
        scratch_shapes=[pltpu.VMEM((whole, channels), f32)],
        compiler_params=GLUE_PARAMS,
    )(chunks)
    part, dexpand, chunks = pl.pallas_call(
        functools.partial(line_kernel, multiplier),
        name="line",
        in_specs=[VMEM] * (1 + Z),
        out_specs=[VMEM] * 3,
        out_shape=[
            shape((each, channels), f32),
            shape((channels * each // hidden, hidden), f32),
            shape((places, each, channels), bf16),
        ],
        compiler_params=GLUE_PARAMS,
    )(exchanged(chunks, "z"), *line)
    dreduce, dkernel, dgain, dscale = pl.pallas_call(
        functools.partial(last_kernel, multiplier),
        name="last",
        in_specs=[VMEM] * 2,
        out_specs=[VMEM] * 4,
        out_shape=[shape((each, channels), f32), shape((side, side, channels), f32)]
        + [shape((1, channels), f32)] * 2,
        compiler_params=GLUE_PARAMS,
    )(exchanged(chunks, ("y", "x")), part)
    grad_features = pl.pallas_call(
        feature_kernel,
        name="features",
        in_specs=[VMEM] * 7,
        out_specs=VMEM,
        out_shape=shape((height, width, channels), bf16),
        scratch_shapes=[pltpu.VMEM(padded_shape, f32)],
        compiler_params=GLUE_PARAMS,
    )(dconv, *edges, kernel, cotangent)
    return (
        grad_features,
        dkernel,
        dgain.reshape(channels),
        dscale.reshape(channels),
        dexpand,
        dreduce,
    )


def solution(mesh):
    pixels = P(ROW, COL, None)
    return jax.shard_map(
        shards,
        mesh=Mesh(mesh.devices.reshape(Y, CORE, X, Z), (*ROW, *COL)),
        in_specs=(pixels, P(), P(), P(), P(), P(), pixels),
        out_specs=(pixels, P(), P(), P(), P((*ROW, *COL), None), P((*ROW, *COL), None)),
        check_vma=False,
    )
```
